32 devices in a mesh: expert: 4 (over z), batch: 8 (over y, x, core).
Axes of the slice: x: 2, y: 2, z: 4, core: 2. Of those that a mesh axis runs over, the one named last changes fastest.
Arguments:
- tokens: bfloat16 [32, 1024, 768], P(('expert', 'batch')), may hold values from -6 to 6
- lengths: int32 [32], P(('expert', 'batch')), may hold values from 64 to 1024, as said below
- routes: int32 [32, 1024, 2], P(('expert', 'batch')), may hold values from 0 to 7, as said below
- ln1_gain: float32 [768], replicated, may hold values from 0.5 to 1.5
- ln1_bias: float32 [768], replicated, may hold values from -1.5 to 1.5
- ln2_gain: float32 [768], replicated, may hold values from 0.5 to 1.5
- ln2_bias: float32 [768], replicated, may hold values from -1.5 to 1.5
- w_qkv: bfloat16 [768, 2304], replicated, may hold values from -0.21875 to 0.21875
- w_proj: bfloat16 [768, 768], replicated, may hold values from -1.25 to 1.25
- w_router: bfloat16 [768, 8], replicated, may hold values from -0.15625 to 0.15625
- old_in: bfloat16 [4, 768, 3072], P('expert', 'batch'), may hold values from -0.21875 to 0.21875
- old_out: bfloat16 [4, 3072, 768], P('expert', 'batch'), may hold values from -0.109375 to 0.109375
- new_in: bfloat16 [4, 768, 3072], P('expert', 'batch'), may hold values from -0.21875 to 0.21875
- new_out: bfloat16 [4, 3072, 768], P('expert', 'batch'), may hold values from -0.109375 to 0.109375
- cotangent: bfloat16 [32, 1024, 768], P(('expert', 'batch')), may hold values from -6 to 6
Outputs:
- output: float32 [32, 1024, 768], P(('expert', 'batch'))
- input_grad: float32 [32, 1024, 768], P(('expert', 'batch'))
- ln1_gain_grad: float32 [768], replicated
- ln1_bias_grad: float32 [768], replicated
- ln2_gain_grad: float32 [768], replicated
- ln2_bias_grad: float32 [768], replicated
- qkv_grad: float32 [768, 2304], replicated
- proj_grad: float32 [768, 768], replicated
- router_grad: float32 [768, 8], replicated
- new_in_grad: float32 [4, 768, 3072], P('expert', 'batch')
- new_out_grad: float32 [4, 3072, 768], P('expert', 'batch')
The draws below stay inside these ranges and needn't reach their ends.
Inputs may be any that keep to these rules, and one draw needn't show every extreme that they name: Positions lengths[r] and beyond of row r are padding. In every draw some row has 1024 tokens and some row 64. `routes`: the two experts of one token always differ. Across the tokens of a sequence row the same expert is named many times, and some experts are named more often than others.
All inputs are finite; a program needn't handle non-finite values.
Results may differ from the reference program's by a relative error of at most 0.012.
Values may be sent and summed in bfloat16 or wider, within the bound.
No kernel may reach another device: no remote copies, remote signals or barrier semaphores. Data moves between devices by JAX's collectives and lax.ppermute only.
A program may use at most 320 MiB of HBM per device.

```python
import math
import jax
import jax.numpy as jnp
from jax import lax

D = 768
HEADS = 12
HEAD_DIM = 64
FF = 3072
ROW_LEN = 1024
MIN_LEN = 64
ROWS = 32
HALF = 4
EXPERTS = 8
CAP = 128


def draw_lengths(key, part):
    keys_split = jax.random.split(key, 3)
    drawn_lens = jax.random.randint(keys_split[0], (ROWS,), MIN_LEN, ROW_LEN + 1)
    longest = jax.random.randint(keys_split[1], (), 0, ROWS)
    offset = jax.random.randint(keys_split[2], (), 1, ROWS)
    shortest = (longest + offset) % ROWS
    positions = jnp.arange(ROWS)
    drawn_lens = jnp.where(positions == longest, ROW_LEN, drawn_lens)
    drawn_lens = jnp.where(positions == shortest, MIN_LEN, drawn_lens)
    return drawn_lens.astype(jnp.int32)


def draw_routes(key, part):
    keys_split = jax.random.split(jax.random.fold_in(key, 7), 4)
    order = jax.random.permutation(keys_split[0], EXPERTS).astype(jnp.int32)
    first_a = jax.random.randint(keys_split[1], (ROWS, ROW_LEN), 0, EXPERTS)
    first_b = jax.random.randint(keys_split[2], (ROWS, ROW_LEN), 0, EXPERTS)
    first = order[jnp.minimum(first_a, first_b)]
    step_by = jax.random.randint(keys_split[3], (ROWS, ROW_LEN), 1, EXPERTS)
    second = (first + step_by) % EXPERTS
    row_pos = jnp.arange(ROWS)[:, None]
    tok_pos = jnp.arange(ROW_LEN)[None, :]
    corner = (row_pos == 0) & (tok_pos == 0)
    first = jnp.where(corner, EXPERTS - 1, first)
    second = jnp.where(corner, 0, second)
    return jnp.stack([first, second], axis=-1).astype(jnp.int32)


def shard_levels(rng, extent, cuts, least, largest):
    def one(axis_at, blocks):
        heights = jax.random.uniform(jax.random.fold_in(jax.random.fold_in(rng, 6), axis_at), (blocks,), jnp.float32, least / len(cuts), largest / len(cuts))
        return jnp.repeat(jnp.exp(heights), extent[axis_at] // blocks).reshape((-1,) + (1,) * (len(extent) - axis_at - 1))

    level = one(*cuts[0])
    for cut in cuts[1:]:
        level = level * one(*cut)
    return level


def bell_draw(own_key, extent, scale, bound, cuts=(), kind=jnp.bfloat16):
    entries = scale * jax.random.normal(own_key, extent, jnp.float32)
    if cuts:
        entries = entries * shard_levels(own_key, extent, cuts, -0.22, 0.18)
    return jnp.clip(entries, -bound, bound).astype(kind)


def setup_inputs(seed: int = 0) -> dict:
    key_of = jax.random.split(jax.random.key(seed), 16)
    tokens = bell_draw(key_of[0], (ROWS, ROW_LEN, D), 1.0, 6.0, ((0, 32),))
    lengths = draw_lengths(jax.random.fold_in(key_of[15], 71), 0)
    routes = draw_routes(jax.random.fold_in(key_of[15], 71), 0)
    ln1_gain = jnp.clip(1.0 + 0.1 * jax.random.normal(key_of[3], (D,), jnp.float32), 0.5, 1.5)
    ln1_bias = bell_draw(key_of[4], (D,), 0.3, 1.5, (), jnp.float32)
    ln2_gain = jnp.clip(1.0 + 0.1 * jax.random.normal(key_of[5], (D,), jnp.float32), 0.5, 1.5)
    ln2_bias = bell_draw(key_of[6], (D,), 0.3, 1.5, (), jnp.float32)
    w_qkv = bell_draw(key_of[7], (D, 3 * D), D ** -0.5, 0.21875)
    w_proj = bell_draw(key_of[8], (D, D), (D // 32) ** -0.5, 1.25)
    w_router = bell_draw(key_of[9], (D, EXPERTS), (2 * D) ** -0.5, 0.15625)
    old_in = bell_draw(key_of[10], (HALF, D, FF), D ** -0.5, 0.21875, ((0, 4), (1, 8)))
    old_out = bell_draw(key_of[11], (HALF, FF, D), FF ** -0.5, 0.109375, ((0, 4), (1, 8)))
    new_in = bell_draw(key_of[12], (HALF, D, FF), D ** -0.5, 0.21875, ((0, 4), (1, 8)))
    new_out = bell_draw(key_of[13], (HALF, FF, D), FF ** -0.5, 0.109375, ((0, 4), (1, 8)))
    cotangent = bell_draw(key_of[14], (ROWS, ROW_LEN, D), 1.0, 6.0, ((0, 32),))
    return {"tokens": tokens, "lengths": lengths, "routes": routes, "ln1_gain": ln1_gain, "ln1_bias": ln1_bias, "ln2_gain": ln2_gain, "ln2_bias": ln2_bias, "w_qkv": w_qkv, "w_proj": w_proj, "w_router": w_router, "old_in": old_in, "old_out": old_out, "new_in": new_in, "new_out": new_out, "cotangent": cotangent}


norm_eps = 1e-05
masked_value = -1e+30
highest = lax.Precision.HIGHEST

@jax.custom_vjp
def low(v):
    return lax.optimization_barrier(v.astype(jnp.bfloat16)).astype(jnp.float32)

@jax.custom_vjp
def low_back(v):
    return v

def low_keep(v):
    return (low(v), None)

def low_pass(kept, grad):
    return (grad,)

def back_keep(v):
    return (v, None)

def back_low(kept, grad):
    return (low(grad),)
low.defvjp(low_keep, low_pass)
low_back.defvjp(back_keep, back_low)

def layer_norm(field_in, gain_vec, bias_vec):
    row_mean = lax.optimization_barrier(jnp.mean(field_in, axis=-1, keepdims=True))
    centred = field_in - row_mean
    row_var = lax.optimization_barrier(jnp.mean(centred * centred, axis=-1, keepdims=True))
    return centred * lax.rsqrt(row_var + norm_eps) * gain_vec + bias_vec

def gelu_tanh(field_in):
    inner_arg = 0.7978845608028654 * (field_in + 0.044715 * field_in * field_in * field_in)
    return 0.5 * field_in * (1.0 + jnp.tanh(inner_arg))

def rank_pairs(route_row, length, experts, capacity):
    seq_len = route_row.shape[0]
    pair_expert = jnp.transpose(route_row).reshape(2 * seq_len)
    live_pair = jnp.tile(jnp.arange(seq_len, dtype=jnp.int32) < length, 2)
    one_hot = (pair_expert[:, None] == jnp.arange(experts, dtype=jnp.int32)[None, :]).astype(jnp.int32) * live_pair[:, None].astype(jnp.int32)
    earlier = jnp.cumsum(one_hot, axis=0, dtype=jnp.int32) - one_hot
    pair_rank = lax.optimization_barrier(jnp.sum(earlier * one_hot, axis=1, dtype=jnp.int32))
    kept_pair = live_pair & (pair_rank < capacity)
    return (jnp.transpose(pair_rank.reshape(2, seq_len)), jnp.transpose(kept_pair.reshape(2, seq_len)))

def attend_row(normed_row, length, qkv_weight, proj_weight):
    seq_len = normed_row.shape[0]
    model_width = normed_row.shape[1]
    qkv_vals = low(low_back(jnp.dot(normed_row, qkv_weight, precision=highest)))
    queries = qkv_vals[:, :model_width].reshape(seq_len, HEADS, HEAD_DIM)
    key_rows = qkv_vals[:, model_width:2 * model_width].reshape(seq_len, HEADS, HEAD_DIM)
    value_rows = qkv_vals[:, 2 * model_width:].reshape(seq_len, HEADS, HEAD_DIM)
    raw_scores = jnp.einsum('qhd,khd->hqk', queries, key_rows, precision=highest)
    scores = low_back(raw_scores * (1.0 / math.sqrt(HEAD_DIM)))
    positions = jnp.arange(seq_len, dtype=jnp.int32)
    allowed = (positions[None, :] <= positions[:, None]) & (positions[None, :] < length)
    scores = jnp.where(allowed[None], scores, masked_value)
    probs_all = jax.nn.softmax(scores, axis=-1)
    mixed_rows = jnp.einsum('hqk,khd->qhd', low(probs_all), value_rows, precision=highest).reshape(seq_len, model_width)
    mixed_rows = low(low_back(mixed_rows))
    return low_back(jnp.dot(mixed_rows, proj_weight, precision=highest))

def reference(tokens, lengths, routes, ln1_gain, ln1_bias, ln2_gain, ln2_bias, w_qkv, w_proj, w_router, old_in, old_out, new_in, new_out, cotangent):
    pair_rank, kept_pair = jax.vmap(rank_pairs, in_axes=(0, 0, None, None))(routes, lengths, EXPERTS, CAP)
    row_ids = jnp.arange(ROWS, dtype=jnp.int32)[:, None, None]
    token_ids = jnp.broadcast_to(jnp.arange(ROW_LEN, dtype=jnp.int32)[None, :, None], routes.shape)
    slot_index = routes * (ROWS * CAP) + row_ids * CAP + pair_rank
    buffer_size = EXPERTS * ROWS * CAP
    target = jnp.where(kept_pair, slot_index, buffer_size).reshape(-1).astype(jnp.int32)
    flat_token = (row_ids * ROW_LEN + token_ids).reshape(-1).astype(jnp.int32)
    source_token = jnp.zeros((buffer_size,), jnp.int32).at[target].set(flat_token, mode='drop')
    slot_filled = jnp.zeros((buffer_size,), jnp.float32).at[target].set(1.0, mode='drop')
    pick_index = jnp.where(kept_pair, slot_index, 0).astype(jnp.int32)
    kept_weight = kept_pair.astype(jnp.float32)
    source_split = source_token.reshape(EXPERTS, ROWS * CAP)
    filled_split = slot_filled.reshape(EXPERTS, ROWS * CAP)
    frozen_in = old_in.astype(jnp.float32)
    frozen_out = old_out.astype(jnp.float32)

    def forward(inputs, norm1_gain, norm1_bias, norm2_gain, norm2_bias, qkv_weight, proj_weight, router_weight, train_in, train_out):
        normed1 = low(layer_norm(inputs, norm1_gain, norm1_bias))
        attend = jax.checkpoint(lambda pieces: attend_row(pieces[0], pieces[1], qkv_weight, proj_weight))
        attn_out = lax.map(attend, (normed1, lengths))
        residual = inputs + attn_out
        normed2 = low(layer_norm(residual, norm2_gain, norm2_bias))
        logits = low_back(jnp.einsum('rtd,de->rte', normed2, router_weight, precision=highest))
        gate_vals = jax.nn.softmax(jnp.take_along_axis(logits, routes, axis=2), axis=-1)
        flat_normed = normed2.reshape(ROWS * ROW_LEN, normed2.shape[2])

        def expert_fn(pieces):
            weight_in, weight_out, index_rows, fill_rows = pieces
            buffer_rows = low_back(flat_normed[index_rows] * fill_rows[:, None])
            pre_act = low_back(jnp.dot(buffer_rows, weight_in, precision=highest))
            hidden = low(gelu_tanh(pre_act))
            return low(low_back(jnp.dot(hidden, weight_out, precision=highest)))
        run_expert = jax.checkpoint(expert_fn)
        old_result = lax.map(run_expert, (frozen_in, frozen_out, source_split[:HALF], filled_split[:HALF]))
        new_result = lax.map(run_expert, (train_in, train_out, source_split[HALF:], filled_split[HALF:]))
        all_results = jnp.concatenate([old_result, new_result], axis=0).reshape(buffer_size, normed2.shape[2])
        gate_kept = gate_vals * kept_weight
        mixture = gate_kept[:, :, 0, None] * all_results[pick_index[:, :, 0]]
        mixture = mixture + gate_kept[:, :, 1, None] * all_results[pick_index[:, :, 1]]
        return residual + mixture
    primals = (tokens.astype(jnp.float32), ln1_gain, ln1_bias, ln2_gain, ln2_bias, w_qkv.astype(jnp.float32), w_proj.astype(jnp.float32), w_router.astype(jnp.float32), new_in.astype(jnp.float32), new_out.astype(jnp.float32))
    output, back_fn = jax.vjp(forward, *primals)
    grad_list = back_fn(cotangent.astype(jnp.float32))
    return (output, grad_list[0], grad_list[1], grad_list[2], grad_list[3], grad_list[4], grad_list[5], grad_list[6], grad_list[7], grad_list[8], grad_list[9])
```

```python
import functools

import jax
import jax.numpy as jnp
from jax import lax
from jax.experimental import pallas as pl
from jax.experimental.pallas import tpu as pltpu
from jax.sharding import PartitionSpec as P

HEAD_DIM = 64
LANES = 128
EPS = 1e-05
MASKED = -1e30
F32 = jnp.float32
BF16 = jnp.bfloat16
VMEM_LIMIT = 56 * 1024 * 1024


def params():
    return pltpu.CompilerParams(vmem_limit_bytes=VMEM_LIMIT)


def dot_nt(left, right):
    return lax.dot_general(left, right, (((1,), (1,)), ((), ())), preferred_element_type=F32)


def dot_tn(left, right):
    return lax.dot_general(left, right, (((0,), (0,)), ((), ())), preferred_element_type=F32)


def dot_nn(left, right):
    return jnp.dot(left, right, preferred_element_type=F32)


def norm_parts(rows):
    mean = jnp.mean(rows, axis=-1, keepdims=True)
    centred = rows - mean
    var = jnp.mean(centred * centred, axis=-1, keepdims=True)
    scale = lax.rsqrt(var + EPS)
    return centred * scale, scale


def norm_back(grad, gain, xhat, scale):
    a = grad * gain
    mean_a = jnp.mean(a, axis=-1, keepdims=True)
    mean_ax = jnp.mean(a * xhat, axis=-1, keepdims=True)
    return scale * (a - mean_a - xhat * mean_ax)


def full(shape):
    return pl.BlockSpec(shape, lambda *_: (0,) * len(shape))


def smem():
    return pl.BlockSpec(memory_space=pltpu.SMEM)


def qkv_kernel(tok_ref, gain_ref, bias_ref, w_ref, normed_ref, qkv_ref):
    xhat, _ = norm_parts(tok_ref[...].astype(F32))
    normed = (xhat * gain_ref[...] + bias_ref[...]).astype(BF16)
    normed_ref[...] = normed
    qkv_ref[...] = dot_nn(normed, w_ref[...]).astype(BF16)


def qkv_call(tokens, gain, bias, weight):
    seq, width = tokens.shape
    block = 256
    cols = weight.shape[1]
    return pl.pallas_call(
        qkv_kernel,
        grid=(seq // block,),
        in_specs=[
            pl.BlockSpec((block, width), lambda i: (i, 0)),
            full((1, width)),
            full((1, width)),
            full((width, cols)),
        ],
        out_specs=[
            pl.BlockSpec((block, width), lambda i: (i, 0)),
            pl.BlockSpec((block, cols), lambda i: (i, 0)),
        ],
        out_shape=[
            jax.ShapeDtypeStruct((seq, width), BF16),
            jax.ShapeDtypeStruct((seq, cols), BF16),
        ],
        compiler_params=params(),
        name="norm_qkv",
    )(tokens, gain, bias, weight)


def head_parts(head, length, q, k):
    seq = q.shape[0]
    lane = lax.broadcasted_iota(jnp.int32, (seq, LANES), 1)
    row = lax.broadcasted_iota(jnp.int32, (seq, LANES), 0)
    inside = (lane // HEAD_DIM) == head
    extra = lane == (1 - head) * HEAD_DIM
    key_bias = jnp.where(row >= length, MASKED, 0.0)
    kf = k.astype(F32)
    qf = q.astype(F32) * (HEAD_DIM**-0.5)
    k_head = jnp.where(inside, kf, jnp.where(extra, key_bias, 0.0)).astype(BF16)
    q_head = jnp.where(inside, qf, jnp.where(extra, 1.0, 0.0)).astype(BF16)
    return inside, k_head, q_head, jnp.where(inside, qf, 0.0).astype(BF16)


def causal(scores, block):
    key = lax.broadcasted_iota(jnp.int32, (block, block), 0)
    query = lax.broadcasted_iota(jnp.int32, (block, block), 1)
    last = jnp.where(key <= query, scores[-block:], MASKED)
    if scores.shape[0] == block:
        return last
    return jnp.concatenate([scores[:-block], last], axis=0)


def attend_kernel(len_ref, q_ref, k_ref, v_ref, out_ref, lse_ref, kh_ref, qh_ref, vt_ref, ot_ref):
    seq = q_ref.shape[0]
    block = 256
    length = len_ref[0]
    vt_ref[...] = v_ref[...].astype(F32).T.astype(BF16)
    lse_ref[...] = jnp.zeros_like(lse_ref)
    for head in range(2):
        _, k_head, q_head, _ = head_parts(head, length, q_ref[...], k_ref[...])
        kh_ref[...] = k_head
        qh_ref[...] = q_head
        for qb in range(seq // block):
            ext = (qb + 1) * block
            cols = slice(qb * block, ext)
            scores = causal(dot_nt(kh_ref[:ext, :], qh_ref[cols, :]), block)
            top = jnp.max(scores, axis=0, keepdims=True)
            probs = jnp.exp(scores - top)
            total = jnp.sum(probs, axis=0, keepdims=True)
            part = dot_nn(vt_ref[head * HEAD_DIM : (head + 1) * HEAD_DIM, :ext], probs.astype(BF16))
            ot_ref[head * HEAD_DIM : (head + 1) * HEAD_DIM, cols] = part * (1.0 / total)
            lse_ref[0, head : head + 1, cols] = top + jnp.log(total)
    out_ref[...] = ot_ref[...].T.astype(BF16)


def attend_call(length, qkv):
    seq = qkv.shape[0]
    width = qkv.shape[1] // 3
    pairs = width // LANES
    return pl.pallas_call(
        attend_kernel,
        grid=(pairs,),
        in_specs=[
            smem(),
            pl.BlockSpec((seq, LANES), lambda p: (0, p)),
            pl.BlockSpec((seq, LANES), lambda p: (0, pairs + p)),
            pl.BlockSpec((seq, LANES), lambda p: (0, 2 * pairs + p)),
        ],
        out_specs=[
            pl.BlockSpec((seq, LANES), lambda p: (0, p)),
            pl.BlockSpec((1, 8, seq), lambda p: (p, 0, 0)),
        ],
        out_shape=[
            jax.ShapeDtypeStruct((seq, width), BF16),
            jax.ShapeDtypeStruct((pairs, 8, seq), F32),
        ],
        scratch_shapes=[
            pltpu.VMEM((seq, LANES), BF16),
            pltpu.VMEM((seq, LANES), BF16),
            pltpu.VMEM((LANES, seq), BF16),
            pltpu.VMEM((LANES, seq), F32),
        ],
        compiler_params=params(),
        name="attend",
    )(length, qkv, qkv, qkv)


def attend_back_kernel(
    len_ref,
    q_ref,
    k_ref,
    v_ref,
    do_ref,
    o_ref,
    lse_ref,
    normed_ref,
    dqkv_ref,
    grad_ref,
    nt_ref,
    kt_ref,
    kh_ref,
    qh_ref,
    qm_ref,
    vh_ref,
    dh_ref,
    dk_ref,
    dv_ref,
    dqt_ref,
    pt_ref,
):
    seq = q_ref.shape[0]
    block = 256
    length = len_ref[0]

    @pl.when(pl.program_id(0) == 0)
    def _():
        nt_ref[...] = normed_ref[...].astype(F32).T.astype(BF16)

    kt_ref[...] = k_ref[...].astype(F32).T.astype(BF16)
    pt_ref[...] = (do_ref[...].astype(F32) * o_ref[...].astype(F32)).T
    dk_ref[...] = jnp.zeros_like(dk_ref)
    dv_ref[...] = jnp.zeros_like(dv_ref)
    for head in range(2):
        rows = slice(head * HEAD_DIM, (head + 1) * HEAD_DIM)
        inside, k_head, q_head, q_masked = head_parts(head, length, q_ref[...], k_ref[...])
        kh_ref[...] = k_head
        qh_ref[...] = q_head
        qm_ref[...] = q_masked
        vh_ref[...] = jnp.where(inside, v_ref[...].astype(F32), 0.0).astype(BF16)
        dh_ref[...] = jnp.where(inside, do_ref[...].astype(F32), 0.0).astype(BF16)
        for qb in range(seq // block):
            ext = (qb + 1) * block
            cols = slice(qb * block, ext)
            delta = jnp.sum(pt_ref[rows, cols], axis=0, keepdims=True)
            scores = causal(dot_nt(kh_ref[:ext, :], qh_ref[cols, :]), block)
            probs = jnp.exp(scores - lse_ref[0, head : head + 1, cols])
            dprobs = dot_nt(vh_ref[:ext, :], dh_ref[cols, :])
            dscores = (probs * (dprobs - delta)).astype(BF16)
            dv_ref[:ext, :] += dot_nn(probs.astype(BF16), dh_ref[cols, :])
            dk_ref[:ext, :] += dot_nn(dscores, qm_ref[cols, :])
            dqt_ref[rows, cols] = dot_nn(kt_ref[rows, :ext], dscores)
    dq = (dqt_ref[...].T * (HEAD_DIM**-0.5)).astype(BF16)
    dk = dk_ref[...].astype(BF16)
    dv = dv_ref[...].astype(BF16)
    dqkv_ref[0] = dq
    dqkv_ref[1] = dk
    dqkv_ref[2] = dv
    joined = dot_nn(nt_ref[...], jnp.concatenate([dq, dk, dv], axis=1)).astype(BF16)
    for part in range(3):
        grad_ref[part] = joined[:, part * LANES : (part + 1) * LANES]


def attend_back_call(length, qkv, dmixed, mixed, lse, normed):
    seq, width = normed.shape
    pairs = width // LANES
    col = lambda p: (0, p)
    return pl.pallas_call(
        attend_back_kernel,
        grid=(pairs,),
        in_specs=[
            smem(),
            pl.BlockSpec((seq, LANES), col),
            pl.BlockSpec((seq, LANES), lambda p: (0, pairs + p)),
            pl.BlockSpec((seq, LANES), lambda p: (0, 2 * pairs + p)),
            pl.BlockSpec((seq, LANES), col),
            pl.BlockSpec((seq, LANES), col),
            pl.BlockSpec((1, 8, seq), lambda p: (p, 0, 0)),
            full((seq, width)),
        ],
        out_specs=[
            pl.BlockSpec((3, seq, LANES), lambda p: (0, 0, p)),
            pl.BlockSpec((3, width, LANES), lambda p: (0, 0, p)),
        ],
        out_shape=[
            jax.ShapeDtypeStruct((3, seq, width), BF16),
            jax.ShapeDtypeStruct((3, width, width), BF16),
        ],
        scratch_shapes=[
            pltpu.VMEM((width, seq), BF16),
            pltpu.VMEM((LANES, seq), BF16),
            pltpu.VMEM((seq, LANES), BF16),
            pltpu.VMEM((seq, LANES), BF16),
            pltpu.VMEM((seq, LANES), BF16),
            pltpu.VMEM((seq, LANES), BF16),
            pltpu.VMEM((seq, LANES), BF16),
            pltpu.VMEM((seq, LANES), F32),
            pltpu.VMEM((seq, LANES), F32),
            pltpu.VMEM((LANES, seq), F32),
            pltpu.VMEM((LANES, seq), F32),
        ],
        compiler_params=params(),
        name="attend_back",
    )(length, qkv, qkv, qkv, dmixed, mixed, lse, normed)


def route_kernel(
    experts, group, capacity, len_ref, me_ref, route_ref, pair_ref, cot_ref, slot_ref, slot_t_ref, *out_refs
):
    seq = route_ref.shape[1]
    half = experts // 2
    per = half // group
    local = 2 * per
    length = len_ref[0]
    me = me_ref[0]
    live = lax.broadcasted_iota(jnp.int32, (1, seq), 1) < length
    ids = lax.broadcasted_iota(jnp.int32, (experts, seq), 0)
    upper = (
        lax.broadcasted_iota(jnp.int32, (seq, seq), 0) < lax.broadcasted_iota(jnp.int32, (seq, seq), 1)
    )
    upper = jnp.where(upper, 1.0, 0.0).astype(BF16)
    before = jnp.zeros((experts, 1), F32)
    slots = []
    for choice in range(2):
        named = route_ref[choice : choice + 1, :]
        hot = jnp.where((ids == named) & live, 1.0, 0.0)
        earlier = dot_nn(hot.astype(BF16), upper) + before
        rank = jnp.sum(hot * earlier, axis=0, keepdims=True).astype(jnp.int32)
        before = before + jnp.sum(hot, axis=1, keepdims=True)
        is_new = named >= half
        within = jnp.where(is_new, named - half, named)
        owner = within // per
        place = jnp.where(is_new, per, 0) + within - owner * per
        shift = owner - me
        shift = jnp.where(shift < 0, shift + group, shift)
        slot = (shift * local + place) * capacity + rank
        slots.append(jnp.where(live & (rank < capacity), slot, -1))
    slot_ref[...] = jnp.concatenate(slots + [jnp.full((6, seq), -1, jnp.int32)], axis=0)
    slot_t_ref[...] = jnp.concatenate(
        [slot.astype(F32) for slot in slots] + [jnp.full((LANES - 2, seq), -1.0, F32)], axis=0
    ).T.astype(jnp.int32)
    total = experts * capacity
    place = lax.broadcasted_iota(jnp.int32, (total, seq), 0)
    select = jnp.where((place == slots[0]) | (place == slots[1]), 1.0, 0.0).astype(BF16)
    rows = dot_nn(select, cot_ref[...]).astype(BF16)
    both = (pair_ref[:, 0:1] + pair_ref[:, 1:2]).astype(F32)
    lane = lax.broadcasted_iota(jnp.int32, (seq, LANES), 1)
    tail = dot_nn(select, jnp.where(lane == 0, both, 0.0).astype(BF16)).astype(BF16)
    width = cot_ref.shape[1]
    size = local * capacity
    for shift in range(group):
        piece = slice(shift * size, (shift + 1) * size)
        out_refs[shift][:, :, :width] = rows[piece].reshape(local, capacity, width)
        out_refs[shift][:, :, width:] = tail[piece].reshape(local, capacity, LANES)


def route_call(length, me, routes, cotangent, experts, group, capacity):
    seq, width = cotangent.shape
    local = experts // group
    wide = width + LANES
    return pl.pallas_call(
        functools.partial(route_kernel, experts, group, capacity),
        in_specs=[smem(), smem(), full((2, seq)), full((seq, 2)), full((seq, width))],
        out_specs=[full((8, seq)), full((seq, LANES))] + [full((local, capacity, wide))] * group,
        out_shape=[
            jax.ShapeDtypeStruct((8, seq), jnp.int32),
            jax.ShapeDtypeStruct((seq, LANES), jnp.int32),
        ]
        + [jax.ShapeDtypeStruct((local, capacity, wide), BF16)] * group,
        grid=(1,),
        compiler_params=params(),
        name="route",
    )(length, me, routes.T, routes, cotangent)


def project_kernel(
    group, mixed_ref, tok_ref, w_ref, gain_ref, bias_ref, slot_ref, res_ref, *refs
):
    out_refs = refs[:group]
    normed_ref = refs[group]
    step = pl.program_id(0)
    block = mixed_ref.shape[0]
    residual = tok_ref[...].astype(F32) + dot_nn(mixed_ref[...], w_ref[...])
    res_ref[...] = residual
    xhat, _ = norm_parts(residual)
    normed = (xhat * gain_ref[...] + bias_ref[...]).astype(BF16)
    normed_ref[pl.ds(pl.multiple_of(step * block, block), block), :] = normed

    @pl.when(step == pl.num_programs(0) - 1)
    def _():
        local, capacity, width = out_refs[0].shape
        size = local * capacity
        seq = normed_ref.shape[0]
        place = lax.broadcasted_iota(jnp.int32, (size * group, seq), 0)
        select = (place == slot_ref[0:1, :]) | (place == slot_ref[1:2, :])
        select = jnp.where(select, 1.0, 0.0).astype(BF16)
        rows = dot_nn(select, normed_ref[...]).astype(BF16)
        for shift in range(group):
            out_refs[shift][...] = rows[shift * size : (shift + 1) * size].reshape(local, capacity, width)


def project_call(mixed, tokens, weight, gain, bias, slots, group, local, capacity):
    seq, width = tokens.shape
    block = 256
    rows = pl.BlockSpec((block, width), lambda i: (i, 0))
    return pl.pallas_call(
        functools.partial(project_kernel, group),
        grid=(seq // block,),
        in_specs=[rows, rows, full((width, width)), full((1, width)), full((1, width)), full((8, seq))],
        out_specs=[rows] + [full((local, capacity, width))] * group,
        out_shape=[jax.ShapeDtypeStruct((seq, width), F32)]
        + [jax.ShapeDtypeStruct((local, capacity, width), BF16)] * group,
        scratch_shapes=[pltpu.VMEM((seq, width), BF16)],
        compiler_params=params(),
        name="project_dispatch",
    )(mixed, tokens, weight, gain, bias, slots)


def expert_kernel(trained, group, own_ref, *refs):
    x_refs = refs[:group]
    g_refs = refs[group : 2 * group]
    wr_ref, wrt_ref, win_ref, wout_ref = refs[2 * group : 2 * group + 4]
    rest = refs[2 * group + 4 :]
    out_refs = rest[:group]
    back_refs = rest[group : 2 * group]
    router_ref = rest[2 * group]
    rest = rest[2 * group + 1 :]
    if trained:
        din_ref, dout_ref = rest[:2]
        rest = rest[2:]
    x_ref, dexp_ref, gate_ref, acc_ref, back_ref, xt_ref = rest
    step = pl.program_id(0)
    capacity, width = out_refs[0].shape
    own = own_ref[0]

    def other_of(tail):
        return tail[:, 0:1].astype(F32).astype(jnp.int32) - own

    @pl.when(step == 0)
    def _():
        for shift in range(group):
            span = slice(shift * capacity, (shift + 1) * capacity)
            rows = x_refs[shift][0]
            x_ref[span, :] = rows
            logits = dot_nn(rows, wr_ref[...])
            lane = lax.broadcasted_iota(jnp.int32, logits.shape, 1)
            other = other_of(g_refs[shift][0, :, width:])
            mine = jnp.sum(jnp.where(lane == own, logits, 0.0), axis=1, keepdims=True)
            theirs = jnp.sum(jnp.where(lane == other, logits, 0.0), axis=1, keepdims=True)
            top = jnp.maximum(mine, theirs)
            up = jnp.exp(mine - top)
            gate = up / (up + jnp.exp(theirs - top))
            gate_ref[span, :] = jnp.broadcast_to(gate, (capacity, LANES))
            dexp_ref[span, :] = (gate * g_refs[shift][0, :, :width].astype(F32)).astype(BF16)
        acc_ref[...] = jnp.zeros_like(acc_ref)
        back_ref[...] = jnp.zeros_like(back_ref)
        xt_ref[...] = x_ref[...].astype(F32).T.astype(BF16)

    win = win_ref[0]
    wout = wout_ref[0]
    pre = dot_nn(x_ref[...], win)
    square = pre * pre
    tanh = jnp.tanh(0.7978845608028654 * (pre + 0.044715 * pre * square))
    half = 0.5 * (1.0 + tanh)
    hid = (pre * half).astype(BF16)
    slope = half + (0.5 * pre) * (1.0 - tanh * tanh) * (0.7978845608028654 + 0.1070322243 * square)
    acc_ref[...] += dot_nn(hid, wout)
    dpre = (dot_nt(dexp_ref[...], wout) * slope).astype(BF16)
    back_ref[...] += dot_nt(dpre, win)
    if trained:
        dout_ref[...] = dot_tn(hid, dexp_ref[...]).astype(BF16)
        din_ref[...] = dot_nn(xt_ref[...], dpre).astype(BF16)

    @pl.when(step == pl.num_programs(0) - 1)
    def _():
        router = jnp.zeros((width, LANES), F32)
        for shift in range(group):
            span = slice(shift * capacity, (shift + 1) * capacity)
            gate = gate_ref[span, 0:1]
            result = acc_ref[span, :]
            out_refs[shift][...] = (gate * result).astype(BF16)
            dot = jnp.sum(result * g_refs[shift][0, :, :width].astype(F32), axis=1, keepdims=True)
            coef = gate * (1.0 - gate) * dot
            lane = lax.broadcasted_iota(jnp.int32, (capacity, LANES), 1)
            other = other_of(g_refs[shift][0, :, width:])
            sign = jnp.where(lane == own, 1.0, 0.0) - jnp.where(lane == other, 1.0, 0.0)
            dlogits = (coef * sign).astype(BF16)
            back_refs[shift][...] = (back_ref[span, :] + dot_nn(dlogits, wrt_ref[...])).astype(BF16)
            router = router + dot_nn(xt_ref[:, span], dlogits)
        router_ref[...] = router


def expert_call(trained, place, own, rows, grads, router, router_t, w_in, w_out):
    group = len(rows)
    _, capacity, width = rows[0].shape
    inner = w_in.shape[2]
    chunk = 512
    wide = grads[0].shape[2]
    many = group * capacity
    fixed = full((capacity, width))
    out_specs = [fixed] * (2 * group) + [full((width, LANES))]
    out_shape = [jax.ShapeDtypeStruct((capacity, width), BF16)] * (2 * group) + [
        jax.ShapeDtypeStruct((width, LANES), F32)
    ]
    if trained:
        out_specs += [
            pl.BlockSpec((width, chunk), lambda f: (0, f)),
            pl.BlockSpec((chunk, width), lambda f: (f, 0)),
        ]
        out_shape += [
            jax.ShapeDtypeStruct((width, inner), BF16),
            jax.ShapeDtypeStruct((inner, width), BF16),
        ]
    return pl.pallas_call(
        functools.partial(expert_kernel, trained, group),
        grid=(inner // chunk,),
        in_specs=[smem()]
        + [pl.BlockSpec((1, capacity, width), lambda f: (place, 0, 0))] * group
        + [pl.BlockSpec((1, capacity, wide), lambda f: (place, 0, 0))] * group
        + [
            full((width, LANES)),
            full((LANES, width)),
            pl.BlockSpec((1, width, chunk), lambda f: (0, 0, f)),
            pl.BlockSpec((1, chunk, width), lambda f: (0, f, 0)),
        ],
        out_specs=out_specs,
        out_shape=out_shape,
        scratch_shapes=[
            pltpu.VMEM((many, width), BF16),
            pltpu.VMEM((many, width), BF16),
            pltpu.VMEM((many, LANES), F32),
            pltpu.VMEM((many, width), F32),
            pltpu.VMEM((many, width), F32),
            pltpu.VMEM((width, many), BF16),
        ],
        compiler_params=params(),
        name="experts_new" if trained else "experts_old",
    )(own, *rows, *grads, router, router_t, w_in, w_out)


def pick_matrix(slot_ref, total):
    place = lax.broadcasted_iota(jnp.int32, (slot_ref.shape[0], total), 1)
    hit = (place == slot_ref[:, 0:1]) | (place == slot_ref[:, 1:2])
    return jnp.where(hit, 1.0, 0.0).astype(BF16)


def pick_rows(slot_ref, part_refs):
    capacity = part_refs[0].shape[0]
    pick = pick_matrix(slot_ref, capacity * len(part_refs))
    total = jnp.zeros((slot_ref.shape[0], part_refs[0].shape[1]), F32)
    held = jnp.concatenate([part[...] for part in part_refs], axis=0)
    return total + dot_nn(pick, held)


def combine_kernel(count, slot_ref, res_ref, *refs):
    refs[count][...] = res_ref[...] + pick_rows(slot_ref, refs[:count])


def combine_call(slots, residual, parts):
    seq, width = residual.shape
    block = 256
    capacity = parts[0].shape[0]
    rows = pl.BlockSpec((block, width), lambda i: (i, 0))
    return pl.pallas_call(
        functools.partial(combine_kernel, len(parts)),
        grid=(seq // block,),
        in_specs=[pl.BlockSpec((block, LANES), lambda i: (i, 0)), rows]
        + [full((capacity, width))] * len(parts),
        out_specs=rows,
        out_shape=jax.ShapeDtypeStruct((seq, width), F32),
        compiler_params=params(),
        name="combine",
    )(slots, residual, *parts)


def middle_kernel(count, slot_ref, res_ref, cot_ref, gain_ref, mixed_ref, w_ref, *refs):
    parts = refs[:count]
    dres_ref, dmix_ref, proj_ref, sums_ref, acc_ref = refs[count:]
    step = pl.program_id(0)
    dnormed = pick_rows(slot_ref, parts)
    xhat, scale = norm_parts(res_ref[...])
    dres = cot_ref[...].astype(F32) + norm_back(dnormed, gain_ref[...], xhat, scale)
    dres_ref[...] = dres
    dattn = dres.astype(BF16)
    dmix_ref[...] = dot_nt(dattn, w_ref[...]).astype(BF16)

    @pl.when(step == 0)
    def _():
        sums_ref[...] = jnp.zeros_like(sums_ref)
        acc_ref[...] = jnp.zeros_like(acc_ref)

    acc_ref[...] += dot_tn(mixed_ref[...], dattn)
    sums_ref[0:1, :] += jnp.sum(dnormed * xhat, axis=0, keepdims=True)
    sums_ref[1:2, :] += jnp.sum(dnormed, axis=0, keepdims=True)

    @pl.when(step == pl.num_programs(0) - 1)
    def _():
        proj_ref[...] = acc_ref[...].astype(BF16)


def middle_call(slots, residual, cotangent, gain, mixed, weight, parts):
    seq, width = residual.shape
    block = 256
    capacity = parts[0].shape[0]
    rows = pl.BlockSpec((block, width), lambda i: (i, 0))
    return pl.pallas_call(
        functools.partial(middle_kernel, len(parts)),
        grid=(seq // block,),
        in_specs=[
            pl.BlockSpec((block, LANES), lambda i: (i, 0)),
            rows,
            rows,
            full((1, width)),
            rows,
            full((width, width)),
        ]
        + [full((capacity, width))] * len(parts),
        out_specs=[rows, rows, full((width, width)), full((8, width))],
        out_shape=[
            jax.ShapeDtypeStruct((seq, width), F32),
            jax.ShapeDtypeStruct((seq, width), BF16),
            jax.ShapeDtypeStruct((width, width), BF16),
            jax.ShapeDtypeStruct((8, width), F32),
        ],
        scratch_shapes=[pltpu.VMEM((width, width), F32)],
        compiler_params=params(),
        name="middle_back",
    )(slots, residual, cotangent, gain, mixed, weight, *parts)


def last_kernel(dqkv_ref, tok_ref, dres_ref, gain_ref, w_ref, out_ref, sums_ref):
    width = tok_ref.shape[1]
    dnormed = dot_nt(dqkv_ref[0], w_ref[:, :width])
    dnormed += dot_nt(dqkv_ref[1], w_ref[:, width : 2 * width])
    dnormed += dot_nt(dqkv_ref[2], w_ref[:, 2 * width :])
    xhat, scale = norm_parts(tok_ref[...].astype(F32))
    out_ref[...] = dres_ref[...] + norm_back(dnormed, gain_ref[...], xhat, scale)

    @pl.when(pl.program_id(0) == 0)
    def _():
        sums_ref[...] = jnp.zeros_like(sums_ref)

    sums_ref[0:1, :] += jnp.sum(dnormed * xhat, axis=0, keepdims=True)
    sums_ref[1:2, :] += jnp.sum(dnormed, axis=0, keepdims=True)


def last_call(dqkv, tokens, dres, gain, weight):
    seq, width = tokens.shape
    block = 256
    rows = pl.BlockSpec((block, width), lambda i: (i, 0))
    return pl.pallas_call(
        last_kernel,
        grid=(seq // block,),
        in_specs=[
            pl.BlockSpec((3, block, width), lambda i: (0, i, 0)),
            rows,
            rows,
            full((1, width)),
            full((width, 3 * width)),
        ],
        out_specs=[rows, full((8, width))],
        out_shape=[
            jax.ShapeDtypeStruct((seq, width), F32),
            jax.ShapeDtypeStruct((8, width), F32),
        ],
        compiler_params=params(),
        name="last_back",
    )(dqkv, tokens, dres, gain, weight)


def body(
    tokens,
    lengths,
    routes,
    ln1_gain,
    ln1_bias,
    ln2_gain,
    ln2_bias,
    w_qkv,
    w_proj,
    w_router,
    old_in,
    old_out,
    new_in,
    new_out,
    cotangent,
):
    group = lax.axis_size("expert")
    me = lax.axis_index("expert")
    token_rows = tokens[0]
    cot_rows = cotangent[0]
    seq, width = token_rows.shape
    experts = w_router.shape[1]
    local = experts // group
    per = old_in.shape[0]
    capacity = max(4, seq // experts)
    gain1, bias1 = ln1_gain[None], ln1_bias[None]
    gain2, bias2 = ln2_gain[None], ln2_bias[None]

    def go(block, shift):
        if shift == 0:
            return block
        return lax.ppermute(block, "expert", [(i, (i + shift) % group) for i in range(group)])

    def come(block, shift):
        if shift == 0:
            return block
        return lax.ppermute(block, "expert", [(i, (i - shift) % group) for i in range(group)])

    me_one = jnp.full((1,), me, jnp.int32)
    full_old_in = lax.all_gather(old_in, "batch", axis=1, tiled=True)
    full_old_out = lax.all_gather(old_out, "batch", axis=1, tiled=True)
    full_new_in = lax.all_gather(new_in, "batch", axis=1, tiled=True)
    full_new_out = lax.all_gather(new_out, "batch", axis=1, tiled=True)
    slots, slots_t, *sent_grads = route_call(
        lengths, me_one, routes[0], cot_rows, experts, group, capacity
    )
    grads = [go(block, shift) for shift, block in enumerate(sent_grads)]
    normed1, qkv = qkv_call(token_rows, gain1, bias1, w_qkv)
    mixed, lse = attend_call(lengths, qkv)
    residual, *sent_rows = project_call(
        mixed, token_rows, w_proj, gain2, bias2, slots, group, local, capacity
    )
    rows = [go(block, shift) for shift, block in enumerate(sent_rows)]
    router = jnp.pad(w_router, ((0, 0), (0, LANES - experts)))
    router_t = jnp.pad(w_router.T, ((0, LANES - experts), (0, 0)))
    outs, backs, router_sum = [], [], 0.0
    half = experts // 2
    for trained, w_in, w_out in ((False, full_old_in, full_old_out), (True, full_new_in, full_new_out)):
        for index in range(per):
            own = jnp.full((1,), me * per + index + (half if trained else 0), jnp.int32)
            got = expert_call(
                trained,
                index + (per if trained else 0),
                own,
                rows,
                grads,
                router,
                router_t,
                w_in[index : index + 1],
                w_out[index : index + 1],
            )
            outs.append(got[:group])
            backs.append(got[group : 2 * group])
            router_sum = router_sum + got[2 * group]
            if trained:
                new_in_local, new_out_local = got[2 * group + 1 :]
    returned = [come(backs[p][shift], shift) for shift in range(group) for p in range(local)]
    dres, dmixed, proj_grad, sums2 = middle_call(
        slots_t, residual, cot_rows, gain2, mixed, w_proj, returned
    )
    new_in_grad = lax.psum_scatter(new_in_local, "batch", scatter_dimension=0, tiled=True)
    new_out_grad = lax.psum_scatter(new_out_local, "batch", scatter_dimension=0, tiled=True)
    dqkv, qkv_grad = attend_back_call(lengths, qkv, dmixed, mixed, lse, normed1)
    big = lax.psum((qkv_grad, proj_grad), ("expert", "batch"))
    input_grad, sums1 = last_call(dqkv, token_rows, dres, gain1, w_qkv)
    back_outs = [come(outs[p][shift], shift) for shift in range(group) for p in range(local)]
    output = combine_call(slots_t, residual, back_outs)
    small = jnp.concatenate([router_sum.T[: 2 * 8], sums1, sums2], axis=0)
    small = jnp.sum(lax.all_gather(small, ("expert", "batch"), axis=0), axis=0)
    qkv_out = jnp.transpose(big[0].astype(F32), (1, 0, 2)).reshape(width, 3 * width)
    return (
        output[None],
        input_grad[None],
        small[16],
        small[17],
        small[24],
        small[25],
        qkv_out,
        big[1].astype(F32),
        small[:experts].T,
        new_in_grad.astype(F32)[None],
        new_out_grad.astype(F32)[None],
    )


def solution(mesh):
    rows = P(("expert", "batch"), None, None)
    weights = P("expert", "batch", None)
    placed = (
        (rows, P(("expert", "batch")), rows)
        + (P(),) * 7
        + (weights,) * 4
        + (rows,)
    )
    return jax.shard_map(
        body,
        mesh=mesh,
        in_specs=placed,
        out_specs=(rows, rows) + (P(),) * 7 + (weights, weights),
        check_vma=False,
    )
```

```python
import functools

import jax
import jax.numpy as jnp
from jax import lax
from jax.experimental import pallas as pl
from jax.experimental.pallas import tpu as pltpu
from jax.sharding import PartitionSpec as P

HEAD_DIM = 64
LANES = 128
EPS = 1e-05
MASKED = -1e30
F32 = jnp.float32
BF16 = jnp.bfloat16
VMEM_LIMIT = 56 * 1024 * 1024
BLOCKS = 32


def params():
    return pltpu.CompilerParams(vmem_limit_bytes=VMEM_LIMIT)


def dot_nt(left, right):
    return lax.dot_general(left, right, (((1,), (1,)), ((), ())), preferred_element_type=F32)


def dot_tn(left, right):
    return lax.dot_general(left, right, (((0,), (0,)), ((), ())), preferred_element_type=F32)


def dot_nn(left, right):
    return jnp.dot(left, right, preferred_element_type=F32)


def norm_parts(rows):
    mean = jnp.mean(rows, axis=-1, keepdims=True)
    centred = rows - mean
    var = jnp.mean(centred * centred, axis=-1, keepdims=True)
    scale = lax.rsqrt(var + EPS)
    return centred * scale, scale


def norm_back(grad, gain, xhat, scale):
    a = grad * gain
    mean_a = jnp.mean(a, axis=-1, keepdims=True)
    mean_ax = jnp.mean(a * xhat, axis=-1, keepdims=True)
    return scale * (a - mean_a - xhat * mean_ax)


def full(shape):
    return pl.BlockSpec(shape, lambda *_: (0,) * len(shape))


def smem():
    return pl.BlockSpec(memory_space=pltpu.SMEM)


def cost(micros):
    return pl.CostEstimate(flops=int(micros * 1.1e9), transcendentals=0, bytes_accessed=int(micros * 3e6))


def block_at(at_ref, chip, core, far):
    return (at_ref[0] ^ (2 * chip + core)) * 4 + ((at_ref[1] + far) & 3)


def qkv_kernel(tok_ref, gain_ref, bias_ref, w_ref, normed_ref, qkv_ref):
    xhat, _ = norm_parts(tok_ref[...].astype(F32))
    normed = (xhat * gain_ref[...] + bias_ref[...]).astype(BF16)
    normed_ref[...] = normed
    qkv_ref[...] = dot_nn(normed, w_ref[...]).astype(BF16)


def qkv_call(tokens, gain, bias, weight):
    seq, width = tokens.shape
    block = 256
    cols = weight.shape[1]
    return pl.pallas_call(
        qkv_kernel,
        grid=(seq // block,),
        in_specs=[
            pl.BlockSpec((block, width), lambda i: (i, 0)),
            full((1, width)),
            full((1, width)),
            full((width, cols)),
        ],
        out_specs=[
            pl.BlockSpec((block, width), lambda i: (i, 0)),
            pl.BlockSpec((block, cols), lambda i: (i, 0)),
        ],
        out_shape=[
            jax.ShapeDtypeStruct((seq, width), BF16),
            jax.ShapeDtypeStruct((seq, cols), BF16),
        ],
        compiler_params=params(),
        cost_estimate=cost(8.7),
        name="norm_qkv",
    )(tokens, gain, bias, weight)


def head_parts(head, length, q, k):
    seq = q.shape[0]
    lane = lax.broadcasted_iota(jnp.int32, (seq, LANES), 1)
    row = lax.broadcasted_iota(jnp.int32, (seq, LANES), 0)
    inside = (lane // HEAD_DIM) == head
    extra = lane == (1 - head) * HEAD_DIM
    key_bias = jnp.where(row >= length, MASKED, 0.0)
    kf = k.astype(F32)
    qf = q.astype(F32) * (HEAD_DIM**-0.5)
    k_head = jnp.where(inside, kf, jnp.where(extra, key_bias, 0.0)).astype(BF16)
    q_head = jnp.where(inside, qf, jnp.where(extra, 1.0, 0.0)).astype(BF16)
    return inside, k_head, q_head, jnp.where(inside, qf, 0.0).astype(BF16)


def causal(scores, block):
    key = lax.broadcasted_iota(jnp.int32, (block, block), 0)
    query = lax.broadcasted_iota(jnp.int32, (block, block), 1)
    last = jnp.where(key <= query, scores[-block:], MASKED)
    if scores.shape[0] == block:
        return last
    return jnp.concatenate([scores[:-block], last], axis=0)


def attend_kernel(len_ref, q_ref, k_ref, v_ref, out_ref, lse_ref, kh_ref, qh_ref, vt_ref, ot_ref):
    seq = q_ref.shape[0]
    block = 256
    length = len_ref[0]
    vt_ref[...] = v_ref[...].astype(F32).T.astype(BF16)
    lse_ref[...] = jnp.zeros_like(lse_ref)
    for head in range(2):
        _, k_head, q_head, _ = head_parts(head, length, q_ref[...], k_ref[...])
        kh_ref[...] = k_head
        qh_ref[...] = q_head
        for qb in range(seq // block):
            ext = (qb + 1) * block
            cols = slice(qb * block, ext)
            scores = causal(dot_nt(kh_ref[:ext, :], qh_ref[cols, :]), block)
            top = jnp.max(scores, axis=0, keepdims=True)
            probs = jnp.exp(scores - top)
            total = jnp.sum(probs, axis=0, keepdims=True)
            part = dot_nn(vt_ref[head * HEAD_DIM : (head + 1) * HEAD_DIM, :ext], probs.astype(BF16))
            ot_ref[head * HEAD_DIM : (head + 1) * HEAD_DIM, cols] = part * (1.0 / total)
            lse_ref[0, head : head + 1, cols] = top + jnp.log(total)
    out_ref[...] = ot_ref[...].T.astype(BF16)


def attend_call(length, qkv):
    seq = qkv.shape[0]
    width = qkv.shape[1] // 3
    pairs = width // LANES
    return pl.pallas_call(
        attend_kernel,
        grid=(pairs,),
        in_specs=[
            smem(),
            pl.BlockSpec((seq, LANES), lambda p: (0, p)),
            pl.BlockSpec((seq, LANES), lambda p: (0, pairs + p)),
            pl.BlockSpec((seq, LANES), lambda p: (0, 2 * pairs + p)),
        ],
        out_specs=[
            pl.BlockSpec((seq, LANES), lambda p: (0, p)),
            pl.BlockSpec((1, 8, seq), lambda p: (p, 0, 0)),
        ],
        out_shape=[
            jax.ShapeDtypeStruct((seq, width), BF16),
            jax.ShapeDtypeStruct((pairs, 8, seq), F32),
        ],
        scratch_shapes=[
            pltpu.VMEM((seq, LANES), BF16),
            pltpu.VMEM((seq, LANES), BF16),
            pltpu.VMEM((LANES, seq), BF16),
            pltpu.VMEM((LANES, seq), F32),
        ],
        compiler_params=params(),
        cost_estimate=cost(24),
        name="attend",
    )(length, qkv, qkv, qkv)


def attend_back_kernel(
    len_ref,
    q_ref,
    k_ref,
    v_ref,
    do_ref,
    o_ref,
    lse_ref,
    normed_ref,
    at_ref,
    dqkv_ref,
    keep_ref,
    send_ref,
    nt_ref,
    kt_ref,
    kh_ref,
    qh_ref,
    qm_ref,
    vh_ref,
    dh_ref,
    dk_ref,
    dv_ref,
    dqt_ref,
    pt_ref,
    join_ref,
):
    seq = q_ref.shape[0]
    block = 256
    length = len_ref[0]

    @pl.when(pl.program_id(0) == 0)
    def _():
        nt_ref[...] = normed_ref[...].astype(F32).T.astype(BF16)

    kt_ref[...] = k_ref[...].astype(F32).T.astype(BF16)
    pt_ref[...] = (do_ref[...].astype(F32) * o_ref[...].astype(F32)).T
    dk_ref[...] = jnp.zeros_like(dk_ref)
    dv_ref[...] = jnp.zeros_like(dv_ref)
    for head in range(2):
        rows = slice(head * HEAD_DIM, (head + 1) * HEAD_DIM)
        inside, k_head, q_head, q_masked = head_parts(head, length, q_ref[...], k_ref[...])
        kh_ref[...] = k_head
        qh_ref[...] = q_head
        qm_ref[...] = q_masked
        vh_ref[...] = jnp.where(inside, v_ref[...].astype(F32), 0.0).astype(BF16)
        dh_ref[...] = jnp.where(inside, do_ref[...].astype(F32), 0.0).astype(BF16)
        for qb in range(seq // block):
            ext = (qb + 1) * block
            cols = slice(qb * block, ext)
            delta = jnp.sum(pt_ref[rows, cols], axis=0, keepdims=True)
            scores = causal(dot_nt(kh_ref[:ext, :], qh_ref[cols, :]), block)
            probs = jnp.exp(scores - lse_ref[0, head : head + 1, cols])
            dprobs = dot_nt(vh_ref[:ext, :], dh_ref[cols, :])
            dscores = (probs * (dprobs - delta)).astype(BF16)
            dv_ref[:ext, :] += dot_nn(probs.astype(BF16), dh_ref[cols, :])
            dk_ref[:ext, :] += dot_nn(dscores, qm_ref[cols, :])
            dqt_ref[rows, cols] = dot_nn(kt_ref[rows, :ext], dscores)
    dq = (dqt_ref[...].T * (HEAD_DIM**-0.5)).astype(BF16)
    dk = dk_ref[...].astype(BF16)
    dv = dv_ref[...].astype(BF16)
    dqkv_ref[0] = dq
    dqkv_ref[1] = dk
    dqkv_ref[2] = dv
    joined = dot_nn(nt_ref[...], jnp.concatenate([dq, dk, dv], axis=1))
    join_ref[...] = joined.reshape(join_ref.shape)
    for chip in range(4):
        for far in range(4):
            for core, ref in enumerate((keep_ref, send_ref)):
                piece = join_ref[block_at(at_ref, chip, core, far)].astype(BF16)
                for part in range(3):
                    ref[chip, far, part] = piece[:, part * LANES : (part + 1) * LANES]


def attend_back_call(length, qkv, dmixed, mixed, lse, normed, at):
    seq, width = normed.shape
    pairs = width // LANES
    tall = width // BLOCKS
    col = lambda p: (0, p)
    return pl.pallas_call(
        attend_back_kernel,
        grid=(pairs,),
        in_specs=[
            smem(),
            pl.BlockSpec((seq, LANES), col),
            pl.BlockSpec((seq, LANES), lambda p: (0, pairs + p)),
            pl.BlockSpec((seq, LANES), lambda p: (0, 2 * pairs + p)),
            pl.BlockSpec((seq, LANES), col),
            pl.BlockSpec((seq, LANES), col),
            pl.BlockSpec((1, 8, seq), lambda p: (p, 0, 0)),
            full((seq, width)),
            smem(),
        ],
        out_specs=[pl.BlockSpec((3, seq, LANES), lambda p: (0, 0, p))]
        + [pl.BlockSpec((4, 4, 3, tall, LANES), lambda p: (0, 0, 0, 0, p))] * 2,
        out_shape=[jax.ShapeDtypeStruct((3, seq, width), BF16)]
        + [jax.ShapeDtypeStruct((4, 4, 3, tall, width), BF16)] * 2,
        scratch_shapes=[
            pltpu.VMEM((width, seq), BF16),
            pltpu.VMEM((LANES, seq), BF16),
            pltpu.VMEM((seq, LANES), BF16),
            pltpu.VMEM((seq, LANES), BF16),
            pltpu.VMEM((seq, LANES), BF16),
            pltpu.VMEM((seq, LANES), BF16),
            pltpu.VMEM((seq, LANES), BF16),
            pltpu.VMEM((seq, LANES), F32),
            pltpu.VMEM((seq, LANES), F32),
            pltpu.VMEM((LANES, seq), F32),
            pltpu.VMEM((LANES, seq), F32),
            pltpu.VMEM((BLOCKS, tall, 3 * LANES), F32),
        ],
        compiler_params=params(),
        cost_estimate=cost(32),
        name="attend_back",
    )(length, qkv, qkv, qkv, dmixed, mixed, lse, normed, at)


def route_kernel(
    experts, group, capacity, len_ref, me_ref, route_ref, pair_ref, cot_ref, slot_ref, slot_t_ref, *out_refs
):
    seq = route_ref.shape[1]
    half = experts // 2
    per = half // group
    local = 2 * per
    length = len_ref[0]
    me = me_ref[0]
    live = lax.broadcasted_iota(jnp.int32, (1, seq), 1) < length
    ids = lax.broadcasted_iota(jnp.int32, (experts, seq), 0)
    upper = (
        lax.broadcasted_iota(jnp.int32, (seq, seq), 0) < lax.broadcasted_iota(jnp.int32, (seq, seq), 1)
    )
    upper = jnp.where(upper, 1.0, 0.0).astype(BF16)
    before = jnp.zeros((experts, 1), F32)
    slots = []
    for choice in range(2):
        named = route_ref[choice : choice + 1, :]
        hot = jnp.where((ids == named) & live, 1.0, 0.0)
        earlier = dot_nn(hot.astype(BF16), upper) + before
        rank = jnp.sum(hot * earlier, axis=0, keepdims=True).astype(jnp.int32)
        before = before + jnp.sum(hot, axis=1, keepdims=True)
        is_new = named >= half
        within = jnp.where(is_new, named - half, named)
        owner = within // per
        place = jnp.where(is_new, per, 0) + within - owner * per
        shift = owner - me
        shift = jnp.where(shift < 0, shift + group, shift)
        slot = (shift * local + place) * capacity + rank
        slots.append(jnp.where(live & (rank < capacity), slot, -1))
    slot_ref[...] = jnp.concatenate(slots + [jnp.full((6, seq), -1, jnp.int32)], axis=0)
    slot_t_ref[...] = jnp.concatenate(
        [slot.astype(F32) for slot in slots] + [jnp.full((LANES - 2, seq), -1.0, F32)], axis=0
    ).T.astype(jnp.int32)
    total = experts * capacity
    place = lax.broadcasted_iota(jnp.int32, (total, seq), 0)
    select = jnp.where((place == slots[0]) | (place == slots[1]), 1.0, 0.0).astype(BF16)
    rows = dot_nn(select, cot_ref[...]).astype(BF16)
    both = (pair_ref[:, 0:1] + pair_ref[:, 1:2]).astype(F32)
    lane = lax.broadcasted_iota(jnp.int32, (seq, LANES), 1)
    tail = dot_nn(select, jnp.where(lane == 0, both, 0.0).astype(BF16)).astype(BF16)
    width = cot_ref.shape[1]
    size = local * capacity
    for shift in range(group):
        piece = slice(shift * size, (shift + 1) * size)
        out_refs[shift][:, :, :width] = rows[piece].reshape(local, capacity, width)
        out_refs[shift][:, :, width:] = tail[piece].reshape(local, capacity, LANES)


def route_call(length, me, routes, cotangent, experts, group, capacity):
    seq, width = cotangent.shape
    local = experts // group
    wide = width + LANES
    return pl.pallas_call(
        functools.partial(route_kernel, experts, group, capacity),
        in_specs=[smem(), smem(), full((2, seq)), full((seq, 2)), full((seq, width))],
        out_specs=[full((8, seq)), full((seq, LANES))] + [full((local, capacity, wide))] * group,
        out_shape=[
            jax.ShapeDtypeStruct((8, seq), jnp.int32),
            jax.ShapeDtypeStruct((seq, LANES), jnp.int32),
        ]
        + [jax.ShapeDtypeStruct((local, capacity, wide), BF16)] * group,
        grid=(1,),
        compiler_params=params(),
        cost_estimate=cost(5.7),
        name="route",
    )(length, me, routes.T, routes, cotangent)


def project_kernel(
    group, mixed_ref, tok_ref, w_ref, gain_ref, bias_ref, slot_ref, res_ref, *refs
):
    out_refs = refs[:group]
    normed_ref = refs[group]
    step = pl.program_id(0)
    block = mixed_ref.shape[0]
    residual = tok_ref[...].astype(F32) + dot_nn(mixed_ref[...], w_ref[...])
    res_ref[...] = residual
    xhat, _ = norm_parts(residual)
    normed = (xhat * gain_ref[...] + bias_ref[...]).astype(BF16)
    normed_ref[pl.ds(pl.multiple_of(step * block, block), block), :] = normed

    @pl.when(step == pl.num_programs(0) - 1)
    def _():
        local, capacity, width = out_refs[0].shape
        size = local * capacity
        seq = normed_ref.shape[0]
        place = lax.broadcasted_iota(jnp.int32, (size * group, seq), 0)
        select = (place == slot_ref[0:1, :]) | (place == slot_ref[1:2, :])
        select = jnp.where(select, 1.0, 0.0).astype(BF16)
        rows = dot_nn(select, normed_ref[...]).astype(BF16)
        for shift in range(group):
            out_refs[shift][...] = rows[shift * size : (shift + 1) * size].reshape(local, capacity, width)


def project_call(mixed, tokens, weight, gain, bias, slots, group, local, capacity):
    seq, width = tokens.shape
    block = 256
    rows = pl.BlockSpec((block, width), lambda i: (i, 0))
    return pl.pallas_call(
        functools.partial(project_kernel, group),
        grid=(seq // block,),
        in_specs=[rows, rows, full((width, width)), full((1, width)), full((1, width)), full((8, seq))],
        out_specs=[rows] + [full((local, capacity, width))] * group,
        out_shape=[jax.ShapeDtypeStruct((seq, width), F32)]
        + [jax.ShapeDtypeStruct((local, capacity, width), BF16)] * group,
        scratch_shapes=[pltpu.VMEM((seq, width), BF16)],
        compiler_params=params(),
        cost_estimate=cost(8.8),
        name="project_dispatch",
    )(mixed, tokens, weight, gain, bias, slots)


def expert_kernel(trained, group, own_ref, *refs):
    x_refs = refs[:group]
    g_refs = refs[group : 2 * group]
    wr_ref, wrt_ref, win_ref, wout_ref = refs[2 * group : 2 * group + 4]
    rest = refs[2 * group + 4 :]
    out_refs = rest[:group]
    back_refs = rest[group : 2 * group]
    router_ref = rest[2 * group]
    rest = rest[2 * group + 1 :]
    if trained:
        din_ref, dout_ref = rest[:2]
        rest = rest[2:]
    x_ref, dexp_ref, gate_ref, acc_ref, back_ref, xt_ref = rest
    step = pl.program_id(0)
    capacity, width = out_refs[0].shape
    own = own_ref[0]

    def other_of(tail):
        return tail[:, 0:1].astype(F32).astype(jnp.int32) - own

    @pl.when(step == 0)
    def _():
        for shift in range(group):
            span = slice(shift * capacity, (shift + 1) * capacity)
            rows = x_refs[shift][0]
            x_ref[span, :] = rows
            logits = dot_nn(rows, wr_ref[...])
            lane = lax.broadcasted_iota(jnp.int32, logits.shape, 1)
            other = other_of(g_refs[shift][0, :, width:])
            mine = jnp.sum(jnp.where(lane == own, logits, 0.0), axis=1, keepdims=True)
            theirs = jnp.sum(jnp.where(lane == other, logits, 0.0), axis=1, keepdims=True)
            top = jnp.maximum(mine, theirs)
            up = jnp.exp(mine - top)
            gate = up / (up + jnp.exp(theirs - top))
            gate_ref[span, :] = jnp.broadcast_to(gate, (capacity, LANES))
            dexp_ref[span, :] = (gate * g_refs[shift][0, :, :width].astype(F32)).astype(BF16)
        acc_ref[...] = jnp.zeros_like(acc_ref)
        back_ref[...] = jnp.zeros_like(back_ref)
        xt_ref[...] = x_ref[...].astype(F32).T.astype(BF16)

    win = win_ref[0]
    wout = wout_ref[0]
    pre = dot_nn(x_ref[...], win)
    square = pre * pre
    tanh = jnp.tanh(0.7978845608028654 * (pre + 0.044715 * pre * square))
    half = 0.5 * (1.0 + tanh)
    hid = (pre * half).astype(BF16)
    slope = half + (0.5 * pre) * (1.0 - tanh * tanh) * (0.7978845608028654 + 0.1070322243 * square)
    acc_ref[...] += dot_nn(hid, wout)
    dpre = (dot_nt(dexp_ref[...], wout) * slope).astype(BF16)
    back_ref[...] += dot_nt(dpre, win)
    if trained:
        dout_ref[...] = dot_tn(hid, dexp_ref[...]).astype(BF16)
        din_ref[...] = dot_nn(xt_ref[...], dpre).astype(BF16)

    @pl.when(step == pl.num_programs(0) - 1)
    def _():
        router = jnp.zeros((width, LANES), F32)
        for shift in range(group):
            span = slice(shift * capacity, (shift + 1) * capacity)
            gate = gate_ref[span, 0:1]
            result = acc_ref[span, :]
            out_refs[shift][...] = (gate * result).astype(BF16)
            dot = jnp.sum(result * g_refs[shift][0, :, :width].astype(F32), axis=1, keepdims=True)
            coef = gate * (1.0 - gate) * dot
            lane = lax.broadcasted_iota(jnp.int32, (capacity, LANES), 1)
            other = other_of(g_refs[shift][0, :, width:])
            sign = jnp.where(lane == own, 1.0, 0.0) - jnp.where(lane == other, 1.0, 0.0)
            dlogits = (coef * sign).astype(BF16)
            back_refs[shift][...] = (back_ref[span, :] + dot_nn(dlogits, wrt_ref[...])).astype(BF16)
            router = router + dot_nn(xt_ref[:, span], dlogits)
        router_ref[...] = router


def expert_call(trained, place, own, rows, grads, router, router_t, w_in, w_out):
    group = len(rows)
    _, capacity, width = rows[0].shape
    inner = w_in.shape[2]
    chunk = 512
    wide = grads[0].shape[2]
    many = group * capacity
    fixed = full((capacity, width))
    out_specs = [fixed] * (2 * group) + [full((width, LANES))]
    out_shape = [jax.ShapeDtypeStruct((capacity, width), BF16)] * (2 * group) + [
        jax.ShapeDtypeStruct((width, LANES), F32)
    ]
    if trained:
        out_specs += [
            pl.BlockSpec((width, chunk), lambda f: (0, f)),
            pl.BlockSpec((chunk, width), lambda f: (f, 0)),
        ]
        out_shape += [
            jax.ShapeDtypeStruct((width, inner), BF16),
            jax.ShapeDtypeStruct((inner, width), BF16),
        ]
    return pl.pallas_call(
        functools.partial(expert_kernel, trained, group),
        grid=(inner // chunk,),
        in_specs=[smem()]
        + [pl.BlockSpec((1, capacity, width), lambda f: (place, 0, 0))] * group
        + [pl.BlockSpec((1, capacity, wide), lambda f: (place, 0, 0))] * group
        + [
            full((width, LANES)),
            full((LANES, width)),
            pl.BlockSpec((1, width, chunk), lambda f: (0, 0, f)),
            pl.BlockSpec((1, chunk, width), lambda f: (0, f, 0)),
        ],
        out_specs=out_specs,
        out_shape=out_shape,
        scratch_shapes=[
            pltpu.VMEM((many, width), BF16),
            pltpu.VMEM((many, width), BF16),
            pltpu.VMEM((many, LANES), F32),
            pltpu.VMEM((many, width), F32),
            pltpu.VMEM((many, width), F32),
            pltpu.VMEM((width, many), BF16),
        ],
        compiler_params=params(),
        cost_estimate=cost(23 if trained else 17),
        name="experts_new" if trained else "experts_old",
    )(own, *rows, *grads, router, router_t, w_in, w_out)


def pick_matrix(slot_ref, total):
    place = lax.broadcasted_iota(jnp.int32, (slot_ref.shape[0], total), 1)
    hit = (place == slot_ref[:, 0:1]) | (place == slot_ref[:, 1:2])
    return jnp.where(hit, 1.0, 0.0).astype(BF16)


def pick_rows(slot_ref, part_refs):
    capacity = part_refs[0].shape[0]
    pick = pick_matrix(slot_ref, capacity * len(part_refs))
    total = jnp.zeros((slot_ref.shape[0], part_refs[0].shape[1]), F32)
    held = jnp.concatenate([part[...] for part in part_refs], axis=0)
    return total + dot_nn(pick, held)


def combine_kernel(count, slot_ref, res_ref, *refs):
    refs[count][...] = res_ref[...] + pick_rows(slot_ref, refs[:count])


def combine_call(slots, residual, parts):
    seq, width = residual.shape
    block = 256
    capacity = parts[0].shape[0]
    rows = pl.BlockSpec((block, width), lambda i: (i, 0))
    return pl.pallas_call(
        functools.partial(combine_kernel, len(parts)),
        grid=(seq // block,),
        in_specs=[pl.BlockSpec((block, LANES), lambda i: (i, 0)), rows]
        + [full((capacity, width))] * len(parts),
        out_specs=rows,
        out_shape=jax.ShapeDtypeStruct((seq, width), F32),
        compiler_params=params(),
        cost_estimate=cost(6.2),
        name="combine",
    )(slots, residual, *parts)


def middle_kernel(count, slot_ref, res_ref, cot_ref, gain_ref, mixed_ref, w_ref, at_ref, *refs):
    parts = refs[:count]
    dres_ref, dmix_ref, keep_ref, send_ref, sums_ref, acc_ref = refs[count:]
    step = pl.program_id(0)
    dnormed = pick_rows(slot_ref, parts)
    xhat, scale = norm_parts(res_ref[...])
    dres = cot_ref[...].astype(F32) + norm_back(dnormed, gain_ref[...], xhat, scale)
    dres_ref[...] = dres
    dattn = dres.astype(BF16)
    dmix_ref[...] = dot_nt(dattn, w_ref[...]).astype(BF16)

    @pl.when(step == 0)
    def _():
        sums_ref[...] = jnp.zeros_like(sums_ref)
        acc_ref[...] = jnp.zeros_like(acc_ref)

    acc_ref[...] += dot_tn(mixed_ref[...], dattn).reshape(acc_ref.shape)
    sums_ref[0:1, :] += jnp.sum(dnormed * xhat, axis=0, keepdims=True)
    sums_ref[1:2, :] += jnp.sum(dnormed, axis=0, keepdims=True)

    @pl.when(step == pl.num_programs(0) - 1)
    def _():
        for chip in range(4):
            for far in range(4):
                for core, ref in enumerate((keep_ref, send_ref)):
                    ref[chip, far, 0] = acc_ref[block_at(at_ref, chip, core, far)].astype(BF16)


def middle_call(slots, residual, cotangent, gain, mixed, weight, at, parts):
    seq, width = residual.shape
    tall = width // BLOCKS
    block = 256
    capacity = parts[0].shape[0]
    rows = pl.BlockSpec((block, width), lambda i: (i, 0))
    return pl.pallas_call(
        functools.partial(middle_kernel, len(parts)),
        grid=(seq // block,),
        in_specs=[
            pl.BlockSpec((block, LANES), lambda i: (i, 0)),
            rows,
            rows,
            full((1, width)),
            rows,
            full((width, width)),
            smem(),
        ]
        + [full((capacity, width))] * len(parts),
        out_specs=[rows, rows] + [full((4, 4, 1, tall, width))] * 2 + [full((8, width))],
        out_shape=[
            jax.ShapeDtypeStruct((seq, width), F32),
            jax.ShapeDtypeStruct((seq, width), BF16),
            jax.ShapeDtypeStruct((4, 4, 1, tall, width), BF16),
            jax.ShapeDtypeStruct((4, 4, 1, tall, width), BF16),
            jax.ShapeDtypeStruct((8, width), F32),
        ],
        scratch_shapes=[pltpu.VMEM((BLOCKS, tall, width), F32)],
        compiler_params=params(),
        cost_estimate=cost(13),
        name="middle_back",
    )(slots, residual, cotangent, gain, mixed, weight, at, *parts)


def last_kernel(dqkv_ref, tok_ref, dres_ref, gain_ref, w_ref, out_ref, sums_ref):
    width = tok_ref.shape[1]
    dnormed = dot_nt(dqkv_ref[0], w_ref[:, :width])
    dnormed += dot_nt(dqkv_ref[1], w_ref[:, width : 2 * width])
    dnormed += dot_nt(dqkv_ref[2], w_ref[:, 2 * width :])
    xhat, scale = norm_parts(tok_ref[...].astype(F32))
    out_ref[...] = dres_ref[...] + norm_back(dnormed, gain_ref[...], xhat, scale)

    @pl.when(pl.program_id(0) == 0)
    def _():
        sums_ref[...] = jnp.zeros_like(sums_ref)

    sums_ref[0:1, :] += jnp.sum(dnormed * xhat, axis=0, keepdims=True)
    sums_ref[1:2, :] += jnp.sum(dnormed, axis=0, keepdims=True)


def last_call(dqkv, tokens, dres, gain, weight):
    seq, width = tokens.shape
    block = 256
    rows = pl.BlockSpec((block, width), lambda i: (i, 0))
    return pl.pallas_call(
        last_kernel,
        grid=(seq // block,),
        in_specs=[
            pl.BlockSpec((3, block, width), lambda i: (0, i, 0)),
            rows,
            rows,
            full((1, width)),
            full((width, 3 * width)),
        ],
        out_specs=[rows, full((8, width))],
        out_shape=[
            jax.ShapeDtypeStruct((seq, width), F32),
            jax.ShapeDtypeStruct((8, width), F32),
        ],
        compiler_params=params(),
        cost_estimate=cost(9.8),
        name="last_back",
    )(dqkv, tokens, dres, gain, weight)


def unpack_kernel(at_ref, *refs):
    pieces = refs[:8]
    qkv_ref, proj_ref = refs[8:]
    tall = pieces[0].shape[2]
    part = pl.program_id(0)

    def put(out_ref):
        for index, piece in enumerate(pieces):
            for far in range(4):
                place = (at_ref[0] ^ index) * 4 + ((at_ref[1] - far) & 3)
                rows = pl.ds(pl.multiple_of(place * tall, 8), tall)
                out_ref[rows, :] = piece[far, 0].astype(F32)

    @pl.when(part < 3)
    def _():
        put(qkv_ref)

    @pl.when(part == 3)
    def _():
        put(proj_ref)


def unpack_call(at, pieces):
    _, _, tall, width = pieces[0].shape
    return pl.pallas_call(
        unpack_kernel,
        grid=(4,),
        in_specs=[smem()] + [pl.BlockSpec((4, 1, tall, width), lambda p: (0, p, 0, 0))] * 8,
        out_specs=[
            pl.BlockSpec((width, width), lambda p: (0, jnp.minimum(p, 2))),
            full((width, width)),
        ],
        out_shape=[
            jax.ShapeDtypeStruct((width, 3 * width), F32),
            jax.ShapeDtypeStruct((width, width), F32),
        ],
        compiler_params=params(),
        cost_estimate=cost(6),
        name="unpack",
    )(at, *pieces)


def swap(block, bits):
    size = lax.axis_size("batch")
    return lax.ppermute(block, "batch", [(i, i ^ bits) for i in range(size)])


def turn(block, shift):
    size = lax.axis_size("expert")
    return lax.ppermute(block, "expert", [(i, (i + shift) % size) for i in range(size)])


def added(*blocks):
    total = blocks[0].astype(F32)
    for block in blocks[1:]:
        total = total + block.astype(F32)
    return total


def sum_dense(fast, keep, send):
    if not fast:
        keep, send = lax.psum((keep, send), ("expert", "batch"))
        pieces = []
        for chip in range(4):
            for half in (keep, send):
                parts = jnp.concatenate([part[chip] for part in half], axis=1)
                pieces.append(jnp.stack([parts[-far % 4] for far in range(4)]))
        return pieces
    got = [swap(part, 1) for part in send]
    halves = []
    for chip in range(4):
        parts = [added(mine[chip], other[chip]) for mine, other in zip(keep, got)]
        halves.append(jnp.concatenate(parts, axis=1).astype(BF16))
    quarter = added(halves[0], *[swap(halves[chip], 2 * chip) for chip in (1, 2, 3)]).astype(BF16)
    own = added(quarter[0], *[turn(quarter[far], far) for far in (1, 2, 3)]).astype(BF16)
    column = jnp.stack([own] + [turn(own, far) for far in (1, 2, 3)])
    chips = [column] + [swap(column, 2 * chip) for chip in (1, 2, 3)]
    pieces = []
    for block in chips:
        pieces += [block, swap(block, 1)]
    return pieces


def sum_small(fast, rows):
    if not fast:
        return jnp.sum(lax.all_gather(rows, ("expert", "batch"), axis=0), axis=0)
    rows = rows + swap(rows, 1)
    rows = added(rows, *[swap(rows, 2 * chip) for chip in (1, 2, 3)])
    return added(rows, *[turn(rows, far) for far in (1, 2, 3)])


def body(
    tokens,
    lengths,
    routes,
    ln1_gain,
    ln1_bias,
    ln2_gain,
    ln2_bias,
    w_qkv,
    w_proj,
    w_router,
    old_in,
    old_out,
    new_in,
    new_out,
    cotangent,
):
    group = lax.axis_size("expert")
    me = lax.axis_index("expert")
    token_rows = tokens[0]
    cot_rows = cotangent[0]
    seq, width = token_rows.shape
    experts = w_router.shape[1]
    local = experts // group
    per = old_in.shape[0]
    capacity = max(4, seq // experts)
    gain1, bias1 = ln1_gain[None], ln1_bias[None]
    gain2, bias2 = ln2_gain[None], ln2_bias[None]

    def go(block, shift):
        if shift == 0:
            return block
        return lax.ppermute(block, "expert", [(i, (i + shift) % group) for i in range(group)])

    def come(block, shift):
        if shift == 0:
            return block
        return lax.ppermute(block, "expert", [(i, (i - shift) % group) for i in range(group)])

    fast = group == 4 and lax.axis_size("batch") == 8
    at = jnp.stack([lax.axis_index("batch"), me]).astype(jnp.int32) if fast else jnp.zeros((2,), jnp.int32)
    me_one = jnp.full((1,), me, jnp.int32)
    full_old_in = lax.all_gather(old_in, "batch", axis=1, tiled=True)
    full_old_out = lax.all_gather(old_out, "batch", axis=1, tiled=True)
    full_new_in = lax.all_gather(new_in, "batch", axis=1, tiled=True)
    full_new_out = lax.all_gather(new_out, "batch", axis=1, tiled=True)
    slots, slots_t, *sent_grads = route_call(
        lengths, me_one, routes[0], cot_rows, experts, group, capacity
    )
    grads = [go(block, shift) for shift, block in enumerate(sent_grads)]
    normed1, qkv = qkv_call(token_rows, gain1, bias1, w_qkv)
    mixed, lse = attend_call(lengths, qkv)
    residual, *sent_rows = project_call(
        mixed, token_rows, w_proj, gain2, bias2, slots, group, local, capacity
    )
    rows = [go(block, shift) for shift, block in enumerate(sent_rows)]
    router = jnp.pad(w_router, ((0, 0), (0, LANES - experts)))
    router_t = jnp.pad(w_router.T, ((0, LANES - experts), (0, 0)))
    outs, backs, router_sum = [], [], 0.0
    half = experts // 2
    for trained, w_in, w_out in ((False, full_old_in, full_old_out), (True, full_new_in, full_new_out)):
        for index in range(per):
            own = jnp.full((1,), me * per + index + (half if trained else 0), jnp.int32)
            got = expert_call(
                trained,
                index + (per if trained else 0),
                own,
                rows,
                grads,
                router,
                router_t,
                w_in[index : index + 1],
                w_out[index : index + 1],
            )
            outs.append(got[:group])
            backs.append(got[group : 2 * group])
            router_sum = router_sum + got[2 * group]
            if trained:
                new_in_local, new_out_local = got[2 * group + 1 :]
    returned = [come(backs[p][shift], shift) for shift in range(group) for p in range(local)]
    dres, dmixed, proj_keep, proj_send, sums2 = middle_call(
        slots_t, residual, cot_rows, gain2, mixed, w_proj, at, returned
    )
    new_in_grad = lax.psum_scatter(new_in_local, "batch", scatter_dimension=0, tiled=True)
    new_out_grad = lax.psum_scatter(new_out_local, "batch", scatter_dimension=0, tiled=True)
    dqkv, qkv_keep, qkv_send = attend_back_call(lengths, qkv, dmixed, mixed, lse, normed1, at)
    pieces = sum_dense(fast, (qkv_keep, proj_keep), (qkv_send, proj_send))
    qkv_grad, proj_grad = unpack_call(at, pieces)
    input_grad, sums1 = last_call(dqkv, token_rows, dres, gain1, w_qkv)
    back_outs = [come(outs[p][shift], shift) for shift in range(group) for p in range(local)]
    output = combine_call(slots_t, residual, back_outs)
    small = sum_small(fast, jnp.concatenate([router_sum.T[:experts], sums1, sums2], axis=0))
    return (
        output[None],
        input_grad[None],
        small[experts],
        small[experts + 1],
        small[experts + 8],
        small[experts + 9],
        qkv_grad,
        proj_grad,
        small[:experts].T,
        new_in_grad.astype(F32)[None],
        new_out_grad.astype(F32)[None],
    )


def solution(mesh):
    rows = P(("expert", "batch"), None, None)
    weights = P("expert", "batch", None)
    placed = (
        (rows, P(("expert", "batch")), rows)
        + (P(),) * 7
        + (weights,) * 4
        + (rows,)
    )
    return jax.shard_map(
        body,
        mesh=mesh,
        in_specs=placed,
        out_specs=(rows, rows) + (P(),) * 7 + (weights, weights),
        check_vma=False,
    )
```

```python
import functools

import jax
import jax.numpy as jnp
from jax import lax
from jax.experimental import pallas as pl
from jax.experimental.pallas import tpu as pltpu
from jax.sharding import PartitionSpec as P

HEAD_DIM = 64
LANES = 128
EPS = 1e-05
MASKED = -1e30
F32 = jnp.float32
BF16 = jnp.bfloat16
VMEM_LIMIT = 56 * 1024 * 1024
BLOCKS = 32
FAR = (0, 2, 1, 3)
PLACES = ((0, 0), (1, 0), (2, 0), (3, 0), (3, 1))


def params():
    return pltpu.CompilerParams(vmem_limit_bytes=VMEM_LIMIT)


def dot_nt(left, right):
    return lax.dot_general(left, right, (((1,), (1,)), ((), ())), preferred_element_type=F32)


def dot_tn(left, right):
    return lax.dot_general(left, right, (((0,), (0,)), ((), ())), preferred_element_type=F32)


def dot_nn(left, right):
    return jnp.dot(left, right, preferred_element_type=F32)


def norm_parts(rows):
    mean = jnp.mean(rows, axis=-1, keepdims=True)
    centred = rows - mean
    var = jnp.mean(centred * centred, axis=-1, keepdims=True)
    scale = lax.rsqrt(var + EPS)
    return centred * scale, scale


def norm_back(grad, gain, xhat, scale):
    a = grad * gain
    mean_a = jnp.mean(a, axis=-1, keepdims=True)
    mean_ax = jnp.mean(a * xhat, axis=-1, keepdims=True)
    return scale * (a - mean_a - xhat * mean_ax)


def full(shape):
    return pl.BlockSpec(shape, lambda *_: (0,) * len(shape))


def smem():
    return pl.BlockSpec(memory_space=pltpu.SMEM)


def cost(micros):
    return pl.CostEstimate(flops=int(micros * 1.1e9), transcendentals=0, bytes_accessed=int(micros * 3e6))


def block_at(at_ref, chip, core, far):
    return (at_ref[0] ^ (2 * chip + core)) * 4 + (at_ref[1] ^ FAR[far])


def qkv_kernel(tok_ref, scale_ref, w_ref, normed_ref, qkv_ref):
    xhat, _ = norm_parts(tok_ref[...].astype(F32))
    normed = (xhat * scale_ref[0:1, :] + scale_ref[1:2, :]).astype(BF16)
    normed_ref[...] = normed
    qkv_ref[...] = dot_nn(normed, w_ref[...]).astype(BF16)


def qkv_call(tokens, scales, weight):
    seq, width = tokens.shape
    block = 256
    cols = weight.shape[1]
    return pl.pallas_call(
        qkv_kernel,
        grid=(seq // block,),
        in_specs=[
            pl.BlockSpec((block, width), lambda i: (i, 0)),
            full((4, width)),
            full((width, cols)),
        ],
        out_specs=[
            pl.BlockSpec((block, width), lambda i: (i, 0)),
            pl.BlockSpec((block, cols), lambda i: (i, 0)),
        ],
        out_shape=[
            jax.ShapeDtypeStruct((seq, width), BF16),
            jax.ShapeDtypeStruct((seq, cols), BF16),
        ],
        compiler_params=params(),
        cost_estimate=cost(8.7),
        name="norm_qkv",
    )(tokens, scales, weight)


def head_parts(head, length, q, k):
    seq = q.shape[0]
    lane = lax.broadcasted_iota(jnp.int32, (seq, LANES), 1)
    row = lax.broadcasted_iota(jnp.int32, (seq, LANES), 0)
    inside = (lane // HEAD_DIM) == head
    extra = lane == (1 - head) * HEAD_DIM
    key_bias = jnp.where(row >= length, MASKED, 0.0)
    kf = k.astype(F32)
    qf = q.astype(F32) * (HEAD_DIM**-0.5)
    k_head = jnp.where(inside, kf, jnp.where(extra, key_bias, 0.0)).astype(BF16)
    q_head = jnp.where(inside, qf, jnp.where(extra, 1.0, 0.0)).astype(BF16)
    return inside, k_head, q_head, jnp.where(inside, qf, 0.0).astype(BF16)


def causal(scores, block):
    key = lax.broadcasted_iota(jnp.int32, (block, block), 0)
    query = lax.broadcasted_iota(jnp.int32, (block, block), 1)
    last = jnp.where(key <= query, scores[-block:], MASKED)
    if scores.shape[0] == block:
        return last
    return jnp.concatenate([scores[:-block], last], axis=0)


def attend_kernel(len_ref, q_ref, k_ref, v_ref, out_ref, lse_ref, kh_ref, qh_ref, vt_ref, ot_ref):
    seq = q_ref.shape[0]
    block = 256
    length = len_ref[0]
    vt_ref[...] = v_ref[...].astype(F32).T.astype(BF16)
    lse_ref[...] = jnp.zeros_like(lse_ref)
    for head in range(2):
        _, k_head, q_head, _ = head_parts(head, length, q_ref[...], k_ref[...])
        kh_ref[...] = k_head
        qh_ref[...] = q_head
        for qb in range(seq // block):
            ext = (qb + 1) * block
            cols = slice(qb * block, ext)
            scores = causal(dot_nt(kh_ref[:ext, :], qh_ref[cols, :]), block)
            top = jnp.max(scores, axis=0, keepdims=True)
            probs = jnp.exp(scores - top)
            total = jnp.sum(probs, axis=0, keepdims=True)
            part = dot_nn(vt_ref[head * HEAD_DIM : (head + 1) * HEAD_DIM, :ext], probs.astype(BF16))
            ot_ref[head * HEAD_DIM : (head + 1) * HEAD_DIM, cols] = part * (1.0 / total)
            lse_ref[0, head : head + 1, cols] = top + jnp.log(total)
    out_ref[...] = ot_ref[...].T.astype(BF16)


def attend_call(length, qkv, first, count):
    seq = qkv.shape[0]
    pairs = qkv.shape[1] // 3 // LANES
    width = count * LANES
    return pl.pallas_call(
        attend_kernel,
        grid=(count,),
        in_specs=[smem()]
        + [pl.BlockSpec((seq, LANES), lambda p, part=part: (0, part * pairs + first + p)) for part in range(3)],
        out_specs=[
            pl.BlockSpec((seq, LANES), lambda p: (0, p)),
            pl.BlockSpec((1, 8, seq), lambda p: (p, 0, 0)),
        ],
        out_shape=[
            jax.ShapeDtypeStruct((seq, width), BF16),
            jax.ShapeDtypeStruct((count, 8, seq), F32),
        ],
        scratch_shapes=[
            pltpu.VMEM((seq, LANES), BF16),
            pltpu.VMEM((seq, LANES), BF16),
            pltpu.VMEM((LANES, seq), BF16),
            pltpu.VMEM((LANES, seq), F32),
        ],
        compiler_params=params(),
        cost_estimate=cost(12),
        name="attend",
    )(length, qkv, qkv, qkv)


def attend_back_kernel(
    len_ref,
    q_ref,
    k_ref,
    v_ref,
    do_ref,
    o_ref,
    lse_ref,
    normed_ref,
    at_ref,
    dqkv_ref,
    keep_ref,
    send_ref,
    nt_ref,
    kt_ref,
    kh_ref,
    qh_ref,
    qm_ref,
    vh_ref,
    dh_ref,
    dk_ref,
    dv_ref,
    dqt_ref,
    pt_ref,
    join_ref,
):
    seq = q_ref.shape[0]
    block = 256
    length = len_ref[0]

    @pl.when(pl.program_id(0) == 0)
    def _():
        nt_ref[...] = normed_ref[...].astype(F32).T.astype(BF16)

    kt_ref[...] = k_ref[...].astype(F32).T.astype(BF16)
    pt_ref[...] = (do_ref[...].astype(F32) * o_ref[...].astype(F32)).T
    dk_ref[...] = jnp.zeros_like(dk_ref)
    dv_ref[...] = jnp.zeros_like(dv_ref)
    for head in range(2):
        rows = slice(head * HEAD_DIM, (head + 1) * HEAD_DIM)
        inside, k_head, q_head, q_masked = head_parts(head, length, q_ref[...], k_ref[...])
        kh_ref[...] = k_head
        qh_ref[...] = q_head
        qm_ref[...] = q_masked
        vh_ref[...] = jnp.where(inside, v_ref[...].astype(F32), 0.0).astype(BF16)
        dh_ref[...] = jnp.where(inside, do_ref[...].astype(F32), 0.0).astype(BF16)
        for qb in range(seq // block):
            ext = (qb + 1) * block
            cols = slice(qb * block, ext)
            delta = jnp.sum(pt_ref[rows, cols], axis=0, keepdims=True)
            scores = causal(dot_nt(kh_ref[:ext, :], qh_ref[cols, :]), block)
            probs = jnp.exp(scores - lse_ref[0, head : head + 1, cols])
            dprobs = dot_nt(vh_ref[:ext, :], dh_ref[cols, :])
            dscores = (probs * (dprobs - delta)).astype(BF16)
            dv_ref[:ext, :] += dot_nn(probs.astype(BF16), dh_ref[cols, :])
            dk_ref[:ext, :] += dot_nn(dscores, qm_ref[cols, :])
            dqt_ref[rows, cols] = dot_nn(kt_ref[rows, :ext], dscores)
    dq = (dqt_ref[...].T * (HEAD_DIM**-0.5)).astype(BF16)
    dk = dk_ref[...].astype(BF16)
    dv = dv_ref[...].astype(BF16)
    dqkv_ref[0] = dq
    dqkv_ref[1] = dk
    dqkv_ref[2] = dv
    joined = dot_nn(nt_ref[...], jnp.concatenate([dq, dk, dv], axis=1))
    join_ref[...] = joined.reshape(join_ref.shape)
    for chip in range(4):
        for far in range(4):
            for core, ref in enumerate((keep_ref, send_ref)):
                piece = join_ref[block_at(at_ref, chip, core, far)].astype(BF16)
                for part in range(3):
                    ref[chip, far, part] = piece[:, part * LANES : (part + 1) * LANES]


def attend_back_call(length, qkv, dmixed, mixed, lse, normed, at, first, count):
    seq, width = normed.shape
    pairs = width // LANES
    tall = width // BLOCKS
    part_width = count * LANES
    col = lambda p: (0, p)
    return pl.pallas_call(
        attend_back_kernel,
        grid=(count,),
        in_specs=[smem()]
        + [pl.BlockSpec((seq, LANES), lambda p, part=part: (0, part * pairs + first + p)) for part in range(3)]
        + [
            pl.BlockSpec((seq, LANES), lambda p: (0, first + p)),
            pl.BlockSpec((seq, LANES), col),
            pl.BlockSpec((1, 8, seq), lambda p: (p, 0, 0)),
            full((seq, width)),
            smem(),
        ],
        out_specs=[pl.BlockSpec((3, seq, LANES), lambda p: (0, 0, p))]
        + [pl.BlockSpec((4, 4, 3, tall, LANES), lambda p: (0, 0, 0, 0, p))] * 2,
        out_shape=[jax.ShapeDtypeStruct((3, seq, part_width), BF16)]
        + [jax.ShapeDtypeStruct((4, 4, 3, tall, part_width), BF16)] * 2,
        scratch_shapes=[
            pltpu.VMEM((width, seq), BF16),
            pltpu.VMEM((LANES, seq), BF16),
            pltpu.VMEM((seq, LANES), BF16),
            pltpu.VMEM((seq, LANES), BF16),
            pltpu.VMEM((seq, LANES), BF16),
            pltpu.VMEM((seq, LANES), BF16),
            pltpu.VMEM((seq, LANES), BF16),
            pltpu.VMEM((seq, LANES), F32),
            pltpu.VMEM((seq, LANES), F32),
            pltpu.VMEM((LANES, seq), F32),
            pltpu.VMEM((LANES, seq), F32),
            pltpu.VMEM((BLOCKS, tall, 3 * LANES), F32),
        ],
        compiler_params=params(),
        cost_estimate=cost(5),
        name="attend_back",
    )(length, qkv, qkv, qkv, dmixed, mixed, lse, normed, at)


def route_kernel(
    experts, group, capacity, len_ref, me_ref, route_ref, pair_ref, cot_ref, slot_ref, slot_t_ref, out_ref
):
    seq = route_ref.shape[1]
    half = experts // 2
    per = half // group
    local = 2 * per
    length = len_ref[0]
    me = me_ref[0]
    live = lax.broadcasted_iota(jnp.int32, (1, seq), 1) < length
    ids = lax.broadcasted_iota(jnp.int32, (experts, seq), 0)
    upper = (
        lax.broadcasted_iota(jnp.int32, (seq, seq), 0) < lax.broadcasted_iota(jnp.int32, (seq, seq), 1)
    )
    upper = jnp.where(upper, 1.0, 0.0).astype(BF16)
    before = jnp.zeros((experts, 1), F32)
    slots = []
    for choice in range(2):
        named = route_ref[choice : choice + 1, :]
        hot = jnp.where((ids == named) & live, 1.0, 0.0)
        earlier = dot_nn(hot.astype(BF16), upper) + before
        rank = jnp.sum(hot * earlier, axis=0, keepdims=True).astype(jnp.int32)
        before = before + jnp.sum(hot, axis=1, keepdims=True)
        is_new = named >= half
        within = jnp.where(is_new, named - half, named)
        owner = within // per
        place = jnp.where(is_new, per, 0) + within - owner * per
        shift = owner - me
        shift = jnp.where(shift < 0, shift + group, shift)
        slot = (shift * local + place) * capacity + rank
        slots.append(jnp.where(live & (rank < capacity), slot, -1))
    slot_ref[...] = jnp.concatenate(slots + [jnp.full((6, seq), -1, jnp.int32)], axis=0)
    slot_t_ref[...] = jnp.concatenate(
        [slot.astype(F32) for slot in slots] + [jnp.full((LANES - 2, seq), -1.0, F32)], axis=0
    ).T.astype(jnp.int32)
    total = experts * capacity
    place = lax.broadcasted_iota(jnp.int32, (total, seq), 0)
    select = jnp.where((place == slots[0]) | (place == slots[1]), 1.0, 0.0).astype(BF16)
    rows = dot_nn(select, cot_ref[...]).astype(BF16)
    both = (pair_ref[:, 0:1] + pair_ref[:, 1:2]).astype(F32)
    lane = lax.broadcasted_iota(jnp.int32, (seq, LANES), 1)
    tail = dot_nn(select, jnp.where(lane == 0, both, 0.0).astype(BF16)).astype(BF16)
    width = cot_ref.shape[1]
    size = local * capacity
    for shift in range(group):
        piece = slice(shift * size, (shift + 1) * size)
        place = lax.rem(me + shift, group)
        out_ref[place, :, :, :width] = rows[piece].reshape(local, capacity, width)
        out_ref[place, :, :, width:] = tail[piece].reshape(local, capacity, LANES)


def route_call(length, me, routes, cotangent, experts, group, capacity):
    seq, width = cotangent.shape
    local = experts // group
    wide = width + LANES
    return pl.pallas_call(
        functools.partial(route_kernel, experts, group, capacity),
        in_specs=[smem(), smem(), full((2, seq)), full((seq, 2)), full((seq, width))],
        out_specs=[full((8, seq)), full((seq, LANES)), full((group, local, capacity, wide))],
        out_shape=[
            jax.ShapeDtypeStruct((8, seq), jnp.int32),
            jax.ShapeDtypeStruct((seq, LANES), jnp.int32),
            jax.ShapeDtypeStruct((group, local, capacity, wide), BF16),
        ],
        grid=(1,),
        compiler_params=params(),
        cost_estimate=cost(5.7),
        name="route",
    )(length, me, routes.T, routes, cotangent)


def project_kernel(
    group, low_ref, high_ref, tok_ref, w_ref, scale_ref, slot_ref, res_ref, *refs
):
    out_refs = refs[:group]
    normed_ref = refs[group]
    step = pl.program_id(0)
    block = tok_ref.shape[0]
    mixed = jnp.concatenate([low_ref[...], high_ref[...]], axis=1)
    residual = tok_ref[...].astype(F32) + dot_nn(mixed, w_ref[...])
    res_ref[...] = residual
    xhat, _ = norm_parts(residual)
    normed = (xhat * scale_ref[2:3, :] + scale_ref[3:4, :]).astype(BF16)
    normed_ref[pl.ds(pl.multiple_of(step * block, block), block), :] = normed

    @pl.when(step == pl.num_programs(0) - 1)
    def _():
        local, capacity, width = out_refs[0].shape
        size = local * capacity
        seq = normed_ref.shape[0]
        place = lax.broadcasted_iota(jnp.int32, (size * group, seq), 0)
        select = (place == slot_ref[0:1, :]) | (place == slot_ref[1:2, :])
        select = jnp.where(select, 1.0, 0.0).astype(BF16)
        rows = dot_nn(select, normed_ref[...]).astype(BF16)
        for shift in range(group):
            out_refs[shift][...] = rows[shift * size : (shift + 1) * size].reshape(local, capacity, width)


def project_call(mixed, tokens, weight, scales, slots, group, local, capacity):
    seq, width = tokens.shape
    block = 256
    rows = pl.BlockSpec((block, width), lambda i: (i, 0))
    half = pl.BlockSpec((block, width // 2), lambda i: (i, 0))
    return pl.pallas_call(
        functools.partial(project_kernel, group),
        grid=(seq // block,),
        in_specs=[half, half, rows, full((width, width)), full((4, width)), full((8, seq))],
        out_specs=[rows] + [full((local, capacity, width))] * group,
        out_shape=[jax.ShapeDtypeStruct((seq, width), F32)]
        + [jax.ShapeDtypeStruct((local, capacity, width), BF16)] * group,
        scratch_shapes=[pltpu.VMEM((seq, width), BF16)],
        compiler_params=params(),
        cost_estimate=cost(8.8),
        name="project_dispatch",
    )(*mixed, tokens, weight, scales, slots)


def expert_kernel(trained, group, held, own_ref, *refs):
    x_refs = refs[:group]
    g_ref, wr_ref, wrt_ref = refs[group : group + 3]
    in_refs = refs[group + 3 : group + 13]
    out_w_refs = refs[group + 13 : group + 23]
    rest = refs[group + 23 + held :]
    out_ref = rest[0]
    back_refs = rest[1 : group + 1]
    router_ref = rest[group + 1]
    rest = rest[group + 2 :]
    if trained:
        grad_refs = rest[:4]
        rest = rest[4:]
    x_ref, dexp_ref, gate_ref, acc_ref, back_ref, xt_ref, win_ref, wout_ref, din_ref, dout_ref = rest
    step = pl.program_id(0)
    capacity, width = back_refs[0].shape
    own = own_ref[0]

    def source(shift):
        return lax.rem(own_ref[3] - shift + group, group)

    def other_of(tail):
        return tail[:, 0:1].astype(F32).astype(jnp.int32) - own

    @pl.when(step == 0)
    def _():
        for shift in range(group):
            span = slice(shift * capacity, (shift + 1) * capacity)
            rows = x_refs[shift][0]
            x_ref[span, :] = rows
            logits = dot_nn(rows, wr_ref[...])
            lane = lax.broadcasted_iota(jnp.int32, logits.shape, 1)
            other = other_of(g_ref[source(shift), 0, :, width:])
            mine = jnp.sum(jnp.where(lane == own, logits, 0.0), axis=1, keepdims=True)
            theirs = jnp.sum(jnp.where(lane == other, logits, 0.0), axis=1, keepdims=True)
            top = jnp.maximum(mine, theirs)
            up = jnp.exp(mine - top)
            gate = up / (up + jnp.exp(theirs - top))
            gate_ref[span, :] = jnp.broadcast_to(gate, (capacity, LANES))
            dexp_ref[span, :] = (gate * g_ref[source(shift), 0, :, :width].astype(F32)).astype(BF16)
        acc_ref[...] = jnp.zeros_like(acc_ref)
        back_ref[...] = jnp.zeros_like(back_ref)
        xt_ref[...] = x_ref[...].astype(F32).T.astype(BF16)

    for which in range(2):
        core = own_ref[1] ^ which
        for index, (chip, lower) in enumerate(PLACES):
            piece = in_refs[5 * which + index]
            tall = piece.shape[1]
            at = ((own_ref[2] ^ chip) * 2 + core) * in_refs[0].shape[1] + lower * tall
            win_ref[pl.ds(pl.multiple_of(at, 16), tall), :] = piece[0]

            @pl.when(step == chip)
            def _(piece=out_w_refs[5 * which + index], lower=lower, core=core):
                tall = piece.shape[1]
                at = core * out_w_refs[0].shape[1] + lower * tall
                wout_ref[pl.ds(pl.multiple_of(at, 16), tall), :] = piece[0]

    win = win_ref[...]
    wout = wout_ref[...]
    pre = dot_nn(x_ref[...], win)
    square = pre * pre
    tanh = jnp.tanh(0.7978845608028654 * (pre + 0.044715 * pre * square))
    half = 0.5 * (1.0 + tanh)
    hid = (pre * half).astype(BF16)
    slope = half + (0.5 * pre) * (1.0 - tanh * tanh) * (0.7978845608028654 + 0.1070322243 * square)
    acc_ref[...] += dot_nn(hid, wout)
    dpre = (dot_nt(dexp_ref[...], wout) * slope).astype(BF16)
    back_ref[...] += dot_nt(dpre, win)
    if trained:
        dout_ref[...] = dot_tn(hid, dexp_ref[...]).astype(BF16).reshape(dout_ref.shape)
        din_ref[...] = dot_nn(xt_ref[...], dpre).astype(BF16).reshape(din_ref.shape)
        for which in range(2):
            core = own_ref[1] ^ which
            for chip in range(4):
                grad_refs[which][chip] = din_ref[(own_ref[2] ^ chip) * 2 + core]
            grad_refs[2 + which][0] = dout_ref[core]

    @pl.when(step == pl.num_programs(0) - 1)
    def _():
        router = jnp.zeros((width, LANES), F32)
        for shift in range(group):
            span = slice(shift * capacity, (shift + 1) * capacity)
            gate = gate_ref[span, 0:1]
            result = acc_ref[span, :]
            out_ref[source(shift), 0] = (gate * result).astype(BF16)
            dot = jnp.sum(result * g_ref[source(shift), 0, :, :width].astype(F32), axis=1, keepdims=True)
            coef = gate * (1.0 - gate) * dot
            lane = lax.broadcasted_iota(jnp.int32, (capacity, LANES), 1)
            other = other_of(g_ref[source(shift), 0, :, width:])
            sign = jnp.where(lane == own, 1.0, 0.0) - jnp.where(lane == other, 1.0, 0.0)
            dlogits = (coef * sign).astype(BF16)
            back_refs[shift][...] = (back_ref[span, :] + dot_nn(dlogits, wrt_ref[...])).astype(BF16)
            router = router + dot_nn(xt_ref[:, span], dlogits)
        router_ref[...] = router


def expert_call(trained, place, local, own, rows, grads, router, router_t, held, pick, w_in, w_out):
    group = len(rows)
    _, capacity, width = rows[0].shape
    inner = w_in[0].shape[2]
    chunk = inner // 4
    block = lambda f, own: own[2] ^ f
    wide = grads.shape[3]
    many = group * capacity
    shard, deep = width // 8, inner // 8
    out_specs = [pl.BlockSpec((group, 1, capacity, width), lambda f, own: (0, place, 0, 0))]
    out_specs += [full((capacity, width))] * group + [full((width, LANES))]
    out_shape = [jax.ShapeDtypeStruct((group, local, capacity, width), BF16)]
    out_shape += [jax.ShapeDtypeStruct((capacity, width), BF16)] * group
    out_shape += [jax.ShapeDtypeStruct((width, LANES), F32)]
    if trained:
        out_specs += [pl.BlockSpec((4, shard, chunk), lambda f, own: (0, 0, block(f, own)))] * 2
        out_specs += [pl.BlockSpec((1, deep, width), lambda f, own: (f, 0, 0))] * 2
        out_shape += [jax.ShapeDtypeStruct((4, shard, inner), BF16)] * 2
        out_shape += [jax.ShapeDtypeStruct((4, deep, width), BF16)] * 2
    return pl.pallas_call(
        functools.partial(expert_kernel, trained, group, len(held)),
        grid_spec=pltpu.PrefetchScalarGridSpec(
            num_scalar_prefetch=1,
            grid=(4,),
            in_specs=[pl.BlockSpec((1, capacity, width), lambda f, own: (place, 0, 0))] * group
            + [pl.BlockSpec((group, 1, capacity, wide), lambda f, own: (0, place, 0, 0))]
            + [full((width, LANES)), full((LANES, width))]
            + [pl.BlockSpec((1, w.shape[1], chunk), lambda f, own: (pick, 0, block(f, own))) for w in w_in]
            + [pl.BlockSpec((1, w.shape[1], width), lambda f, own: (pick, 0, 0)) for w in w_out]
            + [pl.BlockSpec(memory_space=pl.ANY)] * len(held),
            out_specs=out_specs,
            scratch_shapes=[
            pltpu.VMEM((many, width), BF16),
            pltpu.VMEM((many, width), BF16),
            pltpu.VMEM((many, LANES), F32),
            pltpu.VMEM((many, width), F32),
            pltpu.VMEM((many, width), F32),
            pltpu.VMEM((width, many), BF16),
            pltpu.VMEM((width, chunk), BF16),
            pltpu.VMEM((chunk, width), BF16),
            pltpu.VMEM((8, shard, chunk) if trained else (8, LANES), BF16),
            pltpu.VMEM((2, deep, width) if trained else (8, LANES), BF16),
            ],
        ),
        out_shape=out_shape,
        input_output_aliases={group + 24: 0} if held else {},
        compiler_params=params(),
        cost_estimate=cost(23 if trained else 17),
        name="experts_new" if trained else "experts_old",
    )(own, *rows, grads, router, router_t, *w_in, *w_out, *held)


def pick_matrix(slot_ref, total):
    place = lax.broadcasted_iota(jnp.int32, (slot_ref.shape[0], total), 1)
    hit = (place == slot_ref[:, 0:1]) | (place == slot_ref[:, 1:2])
    return jnp.where(hit, 1.0, 0.0).astype(BF16)


def pick_rows(slot_ref, part_refs):
    width = part_refs[0].shape[-1]
    held = jnp.concatenate([part[...].reshape(-1, width) for part in part_refs], axis=0)
    return dot_nn(pick_matrix(slot_ref, held.shape[0]), held)


def combine_kernel(me_ref, slot_ref, res_ref, part_ref, out_ref):
    group, _, _, width = part_ref.shape
    parts = [part_ref[lax.rem(me_ref[0] + shift, group)].reshape(-1, width) for shift in range(group)]
    held = jnp.concatenate(parts, axis=0)
    out_ref[...] = res_ref[...] + dot_nn(pick_matrix(slot_ref, held.shape[0]), held)


def combine_call(me, slots, residual, parts):
    seq, width = residual.shape
    block = 256
    rows = pl.BlockSpec((block, width), lambda i: (i, 0))
    return pl.pallas_call(
        combine_kernel,
        grid=(seq // block,),
        in_specs=[smem(), pl.BlockSpec((block, LANES), lambda i: (i, 0)), rows, full(parts.shape)],
        out_specs=rows,
        out_shape=jax.ShapeDtypeStruct((seq, width), F32),
        compiler_params=params(),
        cost_estimate=cost(6.2),
        name="combine",
    )(me, slots, residual, parts)


def middle_kernel(count, slot_ref, res_ref, cot_ref, gain_ref, low_ref, high_ref, w_ref, at_ref, *refs):
    parts = refs[:count]
    dres_ref, dmix_ref, keep_ref, send_ref, sums_ref, acc_ref = refs[count:]
    step = pl.program_id(0)
    dnormed = pick_rows(slot_ref, parts)
    xhat, scale = norm_parts(res_ref[...])
    dres = cot_ref[...].astype(F32) + norm_back(dnormed, gain_ref[2:3, :], xhat, scale)
    dres_ref[...] = dres
    dattn = dres.astype(BF16)
    dmix_ref[...] = dot_nt(dattn, w_ref[...]).astype(BF16)

    @pl.when(step == 0)
    def _():
        sums_ref[...] = jnp.zeros_like(sums_ref)
        acc_ref[...] = jnp.zeros_like(acc_ref)

    mixed = jnp.concatenate([low_ref[...], high_ref[...]], axis=1)
    acc_ref[...] += dot_tn(mixed, dattn).reshape(acc_ref.shape)
    sums_ref[0:1, :] += jnp.sum(dnormed * xhat, axis=0, keepdims=True)
    sums_ref[1:2, :] += jnp.sum(dnormed, axis=0, keepdims=True)

    @pl.when(step == pl.num_programs(0) - 1)
    def _():
        for chip in range(4):
            for far in range(4):
                for core, ref in enumerate((keep_ref, send_ref)):
                    piece = acc_ref[block_at(at_ref, chip, core, far)].astype(BF16)
                    ref[chip, far, 0] = piece[:, : piece.shape[1] // 2]
                    ref[chip, far, 1] = piece[:, piece.shape[1] // 2 :]


def middle_call(slots, residual, cotangent, gain, mixed, weight, at, parts):
    seq, width = residual.shape
    tall = width // BLOCKS
    block = 256
    capacity = parts[0].shape[0]
    rows = pl.BlockSpec((block, width), lambda i: (i, 0))
    half = pl.BlockSpec((block, width // 2), lambda i: (i, 0))
    return pl.pallas_call(
        functools.partial(middle_kernel, len(parts)),
        grid=(seq // block,),
        in_specs=[
            pl.BlockSpec((block, LANES), lambda i: (i, 0)),
            rows,
            rows,
            full((4, width)),
            half,
            half,
            full((width, width)),
            smem(),
        ]
        + [full((capacity, width))] * len(parts),
        out_specs=[rows, rows] + [full((4, 4, 2, tall, width // 2))] * 2 + [full((8, width))],
        out_shape=[
            jax.ShapeDtypeStruct((seq, width), F32),
            jax.ShapeDtypeStruct((seq, width), BF16),
            jax.ShapeDtypeStruct((4, 4, 2, tall, width // 2), BF16),
            jax.ShapeDtypeStruct((4, 4, 2, tall, width // 2), BF16),
            jax.ShapeDtypeStruct((8, width), F32),
        ],
        scratch_shapes=[pltpu.VMEM((BLOCKS, tall, width), F32)],
        compiler_params=params(),
        cost_estimate=cost(13),
        name="middle_back",
    )(slots, residual, cotangent, gain, *mixed, weight, at, *parts)


def last_kernel(low_ref, high_ref, tok_ref, dres_ref, gain_ref, w_ref, out_ref, sums_ref):
    width = tok_ref.shape[1]
    grads = [ref[part] for part in range(3) for ref in (low_ref, high_ref)]
    dnormed = dot_nt(jnp.concatenate(grads, axis=1), w_ref[...])
    xhat, scale = norm_parts(tok_ref[...].astype(F32))
    out_ref[...] = dres_ref[...] + norm_back(dnormed, gain_ref[0:1, :], xhat, scale)

    @pl.when(pl.program_id(0) == 0)
    def _():
        sums_ref[...] = jnp.zeros_like(sums_ref)

    sums_ref[0:1, :] += jnp.sum(dnormed * xhat, axis=0, keepdims=True)
    sums_ref[1:2, :] += jnp.sum(dnormed, axis=0, keepdims=True)


def last_call(dqkv, tokens, dres, gain, weight):
    seq, width = tokens.shape
    block = 256
    rows = pl.BlockSpec((block, width), lambda i: (i, 0))
    return pl.pallas_call(
        last_kernel,
        grid=(seq // block,),
        in_specs=[
            pl.BlockSpec((3, block, width // 2), lambda i: (0, i, 0)),
            pl.BlockSpec((3, block, width // 2), lambda i: (0, i, 0)),
            rows,
            rows,
            full((4, width)),
            full((width, 3 * width)),
        ],
        out_specs=[rows, full((8, width))],
        out_shape=[
            jax.ShapeDtypeStruct((seq, width), F32),
            jax.ShapeDtypeStruct((8, width), F32),
        ],
        compiler_params=params(),
        cost_estimate=cost(5),
        name="last_back",
    )(*dqkv, tokens, dres, gain, weight)


def unpack_kernel(outs, parts, at_ref, *refs):
    pieces = refs[:8]
    out_refs = refs[-outs:]
    tall = pieces[0].shape[1]
    part = pl.program_id(0)

    def put(out_ref):
        for index, piece in enumerate(pieces):
            for far in range(4):
                place = (at_ref[0] ^ index) * 4 + (at_ref[1] ^ FAR[far])
                rows = pl.ds(pl.multiple_of(place * tall, 8), tall)
                out_ref[rows, :] = piece[far * parts + part].astype(F32)

    @pl.when(part < 3)
    def _():
        put(out_refs[0])

    if outs > 1:

        @pl.when(part >= 3)
        def _():
            put(out_refs[1])


def unpack_call(at, pieces, half, base=None):
    blocks, tall, part_width = pieces[0].shape
    parts = blocks // 4
    width = tall * BLOCKS
    out_specs = [pl.BlockSpec((width, part_width), lambda p: (0, 2 * jnp.minimum(p, 2) + half))]
    out_shape = [jax.ShapeDtypeStruct((width, 6 * part_width), F32)]
    if parts > 3:
        out_specs.append(pl.BlockSpec((width, part_width), lambda p: (0, jnp.maximum(p - 3, 0))))
        out_shape.append(jax.ShapeDtypeStruct((width, width), F32))
    held = [] if base is None else [base]
    return pl.pallas_call(
        functools.partial(unpack_kernel, len(out_shape), parts),
        grid=(parts,),
        in_specs=[smem()]
        + [full((blocks, tall, part_width))] * 8
        + [pl.BlockSpec(memory_space=pl.ANY)] * len(held),
        out_specs=out_specs,
        out_shape=out_shape,
        input_output_aliases={9: 0} if held else {},
        compiler_params=params(),
        cost_estimate=cost(4),
        name="unpack",
    )(at, *pieces, *held)


def swap(block, bits):
    size = lax.axis_size("batch")
    return lax.ppermute(block, "batch", [(i, i ^ bits) for i in range(size)])


def across(block, bits):
    size = lax.axis_size("expert")
    return lax.ppermute(block, "expert", [(i, i ^ bits) for i in range(size)])


def added(*blocks):
    total = blocks[0].astype(F32)
    for block in blocks[1:]:
        total = total + block.astype(F32)
    return total


def gather_shards(shard):
    whole = lax.all_gather(shard, "batch", axis=1, tiled=True)
    some, rows, width = whole.shape
    parts = whole.reshape(some, 4, 2, rows // 8, width)
    half = rows // 16
    return [
        parts[:, chip, core, lower * half : (lower + 1) * half] if chip == 3 else parts[:, chip, core]
        for core in range(2)
        for chip, lower in PLACES
    ]


def near(shard):
    return [swap(shard, 2), swap(shard, 4)]


def relay(full_x, full_y):
    half = full_x.shape[1] // 2
    return [swap(full_y[:, :half], 2), swap(full_x[:, half:], 4)]


def tie(*values):
    return list(lax.optimization_barrier(values))


def sum_all(keep, send):
    keep, send = lax.psum((keep, send), ("expert", "batch"))
    pieces = []
    for chip in range(4):
        for half in (keep, send):
            parts = jnp.concatenate([part[chip] for part in half], axis=1)
            pieces.append(jnp.concatenate([parts[far] for far in range(4)]))
    return pieces


def sum_core(keep, send):
    got = [swap(part, 1) for part in send]
    halves = []
    for chip in range(4):
        parts = [added(mine[chip], other[chip]) for mine, other in zip(keep, got)]
        halves.append(jnp.concatenate(parts, axis=1).astype(BF16))
    return halves


def to_chips(halves):
    return [halves[0]] + [swap(halves[chip], 2 * chip) for chip in (1, 2, 3)]


def total(parts):
    return added(*parts).astype(BF16)


def give(block, bits):
    rows = block.shape[0] // 2
    return [block[:rows], across(block[rows:], bits)]


def spread_chips(column):
    return [column] + [swap(column, 2 * chip) for chip in (1, 2, 3)]


def spread_cores(blocks):
    return [piece for block in blocks for piece in (block, swap(block, 1))]


def scatter_core(keep, send):
    return [added(mine, other).astype(BF16) for mine, other in zip(keep, swap(send, 1))]


def natural(keep, send):
    both = jnp.stack([keep, send], axis=1)
    return both.reshape(-1, both.shape[-1])


def body(
    tokens,
    lengths,
    routes,
    ln1_gain,
    ln1_bias,
    ln2_gain,
    ln2_bias,
    w_qkv,
    w_proj,
    w_router,
    old_in,
    old_out,
    new_in,
    new_out,
    cotangent,
):
    group = lax.axis_size("expert")
    me = lax.axis_index("expert")
    token_rows = tokens[0]
    cot_rows = cotangent[0]
    seq, width = token_rows.shape
    experts = w_router.shape[1]
    local = experts // group
    per = old_in.shape[0]
    capacity = max(4, seq // experts)
    scales = jnp.stack([ln1_gain, ln1_bias, ln2_gain, ln2_bias])

    def go(block, shift):
        if shift == 0:
            return block
        return lax.ppermute(block, "expert", [(i, (i + shift) % group) for i in range(group)])

    def trade(blocks):
        return lax.all_to_all(blocks, "expert", 0, 0, tiled=True)

    def come(block, shift):
        if shift == 0:
            return block
        return lax.ppermute(block, "expert", [(i, (i - shift) % group) for i in range(group)])

    fast = group == 4 and lax.axis_size("batch") == 8 and per == 1 and experts == 8
    at = jnp.stack([lax.axis_index("batch"), me]).astype(jnp.int32) if fast else jnp.zeros((2,), jnp.int32)
    me_one = jnp.full((1,), me, jnp.int32)
    pairs = width // LANES
    first_half = pairs // 2
    halves = ((0, first_half), (first_half, pairs - first_half))
    if fast:
        pair_in = jnp.stack([new_in[0], old_in[0]])
        pair_out = jnp.stack([new_out[0], old_out[0]])
        in_full = near(pair_in)
    slots, slots_t, sent_grads = route_call(
        lengths, me_one, routes[0], cot_rows, experts, group, capacity
    )
    grads = trade(sent_grads)
    token_rows, slots = tie(token_rows, slots)
    normed1, qkv = qkv_call(token_rows, scales, w_qkv)
    mixed_low, lse_low = attend_call(lengths, qkv, *halves[0])
    if fast:
        qkv, mixed_low, pair_in, pair_out, in_full[0], in_full[1] = tie(
            qkv, mixed_low, pair_in, pair_out, *in_full
        )
        in_half = relay(*in_full)
        in_other = [swap(part, 1) for part in (pair_in, *in_full)]
    mixed_high, lse_high = attend_call(lengths, qkv, *halves[1])
    if fast:
        mixed_high, pair_out, *tied = tie(mixed_high, pair_out, *in_half, *in_other)
        in_half, in_other = tied[:2], tied[2:]
        out_full = near(pair_out)
    mixed = (mixed_low, mixed_high)
    residual, *sent_rows = project_call(
        mixed, token_rows, w_proj, scales, slots, group, local, capacity
    )
    rows = [go(sent_rows[shift], shift) for shift in range(group)]
    if fast:
        rows[1], rows[3], pair_out, *tied = tie(rows[1], rows[3], pair_out, *out_full, *in_half)
        out_full, in_half = tied[:2], tied[2:]
        out_half = relay(*out_full)
        in_parts = [pair_in, *in_full, *in_half]
        out_parts = [pair_out, *out_full, *out_half]
        in_parts += in_other + [swap(part, 1) for part in in_half]
        out_parts += [swap(part, 1) for part in out_parts]
        weights = {True: (0, in_parts, out_parts), False: (1, in_parts, out_parts)}
    else:
        weights = {
            trained: (0, gather_shards(w_in), gather_shards(w_out))
            for trained, w_in, w_out in ((True, new_in, new_out), (False, old_in, old_out))
        }
    core, chip = (at[0] & 1, at[0] >> 1) if fast else (0, 0)
    router = jnp.pad(w_router, ((0, 0), (0, LANES - experts)))
    router_t = jnp.pad(w_router.T, ((0, LANES - experts), (0, 0)))
    outs, backs, router_sum = [], {}, 0.0
    half = experts // 2
    for trained in (True, False):
        for index in range(per):
            place = index + (per if trained else 0)
            own = jnp.stack([me * per + index + (half if trained else 0), core, chip, me]).astype(jnp.int32)
            got = expert_call(
                trained,
                place,
                local,
                own,
                rows,
                grads,
                router,
                router_t,
                outs,
                weights[trained][0] + index,
                *weights[trained][1:],
            )
            outs = [got[0]]
            sent = got[1 : group + 1]
            if fast and not trained:
                tied = tie(*sent, *backs[1])
                sent, backs[1] = tied[:group], tied[group:]
            backs[place] = [come(sent[shift], shift) for shift in range(group)]
            router_sum = router_sum + got[group + 1]
            if trained:
                in_keep, in_send, out_keep, out_send = got[group + 2 :]
    returned = [backs[p][shift] for shift in range(group) for p in range(local)]
    if fast:
        in_rs = scatter_core(in_keep, in_send)
        out_rs = scatter_core(out_keep, out_send)
        in_got = [swap(in_rs[chip], 2 * chip) for chip in (1, 2)]
        tied = tie(*returned, *in_got, *in_rs, *out_rs)
        returned, in_got, in_rs, out_rs = tied[:-10], tied[-10:-8], tied[-8:-4], tied[-4:]
        in_got.append(swap(in_rs[3], 6))
        out_got = [swap(out_rs[chip], 2 * chip) for chip in (1, 2)]
    dres, dmixed, proj_keep, proj_send, sums2 = middle_call(
        slots_t, residual, cot_rows, scales, mixed, w_proj, at, returned
    )
    if fast:
        dmixed, outs[0] = tie(dmixed, outs[0])
    else:
        natural_in = natural(in_keep, in_send)
        natural_out = natural(out_keep, out_send)
    back_outs = trade(outs[0])
    dq_low, keep_low, send_low = attend_back_call(
        lengths, qkv, dmixed, mixed_low, lse_low, normed1, at, *halves[0]
    )
    if fast:
        halves_low = sum_core((keep_low, proj_keep), (send_low, proj_send))
        dmixed, dq_low, in_got[2], out_got[0], out_got[1], out_rs[3] = tie(
            dmixed, dq_low, in_got[2], *out_got, out_rs[3]
        )
        out_got.append(swap(out_rs[3], 6))
    dq_high, keep_high, send_high = attend_back_call(
        lengths, qkv, dmixed, mixed_high, lse_high, normed1, at, *halves[1]
    )
    if fast:
        dq_high, keep_high, back_outs, out_got[2], *halves_low = tie(
            dq_high, keep_high, back_outs, out_got[2], *halves_low
        )
        low = to_chips(halves_low)
        halves_high = sum_core((keep_high,), (send_high,))
    input_grad, sums1 = last_call((dq_low, dq_high), token_rows, dres, scales, w_qkv)
    if fast:
        sums1, *halves_high = tie(sums1, *halves_high)
        high = to_chips(halves_high)
        small = jnp.concatenate([router_sum.T[:experts], sums1[:2], sums2[:2]], axis=0)
        low = give(total(low), 1)
        tied = tie(*low, *high)
        low = give(total(tied[:2]), 2)
        high = give(total(tied[2:]), 1)
        tied = tie(*low, *high)
        own_low = total(tied[:2])[0]
        low = [own_low, across(own_low, 2)]
        high = give(total(tied[2:]), 2)
        tied = tie(*low, *high)
        low = jnp.stack(tied[:2])
        low = [low, across(low, 1)]
        own_high = total(tied[2:])[0]
        mine = small.astype(BF16).reshape(1, *own_high.shape[1:])
        high = [jnp.concatenate([own_high, mine])]
        high.append(across(high[0], 2))
        tied = tie(*low, *high)
        column_low = jnp.concatenate(tied[:2]).reshape(-1, *own_low.shape[1:])
        chips_low = spread_chips(column_low)
        parts = own_high.shape[0]
        mine = total([block[parts:] for block in tied[2:]])
        high = jnp.concatenate([block[:parts] for block in tied[2:]] + [mine])
        high = [high, across(high, 1)]
        mine = total([block[2 * parts :] for block in high])
        chips_high = spread_chips(jnp.concatenate([block[: 2 * parts] for block in high] + [mine]))
        pieces_low = spread_cores(chips_low)
        qkv_grad, proj_grad = unpack_call(at, pieces_low, 0)
        qkv_grad, *chips_high = tie(qkv_grad, *chips_high)
        pieces_high = spread_cores(chips_high)
        small = added(*[piece[4 * parts] for piece in pieces_high]).reshape(small.shape)
        new_in_grad = added(in_rs[0], *in_got)
        new_out_grad = added(out_rs[0], *out_got)
    else:
        pieces_low = sum_all((keep_low, proj_keep), (send_low, proj_send))
        pieces_high = sum_all((keep_high,), (send_high,))
        small = jnp.concatenate([router_sum.T[:experts], sums1[:2], sums2[:2]], axis=0)
        small = jnp.sum(lax.all_gather(small, ("expert", "batch"), axis=0), axis=0)
        new_in_grad = lax.psum_scatter(natural_in, "batch", scatter_dimension=0, tiled=True)
        new_out_grad = lax.psum_scatter(natural_out, "batch", scatter_dimension=0, tiled=True)
    output = combine_call(me_one, slots_t, residual, back_outs)
    if not fast:
        qkv_grad, proj_grad = unpack_call(at, pieces_low, 0)
    (qkv_grad,) = unpack_call(at, pieces_high, 1, qkv_grad)
    return (
        output[None],
        input_grad[None],
        small[experts],
        small[experts + 1],
        small[experts + 2],
        small[experts + 3],
        qkv_grad,
        proj_grad,
        small[:experts].T,
        new_in_grad.astype(F32)[None],
        new_out_grad.astype(F32)[None],
    )


def solution(mesh):
    rows = P(("expert", "batch"), None, None)
    weights = P("expert", "batch", None)
    placed = (
        (rows, P(("expert", "batch")), rows)
        + (P(),) * 7
        + (weights,) * 4
        + (rows,)
    )
    return jax.shard_map(
        body,
        mesh=mesh,
        in_specs=placed,
        out_specs=(rows, rows) + (P(),) * 7 + (weights, weights),
        check_vma=False,
    )
```

```python
import functools

import jax
import jax.numpy as jnp
from jax import lax
from jax.experimental import pallas as pl
from jax.experimental.pallas import tpu as pltpu
from jax.sharding import PartitionSpec as P

HEAD_DIM = 64
LANES = 128
EPS = 1e-05
MASKED = -1e30
F32 = jnp.float32
BF16 = jnp.bfloat16
VMEM_LIMIT = 56 * 1024 * 1024
BLOCKS = 32
FAR = (0, 2, 1, 3)
PLACES = ((0, 0), (1, 0), (2, 0), (3, 0), (3, 1))


def params():
    return pltpu.CompilerParams(vmem_limit_bytes=VMEM_LIMIT)


def dot_nt(left, right):
    return lax.dot_general(left, right, (((1,), (1,)), ((), ())), preferred_element_type=F32)


def dot_tn(left, right):
    return lax.dot_general(left, right, (((0,), (0,)), ((), ())), preferred_element_type=F32)


def dot_nn(left, right):
    return jnp.dot(left, right, preferred_element_type=F32)


def norm_parts(rows):
    mean = jnp.mean(rows, axis=-1, keepdims=True)
    centred = rows - mean
    var = jnp.mean(centred * centred, axis=-1, keepdims=True)
    scale = lax.rsqrt(var + EPS)
    return centred * scale, scale


def norm_back(grad, gain, xhat, scale):
    a = grad * gain
    mean_a = jnp.mean(a, axis=-1, keepdims=True)
    mean_ax = jnp.mean(a * xhat, axis=-1, keepdims=True)
    return scale * (a - mean_a - xhat * mean_ax)


def full(shape):
    return pl.BlockSpec(shape, lambda *_: (0,) * len(shape))


def smem():
    return pl.BlockSpec(memory_space=pltpu.SMEM)


def cost(micros):
    return pl.CostEstimate(flops=int(micros * 1.1e9), transcendentals=0, bytes_accessed=int(micros * 3e6))


def block_at(at_ref, chip, core, far):
    return (at_ref[0] ^ (2 * chip + core)) * 4 + (at_ref[1] ^ FAR[far])


def qkv_kernel(tok_ref, scale_ref, w_ref, normed_ref, qkv_ref):
    xhat, _ = norm_parts(tok_ref[...].astype(F32))
    normed = (xhat * scale_ref[0:1, :] + scale_ref[1:2, :]).astype(BF16)
    normed_ref[...] = normed
    qkv_ref[...] = dot_nn(normed, w_ref[...]).astype(BF16)


def qkv_call(tokens, scales, weight):
    seq, width = tokens.shape
    block = 256
    cols = weight.shape[1]
    return pl.pallas_call(
        qkv_kernel,
        grid=(seq // block,),
        in_specs=[
            pl.BlockSpec((block, width), lambda i: (i, 0)),
            full((4, width)),
            full((width, cols)),
        ],
        out_specs=[
            pl.BlockSpec((block, width), lambda i: (i, 0)),
            pl.BlockSpec((block, cols), lambda i: (i, 0)),
        ],
        out_shape=[
            jax.ShapeDtypeStruct((seq, width), BF16),
            jax.ShapeDtypeStruct((seq, cols), BF16),
        ],
        compiler_params=params(),
        cost_estimate=cost(8.7),
        name="norm_qkv",
    )(tokens, scales, weight)


def head_parts(head, length, q, k):
    seq = q.shape[0]
    lane = lax.broadcasted_iota(jnp.int32, (seq, LANES), 1)
    row = lax.broadcasted_iota(jnp.int32, (seq, LANES), 0)
    inside = (lane // HEAD_DIM) == head
    extra = lane == (1 - head) * HEAD_DIM
    key_bias = jnp.where(row >= length, MASKED, 0.0)
    kf = k.astype(F32)
    qf = q.astype(F32) * (HEAD_DIM**-0.5)
    k_head = jnp.where(inside, kf, jnp.where(extra, key_bias, 0.0)).astype(BF16)
    q_head = jnp.where(inside, qf, jnp.where(extra, 1.0, 0.0)).astype(BF16)
    return inside, k_head, q_head, jnp.where(inside, qf, 0.0).astype(BF16)


def causal(scores, block):
    key = lax.broadcasted_iota(jnp.int32, (block, block), 0)
    query = lax.broadcasted_iota(jnp.int32, (block, block), 1)
    last = jnp.where(key <= query, scores[-block:], MASKED)
    if scores.shape[0] == block:
        return last
    return jnp.concatenate([scores[:-block], last], axis=0)


def attend_kernel(len_ref, q_ref, k_ref, v_ref, out_ref, lse_ref, kh_ref, qh_ref, vt_ref, ot_ref):
    seq = q_ref.shape[0]
    block = 256
    length = len_ref[0]
    vt_ref[...] = v_ref[...].astype(F32).T.astype(BF16)
    lse_ref[...] = jnp.zeros_like(lse_ref)
    for head in range(2):
        _, k_head, q_head, _ = head_parts(head, length, q_ref[...], k_ref[...])
        kh_ref[...] = k_head
        qh_ref[...] = q_head
        for qb in range(seq // block):
            ext = (qb + 1) * block
            cols = slice(qb * block, ext)
            scores = causal(dot_nt(kh_ref[:ext, :], qh_ref[cols, :]), block)
            top = jnp.max(scores, axis=0, keepdims=True)
            probs = jnp.exp(scores - top)
            total = jnp.sum(probs, axis=0, keepdims=True)
            part = dot_nn(vt_ref[head * HEAD_DIM : (head + 1) * HEAD_DIM, :ext], probs.astype(BF16))
            ot_ref[head * HEAD_DIM : (head + 1) * HEAD_DIM, cols] = part * (1.0 / total)
            lse_ref[0, head : head + 1, cols] = top + jnp.log(total)
    out_ref[...] = ot_ref[...].T.astype(BF16)


def attend_call(length, qkv, first, count):
    seq = qkv.shape[0]
    pairs = qkv.shape[1] // 3 // LANES
    width = count * LANES
    return pl.pallas_call(
        attend_kernel,
        grid=(count,),
        in_specs=[smem()]
        + [pl.BlockSpec((seq, LANES), lambda p, part=part: (0, part * pairs + first + p)) for part in range(3)],
        out_specs=[
            pl.BlockSpec((seq, LANES), lambda p: (0, p)),
            pl.BlockSpec((1, 8, seq), lambda p: (p, 0, 0)),
        ],
        out_shape=[
            jax.ShapeDtypeStruct((seq, width), BF16),
            jax.ShapeDtypeStruct((count, 8, seq), F32),
        ],
        scratch_shapes=[
            pltpu.VMEM((seq, LANES), BF16),
            pltpu.VMEM((seq, LANES), BF16),
            pltpu.VMEM((LANES, seq), BF16),
            pltpu.VMEM((LANES, seq), F32),
        ],
        compiler_params=params(),
        cost_estimate=cost(12),
        name="attend",
    )(length, qkv, qkv, qkv)


def attend_back_kernel(
    len_ref,
    q_ref,
    k_ref,
    v_ref,
    do_ref,
    o_ref,
    lse_ref,
    normed_ref,
    at_ref,
    dqkv_ref,
    keep_ref,
    send_ref,
    nt_ref,
    kt_ref,
    kh_ref,
    qh_ref,
    qm_ref,
    vh_ref,
    dh_ref,
    dk_ref,
    dv_ref,
    dqt_ref,
    pt_ref,
    join_ref,
):
    seq = q_ref.shape[0]
    block = 256
    length = len_ref[0]

    @pl.when(pl.program_id(0) == 0)
    def _():
        nt_ref[...] = normed_ref[...].astype(F32).T.astype(BF16)

    kt_ref[...] = k_ref[...].astype(F32).T.astype(BF16)
    pt_ref[...] = (do_ref[...].astype(F32) * o_ref[...].astype(F32)).T
    dk_ref[...] = jnp.zeros_like(dk_ref)
    dv_ref[...] = jnp.zeros_like(dv_ref)
    for head in range(2):
        rows = slice(head * HEAD_DIM, (head + 1) * HEAD_DIM)
        inside, k_head, q_head, q_masked = head_parts(head, length, q_ref[...], k_ref[...])
        kh_ref[...] = k_head
        qh_ref[...] = q_head
        qm_ref[...] = q_masked
        vh_ref[...] = jnp.where(inside, v_ref[...].astype(F32), 0.0).astype(BF16)
        dh_ref[...] = jnp.where(inside, do_ref[...].astype(F32), 0.0).astype(BF16)
        for qb in range(seq // block):
            ext = (qb + 1) * block
            cols = slice(qb * block, ext)
            delta = jnp.sum(pt_ref[rows, cols], axis=0, keepdims=True)
            scores = causal(dot_nt(kh_ref[:ext, :], qh_ref[cols, :]), block)
            probs = jnp.exp(scores - lse_ref[0, head : head + 1, cols])
            dprobs = dot_nt(vh_ref[:ext, :], dh_ref[cols, :])
            dscores = (probs * (dprobs - delta)).astype(BF16)
            dv_ref[:ext, :] += dot_nn(probs.astype(BF16), dh_ref[cols, :])
            dk_ref[:ext, :] += dot_nn(dscores, qm_ref[cols, :])
            dqt_ref[rows, cols] = dot_nn(kt_ref[rows, :ext], dscores)
    dq = (dqt_ref[...].T * (HEAD_DIM**-0.5)).astype(BF16)
    dk = dk_ref[...].astype(BF16)
    dv = dv_ref[...].astype(BF16)
    dqkv_ref[0] = dq
    dqkv_ref[1] = dk
    dqkv_ref[2] = dv
    joined = dot_nn(nt_ref[...], jnp.concatenate([dq, dk, dv], axis=1))
    join_ref[...] = joined.reshape(join_ref.shape)
    for chip in range(4):
        for far in range(4):
            for core, ref in enumerate((keep_ref, send_ref)):
                piece = join_ref[block_at(at_ref, chip, core, far)].astype(BF16)
                for part in range(3):
                    ref[chip, far, part] = piece[:, part * LANES : (part + 1) * LANES]


def attend_back_call(length, qkv, dmixed, mixed, lse, normed, at, first, count):
    seq, width = normed.shape
    pairs = width // LANES
    tall = width // BLOCKS
    part_width = count * LANES
    col = lambda p: (0, p)
    return pl.pallas_call(
        attend_back_kernel,
        grid=(count,),
        in_specs=[smem()]
        + [pl.BlockSpec((seq, LANES), lambda p, part=part: (0, part * pairs + first + p)) for part in range(3)]
        + [
            pl.BlockSpec((seq, LANES), lambda p: (0, first + p)),
            pl.BlockSpec((seq, LANES), col),
            pl.BlockSpec((1, 8, seq), lambda p: (p, 0, 0)),
            full((seq, width)),
            smem(),
        ],
        out_specs=[pl.BlockSpec((3, seq, LANES), lambda p: (0, 0, p))]
        + [pl.BlockSpec((4, 4, 3, tall, LANES), lambda p: (0, 0, 0, 0, p))] * 2,
        out_shape=[jax.ShapeDtypeStruct((3, seq, part_width), BF16)]
        + [jax.ShapeDtypeStruct((4, 4, 3, tall, part_width), BF16)] * 2,
        scratch_shapes=[
            pltpu.VMEM((width, seq), BF16),
            pltpu.VMEM((LANES, seq), BF16),
            pltpu.VMEM((seq, LANES), BF16),
            pltpu.VMEM((seq, LANES), BF16),
            pltpu.VMEM((seq, LANES), BF16),
            pltpu.VMEM((seq, LANES), BF16),
            pltpu.VMEM((seq, LANES), BF16),
            pltpu.VMEM((seq, LANES), F32),
            pltpu.VMEM((seq, LANES), F32),
            pltpu.VMEM((LANES, seq), F32),
            pltpu.VMEM((LANES, seq), F32),
            pltpu.VMEM((BLOCKS, tall, 3 * LANES), F32),
        ],
        compiler_params=params(),
        cost_estimate=cost(5),
        name="attend_back",
    )(length, qkv, qkv, qkv, dmixed, mixed, lse, normed, at)


def route_kernel(
    experts, group, capacity, len_ref, me_ref, route_ref, pair_ref, cot_ref, slot_ref, slot_t_ref, out_ref
):
    seq = route_ref.shape[1]
    half = experts // 2
    per = half // group
    local = 2 * per
    length = len_ref[0]
    me = me_ref[0]
    live = lax.broadcasted_iota(jnp.int32, (1, seq), 1) < length
    ids = lax.broadcasted_iota(jnp.int32, (experts, seq), 0)
    upper = (
        lax.broadcasted_iota(jnp.int32, (seq, seq), 0) < lax.broadcasted_iota(jnp.int32, (seq, seq), 1)
    )
    upper = jnp.where(upper, 1.0, 0.0).astype(BF16)
    before = jnp.zeros((experts, 1), F32)
    slots = []
    for choice in range(2):
        named = route_ref[choice : choice + 1, :]
        hot = jnp.where((ids == named) & live, 1.0, 0.0)
        earlier = dot_nn(hot.astype(BF16), upper) + before
        rank = jnp.sum(hot * earlier, axis=0, keepdims=True).astype(jnp.int32)
        before = before + jnp.sum(hot, axis=1, keepdims=True)
        is_new = named >= half
        within = jnp.where(is_new, named - half, named)
        owner = within // per
        place = jnp.where(is_new, per, 0) + within - owner * per
        shift = owner - me
        shift = jnp.where(shift < 0, shift + group, shift)
        slot = (shift * local + place) * capacity + rank
        slots.append(jnp.where(live & (rank < capacity), slot, -1))
    slot_ref[...] = jnp.concatenate(slots + [jnp.full((6, seq), -1, jnp.int32)], axis=0)
    slot_t_ref[...] = jnp.concatenate(
        [slot.astype(F32) for slot in slots] + [jnp.full((LANES - 2, seq), -1.0, F32)], axis=0
    ).T.astype(jnp.int32)
    total = experts * capacity
    place = lax.broadcasted_iota(jnp.int32, (total, seq), 0)
    select = jnp.where((place == slots[0]) | (place == slots[1]), 1.0, 0.0).astype(BF16)
    rows = dot_nn(select, cot_ref[...]).astype(BF16)
    both = (pair_ref[:, 0:1] + pair_ref[:, 1:2]).astype(F32)
    lane = lax.broadcasted_iota(jnp.int32, (seq, LANES), 1)
    tail = dot_nn(select, jnp.where(lane == 0, both, 0.0).astype(BF16)).astype(BF16)
    width = cot_ref.shape[1]
    size = local * capacity
    for shift in range(group):
        piece = slice(shift * size, (shift + 1) * size)
        place = lax.rem(me + shift, group)
        out_ref[place, :, :, :width] = rows[piece].reshape(local, capacity, width)
        out_ref[place, :, :, width:] = tail[piece].reshape(local, capacity, LANES)


def route_call(length, me, routes, cotangent, experts, group, capacity):
    seq, width = cotangent.shape
    local = experts // group
    wide = width + LANES
    return pl.pallas_call(
        functools.partial(route_kernel, experts, group, capacity),
        in_specs=[smem(), smem(), full((2, seq)), full((seq, 2)), full((seq, width))],
        out_specs=[full((8, seq)), full((seq, LANES)), full((group, local, capacity, wide))],
        out_shape=[
            jax.ShapeDtypeStruct((8, seq), jnp.int32),
            jax.ShapeDtypeStruct((seq, LANES), jnp.int32),
            jax.ShapeDtypeStruct((group, local, capacity, wide), BF16),
        ],
        grid=(1,),
        compiler_params=params(),
        cost_estimate=cost(5.7),
        name="route",
    )(length, me, routes.T, routes, cotangent)


def project_kernel(
    group, low_ref, high_ref, tok_ref, w_ref, scale_ref, slot_ref, res_ref, *refs
):
    out_refs = refs[:group]
    normed_ref = refs[group]
    step = pl.program_id(0)
    block = tok_ref.shape[0]
    mixed = jnp.concatenate([low_ref[...], high_ref[...]], axis=1)
    residual = tok_ref[...].astype(F32) + dot_nn(mixed, w_ref[...])
    res_ref[...] = residual
    xhat, _ = norm_parts(residual)
    normed = (xhat * scale_ref[2:3, :] + scale_ref[3:4, :]).astype(BF16)
    normed_ref[pl.ds(pl.multiple_of(step * block, block), block), :] = normed

    @pl.when(step == pl.num_programs(0) - 1)
    def _():
        local, capacity, width = out_refs[0].shape
        size = local * capacity
        seq = normed_ref.shape[0]
        place = lax.broadcasted_iota(jnp.int32, (size * group, seq), 0)
        select = (place == slot_ref[0:1, :]) | (place == slot_ref[1:2, :])
        select = jnp.where(select, 1.0, 0.0).astype(BF16)
        rows = dot_nn(select, normed_ref[...]).astype(BF16)
        for shift in range(group):
            out_refs[shift][...] = rows[shift * size : (shift + 1) * size].reshape(local, capacity, width)


def project_call(mixed, tokens, weight, scales, slots, group, local, capacity):
    seq, width = tokens.shape
    block = 256
    rows = pl.BlockSpec((block, width), lambda i: (i, 0))
    half = pl.BlockSpec((block, width // 2), lambda i: (i, 0))
    return pl.pallas_call(
        functools.partial(project_kernel, group),
        grid=(seq // block,),
        in_specs=[half, half, rows, full((width, width)), full((4, width)), full((8, seq))],
        out_specs=[rows] + [full((local, capacity, width))] * group,
        out_shape=[jax.ShapeDtypeStruct((seq, width), F32)]
        + [jax.ShapeDtypeStruct((local, capacity, width), BF16)] * group,
        scratch_shapes=[pltpu.VMEM((seq, width), BF16)],
        compiler_params=params(),
        cost_estimate=cost(8.8),
        name="project_dispatch",
    )(*mixed, tokens, weight, scales, slots)


def expert_kernel(trained, group, held, pick, own_ref, *refs):
    x_refs = refs[:group]
    g_ref, wr_ref, wrt_ref = refs[group : group + 3]
    in_refs = refs[group + 3 : group + 13]
    out_w_refs = refs[group + 13 : group + 23]
    rest = refs[group + 23 + held :]
    out_ref = rest[0]
    back_refs = rest[1 : group + 1]
    router_ref = rest[group + 1]
    rest = rest[group + 2 :]
    if trained:
        grad_refs = rest[:4]
        rest = rest[4:]
    x_ref, dexp_ref, gate_ref, acc_ref, back_ref, xt_ref, win_ref, wout_ref, din_ref, dout_ref, sems = rest
    step = pl.program_id(0)
    capacity, width = back_refs[0].shape
    own = own_ref[0]

    def source(shift):
        return lax.rem(own_ref[3] - shift + group, group)

    def other_of(tail):
        return tail[:, 0:1].astype(F32).astype(jnp.int32) - own

    def copies(step_chip):
        made = []
        chunk = win_ref.shape[2]
        cols = pl.ds(pl.multiple_of((own_ref[2] ^ step_chip) * chunk, LANES), chunk)
        for which in range(2):
            core = own_ref[1] ^ which
            for index, (chip, lower) in enumerate(PLACES):
                piece = in_refs[5 * which + index]
                tall = piece.shape[1]
                at = ((own_ref[2] ^ chip) * 2 + core) * in_refs[0].shape[1] + lower * tall
                rows = pl.ds(pl.multiple_of(at, 16), tall)
                made.append((piece.at[pick, :, cols], win_ref.at[step_chip, rows, :]))
                if chip == step_chip:
                    piece = out_w_refs[5 * which + index]
                    tall = piece.shape[1]
                    rows = pl.ds(pl.multiple_of(core * out_w_refs[0].shape[1] + lower * tall, 16), tall)
                    made.append((piece.at[pick], wout_ref.at[step_chip, rows, :]))
        return [
            pltpu.make_async_copy(src, dst, sems.at[step_chip, i]) for i, (src, dst) in enumerate(made)
        ]

    @pl.when(step == 0)
    def _():
        for chip in range(4):
            for copy in copies(chip):
                copy.start()
        for shift in range(group):
            span = slice(shift * capacity, (shift + 1) * capacity)
            rows = x_refs[shift][0]
            x_ref[span, :] = rows
            logits = dot_nn(rows, wr_ref[...])
            lane = lax.broadcasted_iota(jnp.int32, logits.shape, 1)
            other = other_of(g_ref[source(shift), 0, :, width:])
            mine = jnp.sum(jnp.where(lane == own, logits, 0.0), axis=1, keepdims=True)
            theirs = jnp.sum(jnp.where(lane == other, logits, 0.0), axis=1, keepdims=True)
            top = jnp.maximum(mine, theirs)
            up = jnp.exp(mine - top)
            gate = up / (up + jnp.exp(theirs - top))
            gate_ref[span, :] = jnp.broadcast_to(gate, (capacity, LANES))
            dexp_ref[span, :] = (gate * g_ref[source(shift), 0, :, :width].astype(F32)).astype(BF16)
        acc_ref[...] = jnp.zeros_like(acc_ref)
        back_ref[...] = jnp.zeros_like(back_ref)
        xt_ref[...] = x_ref[...].astype(F32).T.astype(BF16)

    for chip in range(4):

        @pl.when(step == chip)
        def _(chip=chip):
            for copy in copies(chip):
                copy.wait()

    win = win_ref[step]
    wout = wout_ref[step]
    pre = dot_nn(x_ref[...], win)
    square = pre * pre
    tanh = jnp.tanh(0.7978845608028654 * (pre + 0.044715 * pre * square))
    half = 0.5 * (1.0 + tanh)
    hid = (pre * half).astype(BF16)
    slope = half + (0.5 * pre) * (1.0 - tanh * tanh) * (0.7978845608028654 + 0.1070322243 * square)
    acc_ref[...] += dot_nn(hid, wout)
    dpre = (dot_nt(dexp_ref[...], wout) * slope).astype(BF16)
    back_ref[...] += dot_nt(dpre, win)
    if trained:
        dout_ref[...] = dot_tn(hid, dexp_ref[...]).astype(BF16).reshape(dout_ref.shape)
        din_ref[...] = dot_nn(xt_ref[...], dpre).astype(BF16).reshape(din_ref.shape)
        for which in range(2):
            core = own_ref[1] ^ which
            for chip in range(4):
                grad_refs[which][chip] = din_ref[(own_ref[2] ^ chip) * 2 + core]
            grad_refs[2 + which][0] = dout_ref[core]

    @pl.when(step == pl.num_programs(0) - 1)
    def _():
        router = jnp.zeros((LANES, width), F32)
        for shift in range(group):
            span = slice(shift * capacity, (shift + 1) * capacity)
            gate = gate_ref[span, 0:1]
            result = acc_ref[span, :]
            out_ref[source(shift), 0] = (gate * result).astype(BF16)
            dot = jnp.sum(result * g_ref[source(shift), 0, :, :width].astype(F32), axis=1, keepdims=True)
            coef = gate * (1.0 - gate) * dot
            lane = lax.broadcasted_iota(jnp.int32, (capacity, LANES), 1)
            other = other_of(g_ref[source(shift), 0, :, width:])
            sign = jnp.where(lane == own, 1.0, 0.0) - jnp.where(lane == other, 1.0, 0.0)
            dlogits = (coef * sign).astype(BF16)
            back_refs[shift][...] = (back_ref[span, :] + dot_nn(dlogits, wrt_ref[...])).astype(BF16)
            router = router + dot_tn(dlogits, x_ref[span, :])
        router_ref[...] = router


def expert_call(trained, place, local, own, rows, grads, router, router_t, held, pick, w_in, w_out):
    group = len(rows)
    _, capacity, width = rows[0].shape
    inner = w_in[0].shape[2]
    chunk = inner // 4
    block = lambda f, own: own[2] ^ f
    wide = grads.shape[3]
    many = group * capacity
    shard, deep = width // 8, inner // 8
    out_specs = [pl.BlockSpec((group, 1, capacity, width), lambda f, own: (0, place, 0, 0))]
    out_specs += [full((capacity, width))] * group + [full((LANES, width))]
    out_shape = [jax.ShapeDtypeStruct((group, local, capacity, width), BF16)]
    out_shape += [jax.ShapeDtypeStruct((capacity, width), BF16)] * group
    out_shape += [jax.ShapeDtypeStruct((LANES, width), F32)]
    if trained:
        out_specs += [pl.BlockSpec((4, shard, chunk), lambda f, own: (0, 0, block(f, own)))] * 2
        out_specs += [pl.BlockSpec((1, deep, width), lambda f, own: (f, 0, 0))] * 2
        out_shape += [jax.ShapeDtypeStruct((4, shard, inner), BF16)] * 2
        out_shape += [jax.ShapeDtypeStruct((4, deep, width), BF16)] * 2
    return pl.pallas_call(
        functools.partial(expert_kernel, trained, group, len(held), pick),
        grid_spec=pltpu.PrefetchScalarGridSpec(
            num_scalar_prefetch=1,
            grid=(4,),
            in_specs=[pl.BlockSpec((1, capacity, width), lambda f, own: (place, 0, 0))] * group
            + [pl.BlockSpec((group, 1, capacity, wide), lambda f, own: (0, place, 0, 0))]
            + [full((width, LANES)), full((LANES, width))]
            + [pl.BlockSpec(memory_space=pl.ANY)] * (len(w_in) + len(w_out) + len(held)),
            out_specs=out_specs,
            scratch_shapes=[
            pltpu.VMEM((many, width), BF16),
            pltpu.VMEM((many, width), BF16),
            pltpu.VMEM((many, LANES), F32),
            pltpu.VMEM((many, width), F32),
            pltpu.VMEM((many, width), F32),
            pltpu.VMEM((width, many), BF16),
            pltpu.VMEM((4, width, chunk), BF16),
            pltpu.VMEM((4, chunk, width), BF16),
            pltpu.VMEM((8, shard, chunk) if trained else (8, LANES), BF16),
            pltpu.VMEM((2, deep, width) if trained else (8, LANES), BF16),
            pltpu.SemaphoreType.DMA((4, 14)),
            ],
        ),
        out_shape=out_shape,
        input_output_aliases={group + 24: 0} if held else {},
        compiler_params=params(),
        cost_estimate=cost(23 if trained else 17),
        name="experts_new" if trained else "experts_old",
    )(own, *rows, grads, router, router_t, *w_in, *w_out, *held)


def pick_matrix(slot_ref, total):
    place = lax.broadcasted_iota(jnp.int32, (slot_ref.shape[0], total), 1)
    hit = (place == slot_ref[:, 0:1]) | (place == slot_ref[:, 1:2])
    return jnp.where(hit, 1.0, 0.0).astype(BF16)


def pick_rows(slot_ref, part_refs):
    width = part_refs[0].shape[-1]
    held = jnp.concatenate([part[...].reshape(-1, width) for part in part_refs], axis=0)
    return dot_nn(pick_matrix(slot_ref, held.shape[0]), held)


def combine_kernel(me_ref, slot_ref, res_ref, part_ref, out_ref):
    group, _, _, width = part_ref.shape
    parts = [part_ref[lax.rem(me_ref[0] + shift, group)].reshape(-1, width) for shift in range(group)]
    held = jnp.concatenate(parts, axis=0)
    out_ref[...] = res_ref[...] + dot_nn(pick_matrix(slot_ref, held.shape[0]), held)


def combine_call(me, slots, residual, parts):
    seq, width = residual.shape
    block = 256
    rows = pl.BlockSpec((block, width), lambda i: (i, 0))
    return pl.pallas_call(
        combine_kernel,
        grid=(seq // block,),
        in_specs=[smem(), pl.BlockSpec((block, LANES), lambda i: (i, 0)), rows, full(parts.shape)],
        out_specs=rows,
        out_shape=jax.ShapeDtypeStruct((seq, width), F32),
        compiler_params=params(),
        cost_estimate=cost(6.2),
        name="combine",
    )(me, slots, residual, parts)


def middle_kernel(count, slot_ref, res_ref, cot_ref, gain_ref, low_ref, high_ref, w_ref, at_ref, *refs):
    parts = refs[:count]
    dres_ref, dmix_ref, keep_ref, send_ref, sums_ref, acc_ref = refs[count:]
    step = pl.program_id(0)
    dnormed = pick_rows(slot_ref, parts)
    xhat, scale = norm_parts(res_ref[...])
    dres = cot_ref[...].astype(F32) + norm_back(dnormed, gain_ref[2:3, :], xhat, scale)
    dres_ref[...] = dres
    dattn = dres.astype(BF16)
    dmix_ref[...] = dot_nt(dattn, w_ref[...]).astype(BF16)

    @pl.when(step == 0)
    def _():
        sums_ref[...] = jnp.zeros_like(sums_ref)
        acc_ref[...] = jnp.zeros_like(acc_ref)

    mixed = jnp.concatenate([low_ref[...], high_ref[...]], axis=1)
    acc_ref[...] += dot_tn(mixed, dattn).reshape(acc_ref.shape)
    sums_ref[0:1, :] += jnp.sum(dnormed * xhat, axis=0, keepdims=True)
    sums_ref[1:2, :] += jnp.sum(dnormed, axis=0, keepdims=True)

    @pl.when(step == pl.num_programs(0) - 1)
    def _():
        for chip in range(4):
            for far in range(4):
                for core, ref in enumerate((keep_ref, send_ref)):
                    piece = acc_ref[block_at(at_ref, chip, core, far)].astype(BF16)
                    ref[chip, far, 0] = piece[:, : piece.shape[1] // 2]
                    ref[chip, far, 1] = piece[:, piece.shape[1] // 2 :]


def middle_call(slots, residual, cotangent, gain, mixed, weight, at, parts):
    seq, width = residual.shape
    tall = width // BLOCKS
    block = 256
    capacity = parts[0].shape[0]
    rows = pl.BlockSpec((block, width), lambda i: (i, 0))
    half = pl.BlockSpec((block, width // 2), lambda i: (i, 0))
    return pl.pallas_call(
        functools.partial(middle_kernel, len(parts)),
        grid=(seq // block,),
        in_specs=[
            pl.BlockSpec((block, LANES), lambda i: (i, 0)),
            rows,
            rows,
            full((4, width)),
            half,
            half,
            full((width, width)),
            smem(),
        ]
        + [full((capacity, width))] * len(parts),
        out_specs=[rows, rows] + [full((4, 4, 2, tall, width // 2))] * 2 + [full((8, width))],
        out_shape=[
            jax.ShapeDtypeStruct((seq, width), F32),
            jax.ShapeDtypeStruct((seq, width), BF16),
            jax.ShapeDtypeStruct((4, 4, 2, tall, width // 2), BF16),
            jax.ShapeDtypeStruct((4, 4, 2, tall, width // 2), BF16),
            jax.ShapeDtypeStruct((8, width), F32),
        ],
        scratch_shapes=[pltpu.VMEM((BLOCKS, tall, width), F32)],
        compiler_params=params(),
        cost_estimate=cost(13),
        name="middle_back",
    )(slots, residual, cotangent, gain, *mixed, weight, at, *parts)


def last_kernel(low_ref, high_ref, tok_ref, dres_ref, gain_ref, w_ref, out_ref, sums_ref):
    width = tok_ref.shape[1]
    grads = [ref[part] for part in range(3) for ref in (low_ref, high_ref)]
    dnormed = dot_nt(jnp.concatenate(grads, axis=1), w_ref[...])
    xhat, scale = norm_parts(tok_ref[...].astype(F32))
    out_ref[...] = dres_ref[...] + norm_back(dnormed, gain_ref[0:1, :], xhat, scale)

    @pl.when(pl.program_id(0) == 0)
    def _():
        sums_ref[...] = jnp.zeros_like(sums_ref)

    sums_ref[0:1, :] += jnp.sum(dnormed * xhat, axis=0, keepdims=True)
    sums_ref[1:2, :] += jnp.sum(dnormed, axis=0, keepdims=True)


def last_call(dqkv, tokens, dres, gain, weight):
    seq, width = tokens.shape
    block = 256
    rows = pl.BlockSpec((block, width), lambda i: (i, 0))
    return pl.pallas_call(
        last_kernel,
        grid=(seq // block,),
        in_specs=[
            pl.BlockSpec((3, block, width // 2), lambda i: (0, i, 0)),
            pl.BlockSpec((3, block, width // 2), lambda i: (0, i, 0)),
            rows,
            rows,
            full((4, width)),
            full((width, 3 * width)),
        ],
        out_specs=[rows, full((8, width))],
        out_shape=[
            jax.ShapeDtypeStruct((seq, width), F32),
            jax.ShapeDtypeStruct((8, width), F32),
        ],
        compiler_params=params(),
        cost_estimate=cost(5),
        name="last_back",
    )(*dqkv, tokens, dres, gain, weight)


def unpack_kernel(outs, parts, at_ref, *refs):
    pieces = refs[:8]
    out_refs = refs[-outs:]
    tall = pieces[0].shape[1]
    part = pl.program_id(0)

    def put(out_ref):
        for index, piece in enumerate(pieces):

            def each(far, carry, index=index, piece=piece):
                place = (at_ref[0] ^ index) * 4 + (at_ref[1] ^ ((far >> 1) | ((far & 1) << 1)))
                rows = pl.ds(pl.multiple_of(place * tall, 8), tall)
                out_ref[rows, :] = piece[far * parts + part].astype(F32)
                return carry

            lax.fori_loop(0, 4, each, 0)

    @pl.when(part < 3)
    def _():
        put(out_refs[0])

    if outs > 1:

        @pl.when(part >= 3)
        def _():
            put(out_refs[1])


def unpack_call(at, pieces, half, base=None):
    blocks, tall, part_width = pieces[0].shape
    parts = blocks // 4
    width = tall * BLOCKS
    out_specs = [pl.BlockSpec((width, part_width), lambda p: (0, 2 * jnp.minimum(p, 2) + half))]
    out_shape = [jax.ShapeDtypeStruct((width, 6 * part_width), F32)]
    if parts > 3:
        out_specs.append(pl.BlockSpec((width, part_width), lambda p: (0, jnp.maximum(p - 3, 0))))
        out_shape.append(jax.ShapeDtypeStruct((width, width), F32))
    held = [] if base is None else [base]
    return pl.pallas_call(
        functools.partial(unpack_kernel, len(out_shape), parts),
        grid=(parts,),
        in_specs=[smem()]
        + [full((blocks, tall, part_width))] * 8
        + [pl.BlockSpec(memory_space=pl.ANY)] * len(held),
        out_specs=out_specs,
        out_shape=out_shape,
        input_output_aliases={9: 0} if held else {},
        compiler_params=params(),
        cost_estimate=cost(4),
        name="unpack",
    )(at, *pieces, *held)


def swap(block, bits):
    size = lax.axis_size("batch")
    return lax.ppermute(block, "batch", [(i, i ^ bits) for i in range(size)])


def across(block, bits):
    size = lax.axis_size("expert")
    return lax.ppermute(block, "expert", [(i, i ^ bits) for i in range(size)])


def added(*blocks):
    total = blocks[0].astype(F32)
    for block in blocks[1:]:
        total = total + block.astype(F32)
    return total


def gather_shards(shard):
    whole = lax.all_gather(shard, "batch", axis=1, tiled=True)
    some, rows, width = whole.shape
    parts = whole.reshape(some, 4, 2, rows // 8, width)
    half = rows // 16
    return [
        parts[:, chip, core, lower * half : (lower + 1) * half] if chip == 3 else parts[:, chip, core]
        for core in range(2)
        for chip, lower in PLACES
    ]


def near(shard):
    return [swap(shard, 2), swap(shard, 4)]


def relay(full_x, full_y):
    half = full_x.shape[1] // 2
    return [swap(full_y[:, :half], 2), swap(full_x[:, half:], 4)]


def tie(*values):
    return list(lax.optimization_barrier(values))


def sum_all(keep, send):
    keep, send = lax.psum((keep, send), ("expert", "batch"))
    pieces = []
    for chip in range(4):
        for half in (keep, send):
            parts = jnp.concatenate([part[chip] for part in half], axis=1)
            pieces.append(jnp.concatenate([parts[far] for far in range(4)]))
    return pieces


def sum_core(keep, send):
    got = [swap(part, 1) for part in send]
    halves = []
    for chip in range(4):
        parts = [added(mine[chip], other[chip]) for mine, other in zip(keep, got)]
        halves.append(jnp.concatenate(parts, axis=1).astype(BF16))
    return halves


def to_chips(halves):
    return [halves[0]] + [swap(halves[chip], 2 * chip) for chip in (1, 2, 3)]


def total(parts):
    return added(*parts).astype(BF16)


def give(block, bits):
    rows = block.shape[0] // 2
    return [block[:rows], across(block[rows:], bits)]


def spread_chips(column):
    return [column] + [swap(column, 2 * chip) for chip in (1, 2, 3)]


def spread_cores(blocks):
    return [piece for block in blocks for piece in (block, swap(block, 1))]


def packed(small):
    half = small.shape[1] // 2
    return jnp.concatenate([small[:, :half], small[:, half:]])


def unpacked(small):
    half = small.shape[0] // 2
    return jnp.concatenate([small[:half], small[half:]], axis=1)


def natural(keep, send):
    both = jnp.stack([keep, send], axis=1)
    return both.reshape(-1, both.shape[-1])


def body(
    tokens,
    lengths,
    routes,
    ln1_gain,
    ln1_bias,
    ln2_gain,
    ln2_bias,
    w_qkv,
    w_proj,
    w_router,
    old_in,
    old_out,
    new_in,
    new_out,
    cotangent,
):
    group = lax.axis_size("expert")
    me = lax.axis_index("expert")
    token_rows = tokens[0]
    cot_rows = cotangent[0]
    seq, width = token_rows.shape
    experts = w_router.shape[1]
    local = experts // group
    per = old_in.shape[0]
    capacity = max(4, seq // experts)
    scales = jnp.stack([ln1_gain, ln1_bias, ln2_gain, ln2_bias])

    def go(block, shift):
        if shift == 0:
            return block
        return lax.ppermute(block, "expert", [(i, (i + shift) % group) for i in range(group)])

    def trade(blocks):
        return lax.all_to_all(blocks, "expert", 0, 0, tiled=True)

    def come(block, shift):
        if shift == 0:
            return block
        return lax.ppermute(block, "expert", [(i, (i - shift) % group) for i in range(group)])

    fast = group == 4 and lax.axis_size("batch") == 8 and per == 1 and experts == 8
    at = jnp.stack([lax.axis_index("batch"), me]).astype(jnp.int32) if fast else jnp.zeros((2,), jnp.int32)
    me_one = jnp.full((1,), me, jnp.int32)
    pairs = width // LANES
    first_half = pairs // 2
    halves = ((0, first_half), (first_half, pairs - first_half))
    if fast:
        pair_in = jnp.stack([new_in[0], old_in[0]])
        pair_out = jnp.stack([new_out[0], old_out[0]])
        in_full = near(pair_in)
    slots, slots_t, sent_grads = route_call(
        lengths, me_one, routes[0], cot_rows, experts, group, capacity
    )
    grads = trade(sent_grads)
    token_rows, slots = tie(token_rows, slots)
    normed1, qkv = qkv_call(token_rows, scales, w_qkv)
    mixed_low, lse_low = attend_call(lengths, qkv, *halves[0])
    if fast:
        qkv, mixed_low, pair_in, pair_out, in_full[0], in_full[1] = tie(
            qkv, mixed_low, pair_in, pair_out, *in_full
        )
        in_half = relay(*in_full)
        in_other = [swap(part, 1) for part in (pair_in, *in_full)]
    mixed_high, lse_high = attend_call(lengths, qkv, *halves[1])
    if fast:
        mixed_high, pair_out, *tied = tie(mixed_high, pair_out, *in_half, *in_other)
        in_half, in_other = tied[:2], tied[2:]
        out_full = near(pair_out)
    mixed = (mixed_low, mixed_high)
    residual, *sent_rows = project_call(
        mixed, token_rows, w_proj, scales, slots, group, local, capacity
    )
    rows = [go(sent_rows[shift], shift) for shift in range(group)]
    if fast:
        rows[1], rows[3], pair_out, *tied = tie(rows[1], rows[3], pair_out, *out_full, *in_half)
        out_full, in_half = tied[:2], tied[2:]
        out_half = relay(*out_full)
        in_parts = [pair_in, *in_full, *in_half]
        out_parts = [pair_out, *out_full, *out_half]
        in_parts += in_other + [swap(part, 1) for part in in_half]
        out_parts += [swap(part, 1) for part in out_parts]
        weights = {True: (0, in_parts, out_parts), False: (1, in_parts, out_parts)}
    else:
        weights = {
            trained: (0, gather_shards(w_in), gather_shards(w_out))
            for trained, w_in, w_out in ((True, new_in, new_out), (False, old_in, old_out))
        }
    core, chip = (at[0] & 1, at[0] >> 1) if fast else (0, 0)
    router = jnp.pad(w_router, ((0, 0), (0, LANES - experts)))
    router_t = jnp.pad(w_router.T, ((0, LANES - experts), (0, 0)))
    outs, backs, router_sum = [], {}, 0.0
    half = experts // 2
    for trained in (True, False):
        for index in range(per):
            place = index + (per if trained else 0)
            own = jnp.stack([me * per + index + (half if trained else 0), core, chip, me]).astype(jnp.int32)
            got = expert_call(
                trained,
                place,
                local,
                own,
                rows,
                grads,
                router,
                router_t,
                outs,
                weights[trained][0] + index,
                *weights[trained][1:],
            )
            outs = [got[0]]
            sent = got[1 : group + 1]
            if fast and not trained:
                tied = tie(*sent, *backs[1])
                sent, backs[1] = tied[:group], tied[group:]
            backs[place] = [come(sent[shift], shift) for shift in range(group)]
            router_sum = router_sum + got[group + 1]
            if trained:
                in_keep, in_send, out_keep, out_send = got[group + 2 :]
    returned = [backs[p][shift] for shift in range(group) for p in range(local)]
    if fast:
        in_other, out_other = swap(in_send, 1), swap(out_send, 1)
        outs[0], in_keep, out_keep, in_other, out_other = tie(outs[0], in_keep, out_keep, in_other, out_other)
        in_rs = [total(pair) for pair in zip(in_keep, in_other)]
        out_rs = [total(pair) for pair in zip(out_keep, out_other)]
        in_got = [swap(in_rs[chip], 2 * chip) for chip in (1, 2)]
        tied = tie(*returned, in_rs[3], *out_rs)
        returned, in_rs[3], out_rs = tied[:-5], tied[-5], tied[-4:]
        in_got.append(swap(in_rs[3], 6))
    dres, dmixed, proj_keep, proj_send, sums2 = middle_call(
        slots_t, residual, cot_rows, scales, mixed, w_proj, at, returned
    )
    if fast:
        dmixed, outs[0], in_got[0], in_got[1], *out_rs = tie(dmixed, outs[0], in_got[0], in_got[1], *out_rs)
        out_got = [swap(out_rs[chip], 2 * chip) for chip in (1, 2)]
    else:
        natural_in = natural(in_keep, in_send)
        natural_out = natural(out_keep, out_send)
    back_outs = trade(outs[0])
    dq_low, keep_low, send_low = attend_back_call(
        lengths, qkv, dmixed, mixed_low, lse_low, normed1, at, *halves[0]
    )
    if fast:
        halves_low = sum_core((keep_low, proj_keep), (send_low, proj_send))
        dmixed, dq_low, in_got[2], out_got[0], out_got[1], out_rs[3] = tie(
            dmixed, dq_low, in_got[2], *out_got, out_rs[3]
        )
        out_got.append(swap(out_rs[3], 6))
    dq_high, keep_high, send_high = attend_back_call(
        lengths, qkv, dmixed, mixed_high, lse_high, normed1, at, *halves[1]
    )
    if fast:
        dq_high, keep_high, back_outs, *halves_low = tie(dq_high, keep_high, back_outs, *halves_low)
        low = to_chips(halves_low)
        halves_high = sum_core((keep_high,), (send_high,))
    input_grad, sums1 = last_call((dq_low, dq_high), token_rows, dres, scales, w_qkv)
    if fast:
        sums1, *halves_high = tie(sums1, *halves_high)
        high = to_chips(halves_high)
        small = jnp.concatenate([router_sum[:experts], sums1[:2], sums2[:2]], axis=0)
        low = give(total(low), 1)
        tied = tie(*low, *high)
        low = give(total(tied[:2]), 2)
        high = give(total(tied[2:]), 1)
        new_in_grad = added(in_rs[0], *in_got)
        new_in_grad, *tied = tie(new_in_grad, *low, *high)
        own_low = total(tied[:2])[0]
        low = [own_low, across(own_low, 2)]
        high = give(total(tied[2:]), 2)
        new_out_grad = added(out_rs[0], *out_got)
        new_out_grad, *tied = tie(new_out_grad, *low, *high)
        low = jnp.stack(tied[:2])
        low = [low, across(low, 1)]
        own_high = total(tied[2:])[0]
        mine = packed(small).astype(BF16)[None]
        high = [jnp.concatenate([own_high, mine])]
        high.append(across(high[0], 2))
        tied = tie(*low, *high)
        column_low = jnp.concatenate(tied[:2]).reshape(-1, *own_low.shape[1:])
        chips_low = spread_chips(column_low)
        parts = own_high.shape[0]
        mine = total([block[parts:] for block in tied[2:]])
        high = jnp.concatenate([block[:parts] for block in tied[2:]] + [mine])
        high = [high, across(high, 1)]
        mine = total([block[2 * parts :] for block in high])
        chips_high = spread_chips(jnp.concatenate([block[: 2 * parts] for block in high] + [mine]))
        output = combine_call(me_one, slots_t, residual, back_outs)
        output, *chips_low = tie(output, *chips_low)
        pieces_low = spread_cores(chips_low)
        qkv_grad, proj_grad = unpack_call(at, pieces_low, 0)
        qkv_grad, *chips_high = tie(qkv_grad, *chips_high)
        pieces_high = spread_cores(chips_high)
        small = unpacked(added(*[piece[4 * parts] for piece in pieces_high]))
    else:
        pieces_low = sum_all((keep_low, proj_keep), (send_low, proj_send))
        pieces_high = sum_all((keep_high,), (send_high,))
        small = jnp.concatenate([router_sum[:experts], sums1[:2], sums2[:2]], axis=0)
        small = jnp.sum(lax.all_gather(small, ("expert", "batch"), axis=0), axis=0)
        new_in_grad = lax.psum_scatter(natural_in, "batch", scatter_dimension=0, tiled=True)
        new_out_grad = lax.psum_scatter(natural_out, "batch", scatter_dimension=0, tiled=True)
    if not fast:
        output = combine_call(me_one, slots_t, residual, back_outs)
        qkv_grad, proj_grad = unpack_call(at, pieces_low, 0)
    (qkv_grad,) = unpack_call(at, pieces_high, 1, qkv_grad)
    return (
        output[None],
        input_grad[None],
        small[experts],
        small[experts + 1],
        small[experts + 2],
        small[experts + 3],
        qkv_grad,
        proj_grad,
        small[:experts].T,
        new_in_grad.astype(F32)[None],
        new_out_grad.astype(F32)[None],
    )


def solution(mesh):
    rows = P(("expert", "batch"), None, None)
    weights = P("expert", "batch", None)
    placed = (
        (rows, P(("expert", "batch")), rows)
        + (P(),) * 7
        + (weights,) * 4
        + (rows,)
    )
    return jax.shard_map(
        body,
        mesh=mesh,
        in_specs=placed,
        out_specs=(rows, rows) + (P(),) * 7 + (weights, weights),
        check_vma=False,
    )
```

```python
import functools

import jax
import jax.numpy as jnp
from jax import lax
from jax.experimental import pallas as pl
from jax.experimental.pallas import tpu as pltpu
from jax.sharding import PartitionSpec as P

HEAD_DIM = 64
LANES = 128
EPS = 1e-05
MASKED = -1e30
F32 = jnp.float32
BF16 = jnp.bfloat16
VMEM_LIMIT = 56 * 1024 * 1024
BLOCKS = 32
FAR = (0, 2, 1, 3)
PLACES = ((0, 0), (1, 0), (2, 0), (3, 0), (3, 1))


def params():
    return pltpu.CompilerParams(vmem_limit_bytes=VMEM_LIMIT)


def dot_nt(left, right):
    return lax.dot_general(left, right, (((1,), (1,)), ((), ())), preferred_element_type=F32)


def dot_tn(left, right):
    return lax.dot_general(left, right, (((0,), (0,)), ((), ())), preferred_element_type=F32)


def dot_nn(left, right):
    return jnp.dot(left, right, preferred_element_type=F32)


def norm_parts(rows):
    mean = jnp.mean(rows, axis=-1, keepdims=True)
    centred = rows - mean
    var = jnp.mean(centred * centred, axis=-1, keepdims=True)
    scale = lax.rsqrt(var + EPS)
    return centred * scale, scale


def norm_back(grad, gain, xhat, scale):
    a = grad * gain
    mean_a = jnp.mean(a, axis=-1, keepdims=True)
    mean_ax = jnp.mean(a * xhat, axis=-1, keepdims=True)
    return scale * (a - mean_a - xhat * mean_ax)


def full(shape):
    return pl.BlockSpec(shape, lambda *_: (0,) * len(shape))


def smem():
    return pl.BlockSpec(memory_space=pltpu.SMEM)


def cost(micros):
    return pl.CostEstimate(flops=int(micros * 1.1e9), transcendentals=0, bytes_accessed=int(micros * 3e6))


def block_at(at_ref, chip, core, far):
    return (at_ref[0] ^ (2 * chip + core)) * 4 + (at_ref[1] ^ FAR[far])


def qkv_kernel(tok_ref, scale_ref, w_ref, normed_ref, qkv_ref):
    xhat, _ = norm_parts(tok_ref[...].astype(F32))
    normed = (xhat * scale_ref[0:1, :] + scale_ref[1:2, :]).astype(BF16)
    normed_ref[...] = normed
    qkv_ref[...] = dot_nn(normed, w_ref[...]).astype(BF16)


def qkv_call(tokens, scales, weight):
    seq, width = tokens.shape
    block = 256
    cols = weight.shape[1]
    return pl.pallas_call(
        qkv_kernel,
        grid=(seq // block,),
        in_specs=[
            pl.BlockSpec((block, width), lambda i: (i, 0)),
            full((4, width)),
            full((width, cols)),
        ],
        out_specs=[
            pl.BlockSpec((block, width), lambda i: (i, 0)),
            pl.BlockSpec((block, cols), lambda i: (i, 0)),
        ],
        out_shape=[
            jax.ShapeDtypeStruct((seq, width), BF16),
            jax.ShapeDtypeStruct((seq, cols), BF16),
        ],
        compiler_params=params(),
        cost_estimate=cost(8.7),
        name="norm_qkv",
    )(tokens, scales, weight)


def head_parts(head, length, q, k):
    seq = q.shape[0]
    lane = lax.broadcasted_iota(jnp.int32, (seq, LANES), 1)
    row = lax.broadcasted_iota(jnp.int32, (seq, LANES), 0)
    inside = (lane // HEAD_DIM) == head
    extra = lane == (1 - head) * HEAD_DIM
    key_bias = jnp.where(row >= length, MASKED, 0.0)
    kf = k.astype(F32)
    qf = q.astype(F32) * (HEAD_DIM**-0.5)
    k_head = jnp.where(inside, kf, jnp.where(extra, key_bias, 0.0)).astype(BF16)
    q_head = jnp.where(inside, qf, jnp.where(extra, 1.0, 0.0)).astype(BF16)
    return inside, k_head, q_head, jnp.where(inside, qf, 0.0).astype(BF16)


def causal(scores, block):
    key = lax.broadcasted_iota(jnp.int32, (block, block), 0)
    query = lax.broadcasted_iota(jnp.int32, (block, block), 1)
    last = jnp.where(key <= query, scores[-block:], MASKED)
    if scores.shape[0] == block:
        return last
    return jnp.concatenate([scores[:-block], last], axis=0)


def attend_kernel(len_ref, q_ref, k_ref, v_ref, out_ref, lse_ref, kh_ref, qh_ref, vt_ref, ot_ref):
    seq = q_ref.shape[0]
    block = 256
    length = len_ref[0]
    vt_ref[...] = v_ref[...].astype(F32).T.astype(BF16)
    lse_ref[...] = jnp.zeros_like(lse_ref)
    for head in range(2):
        _, k_head, q_head, _ = head_parts(head, length, q_ref[...], k_ref[...])
        kh_ref[...] = k_head
        qh_ref[...] = q_head
        for qb in range(seq // block):
            ext = (qb + 1) * block
            cols = slice(qb * block, ext)
            scores = causal(dot_nt(kh_ref[:ext, :], qh_ref[cols, :]), block)
            top = jnp.max(scores, axis=0, keepdims=True)
            probs = jnp.exp(scores - top)
            total = jnp.sum(probs, axis=0, keepdims=True)
            part = dot_nn(vt_ref[head * HEAD_DIM : (head + 1) * HEAD_DIM, :ext], probs.astype(BF16))
            ot_ref[head * HEAD_DIM : (head + 1) * HEAD_DIM, cols] = part * (1.0 / total)
            lse_ref[0, head : head + 1, cols] = top + jnp.log(total)
    out_ref[...] = ot_ref[...].T.astype(BF16)


def attend_call(length, qkv, first, count):
    seq = qkv.shape[0]
    pairs = qkv.shape[1] // 3 // LANES
    width = count * LANES
    return pl.pallas_call(
        attend_kernel,
        grid=(count,),
        in_specs=[smem()]
        + [pl.BlockSpec((seq, LANES), lambda p, part=part: (0, part * pairs + first + p)) for part in range(3)],
        out_specs=[
            pl.BlockSpec((seq, LANES), lambda p: (0, p)),
            pl.BlockSpec((1, 8, seq), lambda p: (p, 0, 0)),
        ],
        out_shape=[
            jax.ShapeDtypeStruct((seq, width), BF16),
            jax.ShapeDtypeStruct((count, 8, seq), F32),
        ],
        scratch_shapes=[
            pltpu.VMEM((seq, LANES), BF16),
            pltpu.VMEM((seq, LANES), BF16),
            pltpu.VMEM((LANES, seq), BF16),
            pltpu.VMEM((LANES, seq), F32),
        ],
        compiler_params=params(),
        cost_estimate=cost(12),
        name="attend",
    )(length, qkv, qkv, qkv)


def attend_back_kernel(
    len_ref,
    q_ref,
    k_ref,
    v_ref,
    do_ref,
    o_ref,
    lse_ref,
    normed_ref,
    at_ref,
    dqkv_ref,
    keep_ref,
    send_ref,
    nt_ref,
    kt_ref,
    kh_ref,
    qh_ref,
    qm_ref,
    vh_ref,
    dh_ref,
    dk_ref,
    dv_ref,
    dqt_ref,
    pt_ref,
    join_ref,
):
    seq = q_ref.shape[0]
    block = 256
    length = len_ref[0]

    @pl.when(pl.program_id(0) == 0)
    def _():
        nt_ref[...] = normed_ref[...].astype(F32).T.astype(BF16)

    kt_ref[...] = k_ref[...].astype(F32).T.astype(BF16)
    pt_ref[...] = (do_ref[...].astype(F32) * o_ref[...].astype(F32)).T
    dk_ref[...] = jnp.zeros_like(dk_ref)
    dv_ref[...] = jnp.zeros_like(dv_ref)
    for head in range(2):
        rows = slice(head * HEAD_DIM, (head + 1) * HEAD_DIM)
        inside, k_head, q_head, q_masked = head_parts(head, length, q_ref[...], k_ref[...])
        kh_ref[...] = k_head
        qh_ref[...] = q_head
        qm_ref[...] = q_masked
        vh_ref[...] = jnp.where(inside, v_ref[...].astype(F32), 0.0).astype(BF16)
        dh_ref[...] = jnp.where(inside, do_ref[...].astype(F32), 0.0).astype(BF16)
        for qb in range(seq // block):
            ext = (qb + 1) * block
            cols = slice(qb * block, ext)
            delta = jnp.sum(pt_ref[rows, cols], axis=0, keepdims=True)
            scores = causal(dot_nt(kh_ref[:ext, :], qh_ref[cols, :]), block)
            probs = jnp.exp(scores - lse_ref[0, head : head + 1, cols])
            dprobs = dot_nt(vh_ref[:ext, :], dh_ref[cols, :])
            dscores = (probs * (dprobs - delta)).astype(BF16)
            dv_ref[:ext, :] += dot_nn(probs.astype(BF16), dh_ref[cols, :])
            dk_ref[:ext, :] += dot_nn(dscores, qm_ref[cols, :])
            dqt_ref[rows, cols] = dot_nn(kt_ref[rows, :ext], dscores)
    dq = (dqt_ref[...].T * (HEAD_DIM**-0.5)).astype(BF16)
    dk = dk_ref[...].astype(BF16)
    dv = dv_ref[...].astype(BF16)
    dqkv_ref[0] = dq
    dqkv_ref[1] = dk
    dqkv_ref[2] = dv
    joined = dot_nn(nt_ref[...], jnp.concatenate([dq, dk, dv], axis=1))
    join_ref[...] = joined.reshape(join_ref.shape)
    for chip in range(4):
        for far in range(4):
            for core, ref in enumerate((keep_ref, send_ref)):
                piece = join_ref[block_at(at_ref, chip, core, far)].astype(BF16)
                for part in range(3):
                    ref[chip, far, part] = piece[:, part * LANES : (part + 1) * LANES]


def attend_back_call(length, qkv, dmixed, mixed, lse, normed, at, first, count):
    seq, width = normed.shape
    pairs = width // LANES
    tall = width // BLOCKS
    part_width = count * LANES
    col = lambda p: (0, p)
    return pl.pallas_call(
        attend_back_kernel,
        grid=(count,),
        in_specs=[smem()]
        + [pl.BlockSpec((seq, LANES), lambda p, part=part: (0, part * pairs + first + p)) for part in range(3)]
        + [
            pl.BlockSpec((seq, LANES), lambda p: (0, first + p)),
            pl.BlockSpec((seq, LANES), col),
            pl.BlockSpec((1, 8, seq), lambda p: (p, 0, 0)),
            full((seq, width)),
            smem(),
        ],
        out_specs=[pl.BlockSpec((3, seq, LANES), lambda p: (0, 0, p))]
        + [pl.BlockSpec((4, 4, 3, tall, LANES), lambda p: (0, 0, 0, 0, p))] * 2,
        out_shape=[jax.ShapeDtypeStruct((3, seq, part_width), BF16)]
        + [jax.ShapeDtypeStruct((4, 4, 3, tall, part_width), BF16)] * 2,
        scratch_shapes=[
            pltpu.VMEM((width, seq), BF16),
            pltpu.VMEM((LANES, seq), BF16),
            pltpu.VMEM((seq, LANES), BF16),
            pltpu.VMEM((seq, LANES), BF16),
            pltpu.VMEM((seq, LANES), BF16),
            pltpu.VMEM((seq, LANES), BF16),
            pltpu.VMEM((seq, LANES), BF16),
            pltpu.VMEM((seq, LANES), F32),
            pltpu.VMEM((seq, LANES), F32),
            pltpu.VMEM((LANES, seq), F32),
            pltpu.VMEM((LANES, seq), F32),
            pltpu.VMEM((BLOCKS, tall, 3 * LANES), F32),
        ],
        compiler_params=params(),
        cost_estimate=cost(5),
        name="attend_back",
    )(length, qkv, qkv, qkv, dmixed, mixed, lse, normed, at)


def route_kernel(
    experts, group, capacity, len_ref, me_ref, route_ref, pair_ref, cot_ref, slot_ref, slot_t_ref, out_ref
):
    seq = route_ref.shape[1]
    half = experts // 2
    per = half // group
    local = 2 * per
    length = len_ref[0]
    me = me_ref[0]
    live = lax.broadcasted_iota(jnp.int32, (1, seq), 1) < length
    ids = lax.broadcasted_iota(jnp.int32, (experts, seq), 0)
    upper = (
        lax.broadcasted_iota(jnp.int32, (seq, seq), 0) < lax.broadcasted_iota(jnp.int32, (seq, seq), 1)
    )
    upper = jnp.where(upper, 1.0, 0.0).astype(BF16)
    before = jnp.zeros((experts, 1), F32)
    slots = []
    for choice in range(2):
        named = route_ref[choice : choice + 1, :]
        hot = jnp.where((ids == named) & live, 1.0, 0.0)
        earlier = dot_nn(hot.astype(BF16), upper) + before
        rank = jnp.sum(hot * earlier, axis=0, keepdims=True).astype(jnp.int32)
        before = before + jnp.sum(hot, axis=1, keepdims=True)
        is_new = named >= half
        within = jnp.where(is_new, named - half, named)
        owner = within // per
        place = jnp.where(is_new, per, 0) + within - owner * per
        shift = owner - me
        shift = jnp.where(shift < 0, shift + group, shift)
        slot = (shift * local + place) * capacity + rank
        slots.append(jnp.where(live & (rank < capacity), slot, -1))
    slot_ref[...] = jnp.concatenate(slots + [jnp.full((6, seq), -1, jnp.int32)], axis=0)
    slot_t_ref[...] = jnp.concatenate(
        [slot.astype(F32) for slot in slots] + [jnp.full((LANES - 2, seq), -1.0, F32)], axis=0
    ).T.astype(jnp.int32)
    total = experts * capacity
    place = lax.broadcasted_iota(jnp.int32, (total, seq), 0)
    select = jnp.where((place == slots[0]) | (place == slots[1]), 1.0, 0.0).astype(BF16)
    rows = dot_nn(select, cot_ref[...]).astype(BF16)
    both = (pair_ref[:, 0:1] + pair_ref[:, 1:2]).astype(F32)
    lane = lax.broadcasted_iota(jnp.int32, (seq, LANES), 1)
    tail = dot_nn(select, jnp.where(lane == 0, both, 0.0).astype(BF16)).astype(BF16)
    width = cot_ref.shape[1]
    size = local * capacity
    for shift in range(group):
        piece = slice(shift * size, (shift + 1) * size)
        place = lax.rem(me + shift, group)
        out_ref[place, :, :, :width] = rows[piece].reshape(local, capacity, width)
        out_ref[place, :, :, width:] = tail[piece].reshape(local, capacity, LANES)


def route_call(length, me, routes, cotangent, experts, group, capacity):
    seq, width = cotangent.shape
    local = experts // group
    wide = width + LANES
    return pl.pallas_call(
        functools.partial(route_kernel, experts, group, capacity),
        in_specs=[smem(), smem(), full((2, seq)), full((seq, 2)), full((seq, width))],
        out_specs=[full((8, seq)), full((seq, LANES)), full((group, local, capacity, wide))],
        out_shape=[
            jax.ShapeDtypeStruct((8, seq), jnp.int32),
            jax.ShapeDtypeStruct((seq, LANES), jnp.int32),
            jax.ShapeDtypeStruct((group, local, capacity, wide), BF16),
        ],
        grid=(1,),
        compiler_params=params(),
        cost_estimate=cost(5.7),
        name="route",
    )(length, me, routes.T, routes, cotangent)


def project_kernel(
    group, low_ref, high_ref, tok_ref, w_ref, scale_ref, slot_ref, res_ref, *refs
):
    out_refs = refs[:group]
    normed_ref = refs[group]
    step = pl.program_id(0)
    block = tok_ref.shape[0]
    mixed = jnp.concatenate([low_ref[...], high_ref[...]], axis=1)
    residual = tok_ref[...].astype(F32) + dot_nn(mixed, w_ref[...])
    res_ref[...] = residual
    xhat, _ = norm_parts(residual)
    normed = (xhat * scale_ref[2:3, :] + scale_ref[3:4, :]).astype(BF16)
    normed_ref[pl.ds(pl.multiple_of(step * block, block), block), :] = normed

    @pl.when(step == pl.num_programs(0) - 1)
    def _():
        local, capacity, width = out_refs[0].shape
        size = local * capacity
        seq = normed_ref.shape[0]
        place = lax.broadcasted_iota(jnp.int32, (size * group, seq), 0)
        select = (place == slot_ref[0:1, :]) | (place == slot_ref[1:2, :])
        select = jnp.where(select, 1.0, 0.0).astype(BF16)
        rows = dot_nn(select, normed_ref[...]).astype(BF16)
        for shift in range(group):
            out_refs[shift][...] = rows[shift * size : (shift + 1) * size].reshape(local, capacity, width)


def project_call(mixed, tokens, weight, scales, slots, group, local, capacity):
    seq, width = tokens.shape
    block = 256
    rows = pl.BlockSpec((block, width), lambda i: (i, 0))
    half = pl.BlockSpec((block, width // 2), lambda i: (i, 0))
    return pl.pallas_call(
        functools.partial(project_kernel, group),
        grid=(seq // block,),
        in_specs=[half, half, rows, full((width, width)), full((4, width)), full((8, seq))],
        out_specs=[rows] + [full((local, capacity, width))] * group,
        out_shape=[jax.ShapeDtypeStruct((seq, width), F32)]
        + [jax.ShapeDtypeStruct((local, capacity, width), BF16)] * group,
        scratch_shapes=[pltpu.VMEM((seq, width), BF16)],
        compiler_params=params(),
        cost_estimate=cost(8.8),
        name="project_dispatch",
    )(*mixed, tokens, weight, scales, slots)


def expert_kernel(trained, group, held, pick, own_ref, *refs):
    x_refs = refs[:group]
    g_ref, wr_ref, wrt_ref = refs[group : group + 3]
    in_refs = refs[group + 3 : group + 13]
    out_w_refs = refs[group + 13 : group + 23]
    rest = refs[group + 23 + held :]
    out_ref = rest[0]
    back_refs = rest[1 : group + 1]
    router_ref = rest[group + 1]
    rest = rest[group + 2 :]
    if trained:
        grad_refs = rest[:4]
        rest = rest[4:]
    x_ref, dexp_ref, gate_ref, acc_ref, back_ref, xt_ref, win_ref, wout_ref, din_ref, dout_ref, sems = rest
    step = pl.program_id(0)
    capacity, width = back_refs[0].shape
    own = own_ref[0]

    def source(shift):
        return lax.rem(own_ref[3] - shift + group, group)

    def other_of(tail):
        return tail[:, 0:1].astype(F32).astype(jnp.int32) - own

    def copies(step_chip):
        made = []
        chunk = win_ref.shape[2]
        cols = pl.ds(pl.multiple_of((own_ref[2] ^ step_chip) * chunk, LANES), chunk)
        for which in range(2):
            core = own_ref[1] ^ which
            for index, (chip, lower) in enumerate(PLACES):
                piece = in_refs[5 * which + index]
                tall = piece.shape[1]
                at = ((own_ref[2] ^ chip) * 2 + core) * in_refs[0].shape[1] + lower * tall
                rows = pl.ds(pl.multiple_of(at, 16), tall)
                made.append((piece.at[pick, :, cols], win_ref.at[step_chip, rows, :]))
                if chip == step_chip:
                    piece = out_w_refs[5 * which + index]
                    tall = piece.shape[1]
                    rows = pl.ds(pl.multiple_of(core * out_w_refs[0].shape[1] + lower * tall, 16), tall)
                    made.append((piece.at[pick], wout_ref.at[step_chip, rows, :]))
        return [
            pltpu.make_async_copy(src, dst, sems.at[step_chip, i]) for i, (src, dst) in enumerate(made)
        ]

    @pl.when(step == 0)
    def _():
        for chip in range(4):
            for copy in copies(chip):
                copy.start()
        for shift in range(group):
            span = slice(shift * capacity, (shift + 1) * capacity)
            rows = x_refs[shift][0]
            x_ref[span, :] = rows
            logits = dot_nn(rows, wr_ref[...])
            lane = lax.broadcasted_iota(jnp.int32, logits.shape, 1)
            other = other_of(g_ref[source(shift), 0, :, width:])
            mine = jnp.sum(jnp.where(lane == own, logits, 0.0), axis=1, keepdims=True)
            theirs = jnp.sum(jnp.where(lane == other, logits, 0.0), axis=1, keepdims=True)
            top = jnp.maximum(mine, theirs)
            up = jnp.exp(mine - top)
            gate = up / (up + jnp.exp(theirs - top))
            gate_ref[span, :] = jnp.broadcast_to(gate, (capacity, LANES))
            dexp_ref[span, :] = (gate * g_ref[source(shift), 0, :, :width].astype(F32)).astype(BF16)
        acc_ref[...] = jnp.zeros_like(acc_ref)
        back_ref[...] = jnp.zeros_like(back_ref)
        xt_ref[...] = x_ref[...].astype(F32).T.astype(BF16)

    for chip in range(4):

        @pl.when(step == chip)
        def _(chip=chip):
            for copy in copies(chip):
                copy.wait()

    win = win_ref[step]
    wout = wout_ref[step]
    pre = dot_nn(x_ref[...], win)
    square = pre * pre
    tanh = jnp.tanh(0.7978845608028654 * (pre + 0.044715 * pre * square))
    half = 0.5 * (1.0 + tanh)
    hid = (pre * half).astype(BF16)
    slope = half + (0.5 * pre) * (1.0 - tanh * tanh) * (0.7978845608028654 + 0.1070322243 * square)
    acc_ref[...] += dot_nn(hid, wout)
    dpre = (dot_nt(dexp_ref[...], wout) * slope).astype(BF16)
    back_ref[...] += dot_nt(dpre, win)
    if trained:
        dout_ref[...] = dot_tn(hid, dexp_ref[...]).astype(BF16).reshape(dout_ref.shape)
        din_ref[...] = dot_nn(xt_ref[...], dpre).astype(BF16).reshape(din_ref.shape)
        for which in range(2):
            core = own_ref[1] ^ which
            for chip in range(4):
                grad_refs[which][chip] = din_ref[(own_ref[2] ^ chip) * 2 + core]
            grad_refs[2 + which][0] = dout_ref[core]

    @pl.when(step == pl.num_programs(0) - 1)
    def _():
        router = jnp.zeros((LANES, width), F32)
        for shift in range(group):
            span = slice(shift * capacity, (shift + 1) * capacity)
            gate = gate_ref[span, 0:1]
            result = acc_ref[span, :]
            out_ref[source(shift), 0] = (gate * result).astype(BF16)
            dot = jnp.sum(result * g_ref[source(shift), 0, :, :width].astype(F32), axis=1, keepdims=True)
            coef = gate * (1.0 - gate) * dot
            lane = lax.broadcasted_iota(jnp.int32, (capacity, LANES), 1)
            other = other_of(g_ref[source(shift), 0, :, width:])
            sign = jnp.where(lane == own, 1.0, 0.0) - jnp.where(lane == other, 1.0, 0.0)
            dlogits = (coef * sign).astype(BF16)
            back_refs[shift][...] = (back_ref[span, :] + dot_nn(dlogits, wrt_ref[...])).astype(BF16)
            router = router + dot_tn(dlogits, x_ref[span, :])
        router_ref[...] = router


def expert_call(trained, place, local, own, rows, grads, router, router_t, held, pick, w_in, w_out):
    group = len(rows)
    _, capacity, width = rows[0].shape
    inner = w_in[0].shape[2]
    chunk = inner // 4
    block = lambda f, own: own[2] ^ f
    wide = grads.shape[3]
    many = group * capacity
    shard, deep = width // 8, inner // 8
    out_specs = [pl.BlockSpec((group, 1, capacity, width), lambda f, own: (0, place, 0, 0))]
    out_specs += [full((capacity, width))] * group + [full((LANES, width))]
    out_shape = [jax.ShapeDtypeStruct((group, local, capacity, width), BF16)]
    out_shape += [jax.ShapeDtypeStruct((capacity, width), BF16)] * group
    out_shape += [jax.ShapeDtypeStruct((LANES, width), F32)]
    if trained:
        out_specs += [pl.BlockSpec((4, shard, chunk), lambda f, own: (0, 0, block(f, own)))] * 2
        out_specs += [pl.BlockSpec((1, deep, width), lambda f, own: (f, 0, 0))] * 2
        out_shape += [jax.ShapeDtypeStruct((4, shard, inner), BF16)] * 2
        out_shape += [jax.ShapeDtypeStruct((4, deep, width), BF16)] * 2
    return pl.pallas_call(
        functools.partial(expert_kernel, trained, group, len(held), pick),
        grid_spec=pltpu.PrefetchScalarGridSpec(
            num_scalar_prefetch=1,
            grid=(4,),
            in_specs=[pl.BlockSpec((1, capacity, width), lambda f, own: (place, 0, 0))] * group
            + [pl.BlockSpec((group, 1, capacity, wide), lambda f, own: (0, place, 0, 0))]
            + [full((width, LANES)), full((LANES, width))]
            + [pl.BlockSpec(memory_space=pl.ANY)] * (len(w_in) + len(w_out) + len(held)),
            out_specs=out_specs,
            scratch_shapes=[
            pltpu.VMEM((many, width), BF16),
            pltpu.VMEM((many, width), BF16),
            pltpu.VMEM((many, LANES), F32),
            pltpu.VMEM((many, width), F32),
            pltpu.VMEM((many, width), F32),
            pltpu.VMEM((width, many), BF16),
            pltpu.VMEM((4, width, chunk), BF16),
            pltpu.VMEM((4, chunk, width), BF16),
            pltpu.VMEM((8, shard, chunk) if trained else (8, LANES), BF16),
            pltpu.VMEM((2, deep, width) if trained else (8, LANES), BF16),
            pltpu.SemaphoreType.DMA((4, 14)),
            ],
        ),
        out_shape=out_shape,
        input_output_aliases={group + 24: 0} if held else {},
        compiler_params=params(),
        cost_estimate=cost(23 if trained else 17),
        name="experts_new" if trained else "experts_old",
    )(own, *rows, grads, router, router_t, *w_in, *w_out, *held)


def pick_matrix(slot_ref, total):
    place = lax.broadcasted_iota(jnp.int32, (slot_ref.shape[0], total), 1)
    hit = (place == slot_ref[:, 0:1]) | (place == slot_ref[:, 1:2])
    return jnp.where(hit, 1.0, 0.0).astype(BF16)


def pick_rows(slot_ref, part_refs):
    width = part_refs[0].shape[-1]
    held = jnp.concatenate([part[...].reshape(-1, width) for part in part_refs], axis=0)
    return dot_nn(pick_matrix(slot_ref, held.shape[0]), held)


def combine_kernel(me_ref, slot_ref, res_ref, part_ref, out_ref):
    group, _, _, width = part_ref.shape
    parts = [part_ref[lax.rem(me_ref[0] + shift, group)].reshape(-1, width) for shift in range(group)]
    held = jnp.concatenate(parts, axis=0)
    out_ref[...] = res_ref[...] + dot_nn(pick_matrix(slot_ref, held.shape[0]), held)


def combine_call(me, slots, residual, parts):
    seq, width = residual.shape
    block = 256
    rows = pl.BlockSpec((block, width), lambda i: (i, 0))
    return pl.pallas_call(
        combine_kernel,
        grid=(seq // block,),
        in_specs=[smem(), pl.BlockSpec((block, LANES), lambda i: (i, 0)), rows, full(parts.shape)],
        out_specs=rows,
        out_shape=jax.ShapeDtypeStruct((seq, width), F32),
        compiler_params=params(),
        cost_estimate=cost(6.2),
        name="combine",
    )(me, slots, residual, parts)


def middle_kernel(count, slot_ref, res_ref, cot_ref, gain_ref, low_ref, high_ref, w_ref, at_ref, *refs):
    parts = refs[:count]
    dres_ref, dmix_ref, keep_ref, send_ref, sums_ref, acc_ref = refs[count:]
    step = pl.program_id(0)
    dnormed = pick_rows(slot_ref, parts)
    xhat, scale = norm_parts(res_ref[...])
    dres = cot_ref[...].astype(F32) + norm_back(dnormed, gain_ref[2:3, :], xhat, scale)
    dres_ref[...] = dres
    dattn = dres.astype(BF16)
    dmix_ref[...] = dot_nt(dattn, w_ref[...]).astype(BF16)

    @pl.when(step == 0)
    def _():
        sums_ref[...] = jnp.zeros_like(sums_ref)
        acc_ref[...] = jnp.zeros_like(acc_ref)

    mixed = jnp.concatenate([low_ref[...], high_ref[...]], axis=1)
    acc_ref[...] += dot_tn(mixed, dattn).reshape(acc_ref.shape)
    sums_ref[0:1, :] += jnp.sum(dnormed * xhat, axis=0, keepdims=True)
    sums_ref[1:2, :] += jnp.sum(dnormed, axis=0, keepdims=True)

    @pl.when(step == pl.num_programs(0) - 1)
    def _():
        for chip in range(4):
            for far in range(4):
                for core, ref in enumerate((keep_ref, send_ref)):
                    piece = acc_ref[block_at(at_ref, chip, core, far)].astype(BF16)
                    ref[chip, far, 0] = piece[:, : piece.shape[1] // 2]
                    ref[chip, far, 1] = piece[:, piece.shape[1] // 2 :]


def middle_call(slots, residual, cotangent, gain, mixed, weight, at, parts):
    seq, width = residual.shape
    tall = width // BLOCKS
    block = 256
    capacity = parts[0].shape[0]
    rows = pl.BlockSpec((block, width), lambda i: (i, 0))
    half = pl.BlockSpec((block, width // 2), lambda i: (i, 0))
    return pl.pallas_call(
        functools.partial(middle_kernel, len(parts)),
        grid=(seq // block,),
        in_specs=[
            pl.BlockSpec((block, LANES), lambda i: (i, 0)),
            rows,
            rows,
            full((4, width)),
            half,
            half,
            full((width, width)),
            smem(),
        ]
        + [full((capacity, width))] * len(parts),
        out_specs=[rows, rows] + [full((4, 4, 2, tall, width // 2))] * 2 + [full((8, width))],
        out_shape=[
            jax.ShapeDtypeStruct((seq, width), F32),
            jax.ShapeDtypeStruct((seq, width), BF16),
            jax.ShapeDtypeStruct((4, 4, 2, tall, width // 2), BF16),
            jax.ShapeDtypeStruct((4, 4, 2, tall, width // 2), BF16),
            jax.ShapeDtypeStruct((8, width), F32),
        ],
        scratch_shapes=[pltpu.VMEM((BLOCKS, tall, width), F32)],
        compiler_params=params(),
        cost_estimate=cost(13),
        name="middle_back",
    )(slots, residual, cotangent, gain, *mixed, weight, at, *parts)


def last_kernel(low_ref, high_ref, tok_ref, dres_ref, gain_ref, w_ref, out_ref, sums_ref):
    width = tok_ref.shape[1]
    grads = [ref[part] for part in range(3) for ref in (low_ref, high_ref)]
    dnormed = dot_nt(jnp.concatenate(grads, axis=1), w_ref[...])
    xhat, scale = norm_parts(tok_ref[...].astype(F32))
    out_ref[...] = dres_ref[...] + norm_back(dnormed, gain_ref[0:1, :], xhat, scale)

    @pl.when(pl.program_id(0) == 0)
    def _():
        sums_ref[...] = jnp.zeros_like(sums_ref)

    sums_ref[0:1, :] += jnp.sum(dnormed * xhat, axis=0, keepdims=True)
    sums_ref[1:2, :] += jnp.sum(dnormed, axis=0, keepdims=True)


def last_call(dqkv, tokens, dres, gain, weight):
    seq, width = tokens.shape
    block = 256
    rows = pl.BlockSpec((block, width), lambda i: (i, 0))
    return pl.pallas_call(
        last_kernel,
        grid=(seq // block,),
        in_specs=[
            pl.BlockSpec((3, block, width // 2), lambda i: (0, i, 0)),
            pl.BlockSpec((3, block, width // 2), lambda i: (0, i, 0)),
            rows,
            rows,
            full((4, width)),
            full((width, 3 * width)),
        ],
        out_specs=[rows, full((8, width))],
        out_shape=[
            jax.ShapeDtypeStruct((seq, width), F32),
            jax.ShapeDtypeStruct((8, width), F32),
        ],
        compiler_params=params(),
        cost_estimate=cost(5),
        name="last_back",
    )(*dqkv, tokens, dres, gain, weight)


def unpack_kernel(outs, parts, at_ref, *refs):
    pieces = refs[:8]
    out_refs = refs[-outs:]
    tall = pieces[0].shape[1]
    part = pl.program_id(0)

    def put(out_ref):
        for index, piece in enumerate(pieces):

            def each(far, carry, index=index, piece=piece):
                place = (at_ref[0] ^ index) * 4 + (at_ref[1] ^ ((far >> 1) | ((far & 1) << 1)))
                rows = pl.ds(pl.multiple_of(place * tall, 8), tall)
                out_ref[rows, :] = piece[far * parts + part].astype(F32)
                return carry

            lax.fori_loop(0, 4, each, 0)

    @pl.when(part < 3)
    def _():
        put(out_refs[0])

    if outs > 1:

        @pl.when(part >= 3)
        def _():
            put(out_refs[1])


def unpack_call(at, pieces, half, base=None):
    blocks, tall, part_width = pieces[0].shape
    parts = blocks // 4
    width = tall * BLOCKS
    out_specs = [pl.BlockSpec((width, part_width), lambda p: (0, 2 * jnp.minimum(p, 2) + half))]
    out_shape = [jax.ShapeDtypeStruct((width, 6 * part_width), F32)]
    if parts > 3:
        out_specs.append(pl.BlockSpec((width, part_width), lambda p: (0, jnp.maximum(p - 3, 0))))
        out_shape.append(jax.ShapeDtypeStruct((width, width), F32))
    held = [] if base is None else [base]
    return pl.pallas_call(
        functools.partial(unpack_kernel, len(out_shape), parts),
        grid=(parts,),
        in_specs=[smem()]
        + [full((blocks, tall, part_width))] * 8
        + [pl.BlockSpec(memory_space=pl.ANY)] * len(held),
        out_specs=out_specs,
        out_shape=out_shape,
        input_output_aliases={9: 0} if held else {},
        compiler_params=params(),
        cost_estimate=cost(4),
        name="unpack",
    )(at, *pieces, *held)


def swap(block, bits):
    size = lax.axis_size("batch")
    return lax.ppermute(block, "batch", [(i, i ^ bits) for i in range(size)])


def across(block, bits):
    size = lax.axis_size("expert")
    return lax.ppermute(block, "expert", [(i, i ^ bits) for i in range(size)])


def added(*blocks):
    total = blocks[0].astype(F32)
    for block in blocks[1:]:
        total = total + block.astype(F32)
    return total


def gather_shards(shard):
    whole = lax.all_gather(shard, "batch", axis=1, tiled=True)
    some, rows, width = whole.shape
    parts = whole.reshape(some, 4, 2, rows // 8, width)
    half = rows // 16
    return [
        parts[:, chip, core, lower * half : (lower + 1) * half] if chip == 3 else parts[:, chip, core]
        for core in range(2)
        for chip, lower in PLACES
    ]


def near(shard):
    return [swap(shard, 2), swap(shard, 4)]


def relay(full_x, full_y):
    half = full_x.shape[1] // 2
    return [swap(full_y[:, :half], 2), swap(full_x[:, half:], 4)]


def tie(*values):
    return list(lax.optimization_barrier(values))


def sum_all(keep, send):
    keep, send = lax.psum((keep, send), ("expert", "batch"))
    pieces = []
    for chip in range(4):
        for half in (keep, send):
            parts = jnp.concatenate([part[chip] for part in half], axis=1)
            pieces.append(jnp.concatenate([parts[far] for far in range(4)]))
    return pieces


def sum_core(keep, send):
    got = [swap(part, 1) for part in send]
    halves = []
    for chip in range(4):
        parts = [added(mine[chip], other[chip]) for mine, other in zip(keep, got)]
        halves.append(jnp.concatenate(parts, axis=1).astype(BF16))
    return halves


def to_chips(halves):
    return [halves[0]] + [swap(halves[chip], 2 * chip) for chip in (1, 2, 3)]


def total(parts):
    return added(*parts).astype(BF16)


def give(block, bits):
    rows = block.shape[0] // 2
    return [block[:rows], across(block[rows:], bits)]


def spread_chips(column):
    return [column] + [swap(column, 2 * chip) for chip in (1, 2, 3)]


def spread_cores(blocks):
    return [piece for block in blocks for piece in (block, swap(block, 1))]


def packed(small):
    half = small.shape[1] // 2
    return jnp.concatenate([small[:, :half], small[:, half:]])


def unpacked(small):
    half = small.shape[0] // 2
    return jnp.concatenate([small[:half], small[half:]], axis=1)


def natural(keep, send):
    both = jnp.stack([keep, send], axis=1)
    return both.reshape(-1, both.shape[-1])


def body(
    tokens,
    lengths,
    routes,
    ln1_gain,
    ln1_bias,
    ln2_gain,
    ln2_bias,
    w_qkv,
    w_proj,
    w_router,
    old_in,
    old_out,
    new_in,
    new_out,
    cotangent,
):
    group = lax.axis_size("expert")
    me = lax.axis_index("expert")
    token_rows = tokens[0]
    cot_rows = cotangent[0]
    seq, width = token_rows.shape
    experts = w_router.shape[1]
    local = experts // group
    per = old_in.shape[0]
    capacity = max(4, seq // experts)
    scales = jnp.stack([ln1_gain, ln1_bias, ln2_gain, ln2_bias])

    def go(block, shift):
        if shift == 0:
            return block
        return lax.ppermute(block, "expert", [(i, (i + shift) % group) for i in range(group)])

    def trade(blocks):
        return lax.all_to_all(blocks, "expert", 0, 0, tiled=True)

    def come(block, shift):
        if shift == 0:
            return block
        return lax.ppermute(block, "expert", [(i, (i - shift) % group) for i in range(group)])

    fast = group == 4 and lax.axis_size("batch") == 8 and per == 1 and experts == 8
    at = jnp.stack([lax.axis_index("batch"), me]).astype(jnp.int32) if fast else jnp.zeros((2,), jnp.int32)
    me_one = jnp.full((1,), me, jnp.int32)
    pairs = width // LANES
    first_half = pairs // 2
    halves = ((0, first_half), (first_half, pairs - first_half))
    if fast:
        pair_in = jnp.stack([new_in[0], old_in[0]])
        pair_out = jnp.stack([new_out[0], old_out[0]])
        in_full = near(pair_in)
    slots, slots_t, sent_grads = route_call(
        lengths, me_one, routes[0], cot_rows, experts, group, capacity
    )
    grads = trade(sent_grads)
    token_rows, slots = tie(token_rows, slots)
    normed1, qkv = qkv_call(token_rows, scales, w_qkv)
    mixed_low, lse_low = attend_call(lengths, qkv, *halves[0])
    if fast:
        qkv, mixed_low, pair_in, pair_out, in_full[0], in_full[1] = tie(
            qkv, mixed_low, pair_in, pair_out, *in_full
        )
        in_half = relay(*in_full)
        in_other = [swap(part, 1) for part in (pair_in, *in_full)]
    mixed_high, lse_high = attend_call(lengths, qkv, *halves[1])
    if fast:
        mixed_high, pair_out, *tied = tie(mixed_high, pair_out, *in_half, *in_other)
        in_half, in_other = tied[:2], tied[2:]
        out_full = near(pair_out)
    mixed = (mixed_low, mixed_high)
    residual, *sent_rows = project_call(
        mixed, token_rows, w_proj, scales, slots, group, local, capacity
    )
    rows = [go(sent_rows[shift], shift) for shift in range(group)]
    router = jnp.pad(w_router, ((0, 0), (0, LANES - experts)))
    router_t = jnp.pad(w_router.T, ((0, LANES - experts), (0, 0)))
    if fast:
        rows[1], rows[3], router, router_t, pair_out, *tied = tie(
            rows[1], rows[3], router, router_t, pair_out, *out_full, *in_half
        )
        out_full, in_half = tied[:2], tied[2:]
        out_half = relay(*out_full)
        in_parts = [pair_in, *in_full, *in_half]
        out_parts = [pair_out, *out_full, *out_half]
        in_parts += in_other + [swap(part, 1) for part in in_half]
        out_parts += [swap(part, 1) for part in out_parts]
        weights = {True: (0, in_parts, out_parts), False: (1, in_parts, out_parts)}
    else:
        weights = {
            trained: (0, gather_shards(w_in), gather_shards(w_out))
            for trained, w_in, w_out in ((True, new_in, new_out), (False, old_in, old_out))
        }
    core, chip = (at[0] & 1, at[0] >> 1) if fast else (0, 0)
    outs, backs, router_sum = [], {}, 0.0
    half = experts // 2
    for trained in (True, False):
        for index in range(per):
            place = index + (per if trained else 0)
            own = jnp.stack([me * per + index + (half if trained else 0), core, chip, me]).astype(jnp.int32)
            got = expert_call(
                trained,
                place,
                local,
                own,
                rows,
                grads,
                router,
                router_t,
                outs,
                weights[trained][0] + index,
                *weights[trained][1:],
            )
            outs = [got[0]]
            sent = got[1 : group + 1]
            if fast and not trained:
                tied = tie(*sent, *backs[1])
                sent, backs[1] = tied[:group], tied[group:]
            backs[place] = [come(sent[shift], shift) for shift in range(group)]
            router_sum = router_sum + got[group + 1]
            if trained:
                in_keep, in_send, out_keep, out_send = got[group + 2 :]
    returned = [backs[p][shift] for shift in range(group) for p in range(local)]
    if fast:
        in_other, out_other = swap(in_send, 1), swap(out_send, 1)
        outs[0], in_keep, out_keep, in_other, out_other = tie(outs[0], in_keep, out_keep, in_other, out_other)
        in_rs = [total(pair) for pair in zip(in_keep, in_other)]
        out_rs = [total(pair) for pair in zip(out_keep, out_other)]
        in_got = [swap(in_rs[chip], 2 * chip) for chip in (1, 2)]
        tied = tie(*returned, in_rs[3], *out_rs)
        returned, in_rs[3], out_rs = tied[:-5], tied[-5], tied[-4:]
        in_got.append(swap(in_rs[3], 6))
    dres, dmixed, proj_keep, proj_send, sums2 = middle_call(
        slots_t, residual, cot_rows, scales, mixed, w_proj, at, returned
    )
    if fast:
        dmixed, outs[0], in_got[0], in_got[1], *out_rs = tie(dmixed, outs[0], in_got[0], in_got[1], *out_rs)
        out_got = [swap(out_rs[chip], 2 * chip) for chip in (1, 2)]
    else:
        natural_in = natural(in_keep, in_send)
        natural_out = natural(out_keep, out_send)
    back_outs = trade(outs[0])
    dq_low, keep_low, send_low = attend_back_call(
        lengths, qkv, dmixed, mixed_low, lse_low, normed1, at, *halves[0]
    )
    if fast:
        halves_low = sum_core((keep_low, proj_keep), (send_low, proj_send))
        dmixed, dq_low, in_got[2], out_got[0], out_got[1], out_rs[3] = tie(
            dmixed, dq_low, in_got[2], *out_got, out_rs[3]
        )
        out_got.append(swap(out_rs[3], 6))
    dq_high, keep_high, send_high = attend_back_call(
        lengths, qkv, dmixed, mixed_high, lse_high, normed1, at, *halves[1]
    )
    if fast:
        dq_high, keep_high, back_outs, *halves_low = tie(dq_high, keep_high, back_outs, *halves_low)
        low = to_chips(halves_low)
        halves_high = sum_core((keep_high,), (send_high,))
    input_grad, sums1 = last_call((dq_low, dq_high), token_rows, dres, scales, w_qkv)
    if fast:
        sums1, *halves_high = tie(sums1, *halves_high)
        high = to_chips(halves_high)
        small = jnp.concatenate([router_sum[:experts], sums1[:2], sums2[:2]], axis=0)
        low = give(total(low), 1)
        tied = tie(*low, *high)
        low = give(total(tied[:2]), 2)
        high = give(total(tied[2:]), 1)
        new_in_grad = added(in_rs[0], *in_got)
        new_in_grad, *tied = tie(new_in_grad, *low, *high)
        own_low = total(tied[:2])[0]
        low = [own_low, across(own_low, 2)]
        high = give(total(tied[2:]), 2)
        new_out_grad = added(out_rs[0], *out_got)
        new_out_grad, *tied = tie(new_out_grad, *low, *high)
        low = jnp.stack(tied[:2])
        low = [low, across(low, 1)]
        own_high = total(tied[2:])[0]
        mine = packed(small).astype(BF16)[None]
        high = [jnp.concatenate([own_high, mine])]
        high.append(across(high[0], 2))
        tied = tie(*low, *high)
        column_low = jnp.concatenate(tied[:2]).reshape(-1, *own_low.shape[1:])
        chips_low = spread_chips(column_low)
        parts = own_high.shape[0]
        mine = total([block[parts:] for block in tied[2:]])
        high = jnp.concatenate([block[:parts] for block in tied[2:]] + [mine])
        high = [high, across(high, 1)]
        mine = total([block[2 * parts :] for block in high])
        chips_high = spread_chips(jnp.concatenate([block[: 2 * parts] for block in high] + [mine]))
        output = combine_call(me_one, slots_t, residual, back_outs)
        output, *chips_low = tie(output, *chips_low)
        pieces_low = spread_cores(chips_low)
        qkv_grad, proj_grad = unpack_call(at, pieces_low, 0)
        qkv_grad, *chips_high = tie(qkv_grad, *chips_high)
        pieces_high = spread_cores(chips_high)
        small = unpacked(added(*[piece[4 * parts] for piece in pieces_high]))
    else:
        pieces_low = sum_all((keep_low, proj_keep), (send_low, proj_send))
        pieces_high = sum_all((keep_high,), (send_high,))
        small = jnp.concatenate([router_sum[:experts], sums1[:2], sums2[:2]], axis=0)
        small = jnp.sum(lax.all_gather(small, ("expert", "batch"), axis=0), axis=0)
        new_in_grad = lax.psum_scatter(natural_in, "batch", scatter_dimension=0, tiled=True)
        new_out_grad = lax.psum_scatter(natural_out, "batch", scatter_dimension=0, tiled=True)
    if not fast:
        output = combine_call(me_one, slots_t, residual, back_outs)
        qkv_grad, proj_grad = unpack_call(at, pieces_low, 0)
    (qkv_grad,) = unpack_call(at, pieces_high, 1, qkv_grad)
    return (
        output[None],
        input_grad[None],
        small[experts],
        small[experts + 1],
        small[experts + 2],
        small[experts + 3],
        qkv_grad,
        proj_grad,
        small[:experts].T,
        new_in_grad.astype(F32)[None],
        new_out_grad.astype(F32)[None],
    )


def solution(mesh):
    rows = P(("expert", "batch"), None, None)
    weights = P("expert", "batch", None)
    placed = (
        (rows, P(("expert", "batch")), rows)
        + (P(),) * 7
        + (weights,) * 4
        + (rows,)
    )
    return jax.shard_map(
        body,
        mesh=mesh,
        in_specs=placed,
        out_specs=(rows, rows) + (P(),) * 7 + (weights, weights),
        check_vma=False,
    )
```
